32 devices in a mesh: groups: 2 (over x), ctx: 16 (over z, y, core).
Axes of the slice: x: 2, y: 2, z: 4, core: 2. Of those that a mesh axis runs over, the one named last changes fastest.
Arguments:
- queries: bfloat16 [256, 2048], P(('groups', 'ctx')), parts along dimension 0, may hold values from -8 to 8, as said below
- keys: bfloat16 [2, 8192, 256], P('groups', 'ctx'), parts along dimension 0, may hold values from -8 to 8
- values: bfloat16 [2, 8192, 256], P('groups', 'ctx'), parts along dimension 0, may hold values from -16 to 16
- lengths: int32 [2], P('groups'), parts along dimension 0, may hold values from 4096 to 8192, as said below
- owner_counts: int32 [32], P('groups'), parts along dimension 0, may hold values from 1 to 16, 128 in all
- row_order: int32 [256], P('groups'), parts along dimension 0, may hold values from 0 to 127, each once
- residual: bfloat16 [512, 2048], P(('groups', 'ctx')), parts along dimension 0, may hold values from -40 to 40, as said below
- out_weight: bfloat16 [2048, 2048], P('ctx'), may hold values from -0.125 to 0.125
- norm_gain: float32 [2048], replicated, may hold values from 0.1 to 1.9
- expert_ids: int32 [512, 8], P(('groups', 'ctx')), parts along dimension 0, may hold values from 0 to 15, all different within a row; in each aligned block of 16 rows (0 to 15, 16 to 31, ...) at most 16 rows name the same one
- route_weights: float32 [512, 8], P(('groups', 'ctx')), parts along dimension 0, may hold values from 0.1 to 1
- gate_up: bfloat16 [16, 2048, 1536], P('ctx'), may hold values from -0.125 to 0.125
- expert_down: bfloat16 [16, 768, 2048], P('ctx'), may hold values from -0.21875 to 0.21875
Outputs:
- attn_slots: bfloat16 [512, 2048], P(('groups', 'ctx')), parts along dimension 0
- layer_out: bfloat16 [512, 2048], P(('groups', 'ctx')), parts along dimension 0
The draws below stay inside these ranges and needn't reach their ends.
There are 2 independent parts, one for each index of `groups`. The reference program is written for one: setup_inputs(seed, part) draws one part's arguments, and reference() takes and returns one part's arrays. A program takes and returns all parts, laid end to end along the dimension named above; an argument that names none is the same for every part. Nothing has to cross between parts.
Inputs may be any that keep to these rules, and one draw needn't show every extreme that they name: Large entries of queries and keys may line up. `lengths`: at least 4096; one request has exactly 8192. `owner_counts`: sum to 128; the largest is exactly 16. `row_order`: each row once. `residual`: entries may be any real values in the range. `expert_ids`: each slot names 8 different experts; within the 16 slots of one owner no expert is named more than 16 times, and some expert exactly that many times.
All inputs are finite; a program needn't handle non-finite values.
Results may differ from the reference program's by a relative error of at most 0.009.
Values may be sent and summed in bfloat16 or wider, within the bound.
No kernel may reach another device: no remote copies, remote signals or barrier semaphores. Data moves between devices by JAX's collectives and lax.ppermute only.
A program may use at most 128 MiB of HBM per device.

```python
import math
import jax
import jax.numpy as jnp
import numpy as np
from jax import lax

D = 2048
HQ = 16
KVH = 2
HD = 128
EFF = 768
TOPK = 8
STRETCH = 128
CACHE_DEV = 512
ROWS = 128
REQS = 1
CTX_LEN = 8192
CAP_ROWS = 16
SLOTS = 256
EXPERTS = 16
ROUTE_CAP = 16
N_CTX = 16


def quiet_blocks(key):
    quarter = max(1, N_CTX // 4)
    picks_count = min(4, quarter)
    request_keys = jax.random.split(jax.random.fold_in(key, 7001), REQS)

    def one_order(one_key):
        return jax.random.permutation(one_key, quarter)
    orders = jax.vmap(one_order)(request_keys)
    chosen = orders[:, :picks_count].astype(jnp.int32)
    block_of = (jnp.arange(CTX_LEN, dtype=jnp.int32) // CACHE_DEV).astype(jnp.int32)
    return jnp.any(block_of[None, :, None] == chosen[:, None, :], axis=-1)


def draw_queries(key, part):
    drawn = jnp.clip(jax.random.normal(jax.random.fold_in(key, 11), (ROWS, HQ * HD), jnp.float32) * 1.6, -8.0, 8.0)
    return drawn.astype(jnp.bfloat16)


def draw_keys(key, part):
    drawn = jnp.clip(jax.random.normal(jax.random.fold_in(key, 21), (REQS, CTX_LEN, KVH * HD), jnp.float32) * 2.0, -8.0, 8.0)
    softer = jax.random.normal(jax.random.fold_in(key, 24), (REQS, CTX_LEN, KVH * HD), jnp.float32) * 0.25
    silent = quiet_blocks(key)
    drawn = jnp.where(silent[..., None], jnp.clip(softer, -8.0, 8.0), drawn)
    return drawn.astype(jnp.bfloat16)


def draw_values(key, part):
    silent = quiet_blocks(key)
    polarity = jnp.where(jax.random.bernoulli(jax.random.fold_in(key, 51), 0.5, (REQS, 1, KVH * HD)), 1.0, -1.0)
    magnitude = jax.random.uniform(jax.random.fold_in(key, 54), (REQS, CTX_LEN, KVH * HD), jnp.float32, 10.0, 14.0)
    entries = jnp.clip(jax.random.normal(jax.random.fold_in(key, 55), (REQS, CTX_LEN, KVH * HD), jnp.float32) * 0.15, -1.0, 1.0)
    drawn = jnp.where(silent[..., None], polarity * magnitude, entries)
    return jnp.clip(drawn, -16.0, 16.0).astype(jnp.bfloat16)


def draw_lengths(key, part):
    drawn = jax.random.randint(jax.random.fold_in(key, 31), (REQS,), CTX_LEN // 2, CTX_LEN + 1)
    which = jax.random.randint(jax.random.fold_in(key, 32), (), 0, REQS)
    return jnp.where(jnp.arange(REQS) == which, CTX_LEN, drawn).astype(jnp.int32)


def draw_residual(key, part):
    row_scale = jnp.exp(jax.random.uniform(jax.random.fold_in(key, 41), (SLOTS, 1), jnp.float32, jnp.log(0.3), jnp.log(3.0)))
    col_scale = jnp.exp(jax.random.uniform(jax.random.fold_in(key, 42), (1, D), jnp.float32, jnp.log(0.3), jnp.log(3.0)))
    drawn = row_scale * col_scale * jnp.clip(jax.random.normal(jax.random.fold_in(key, 45), (SLOTS, D), jnp.float32), -4.0, 4.0)
    return jnp.clip(drawn, -40.0, 40.0).astype(jnp.bfloat16)


def block_levels(own_key, shape, cuts, least, top_value):
    level = 1.0
    for position, parts in cuts:
        draws = jax.random.uniform(jax.random.fold_in(jax.random.fold_in(own_key, 6), position), (parts,), jnp.float32, least / len(cuts), top_value / len(cuts))
        level = level * jnp.repeat(jnp.exp(draws), shape[position] // parts).reshape((-1,) + (1,) * (len(shape) - 1 - position))
    return level


def profile(count, total, reach, slope):
    loads = [(1 << 20) // math.isqrt(standing ** slope) + 1 for standing in range(2, count + 1)]
    spare, given = total - reach - (count - 1), [1] * (count - 1)
    while spare > 0:
        free = [i for i in range(count - 1) if given[i] < reach]
        mass, remaining = sum([loads[i] for i in free]), spare
        for i in free:
            extra = min(reach - given[i], max(1, remaining * loads[i] // mass), spare)
            given[i] = given[i] + extra
            spare = spare - extra
    return np.array([reach] + given)


def uneven(rng, count, total, reach, slope):
    if count == 2:
        one = jax.random.randint(rng, (), max(1, total - reach), min(reach, total - 1) + 1)
        return jnp.stack([one, total - one])
    sizes = jnp.asarray(profile(count, total, reach, slope), jnp.int32)
    couples = (count - 1) // 2
    source_of, taker = sizes[1:1 + 2 * couples:2], sizes[2:2 + 2 * couples:2]
    margin = jnp.minimum(source_of - 1, reach - taker)
    shifted = jax.random.randint(jax.random.fold_in(rng, 1), (couples,), 0, 1 << 20) % (margin + 1)
    sizes = sizes.at[1:1 + 2 * couples:2].set(source_of - shifted).at[2:2 + 2 * couples:2].set(taker + shifted)
    return sizes[jax.random.permutation(jax.random.fold_in(rng, 2), count)]


def assign_block(key, own, number, rows, count, top, reach, slope):
    ranking = jax.random.permutation(key, count)
    packed, usual = load_shares(count, rows * top, reach, slope, True), load_shares(count, rows * top, reach, slope, False)
    places = jnp.arange(count)

    def named(tallies, offset_by):
        used = int((tallies > 0).sum())
        fixed = max(1, used // 4)
        moved = fixed + (places - fixed + offset_by * (used - fixed)) % max(1, count - fixed)
        return jnp.zeros((count,), jnp.int32).at[ranking[jnp.where(places < fixed, places, moved)]].set(jnp.asarray(tallies, jnp.int32))

    tallies = jnp.where(number % 4 == 0, named(packed, number // 4), named(usual, number - number // 4 - 1))
    mixed = jax.random.permutation(jax.random.fold_in(own, 3), count)
    giver, sink = mixed[0:count // 2 * 2:2], mixed[1:count // 2 * 2:2]
    slack = jnp.minimum(tallies[giver] - 1, reach - tallies[sink]) // 2
    slack = jnp.where((giver == ranking[0]) | (sink == ranking[0]) | (tallies[sink] == 0), 0, jnp.maximum(slack, 0))
    moved = jax.random.randint(jax.random.fold_in(own, 4), (count // 2,), 0, 1 << 20) % (slack + 1)
    tallies = tallies.at[giver].add(-moved).at[sink].add(moved)
    items = jnp.searchsorted(jnp.cumsum(tallies), jnp.arange(rows * top), side="right").astype(jnp.int32)
    listing = items.reshape(top, rows).T
    listing = listing[jax.random.permutation(jax.random.fold_in(own, 1), rows)]
    offset_by = jax.random.randint(jax.random.fold_in(own, 2), (rows, 1), 0, top)
    return jnp.take_along_axis(listing, (jnp.arange(top)[None, :] + offset_by) % top, axis=1)


def load_shares(number_of, total, limit, slope, full):
    loads = [(1 << 20) // math.isqrt(grade ** slope) + 1 for grade in range(1, number_of + 1)]
    largest = limit if full else min(limit, max(-(-total // number_of), total * loads[0] // sum(loads)))
    least = 1 if total - largest >= number_of - 1 else 0
    holding, rest = [largest] + [least] * (number_of - 1), total - largest - least * (number_of - 1)
    while rest > 0:
        free = [i for i in range(1, number_of) if holding[i] < largest] or [i for i in range(1, number_of) if holding[i] < limit]
        whole, remaining = sum([loads[i] for i in free]), rest
        for i in free:
            more = min(limit - holding[i], max(1, remaining * loads[i] // whole), rest)
            holding[i] = holding[i] + more
            rest = rest - more
    return np.array(holding)


def gaussian(stream_key, shape, width, limit, shards=(), kind=jnp.bfloat16):
    array = jax.random.normal(stream_key, shape, jnp.float32) * width
    if len(shards) > 0:
        array = block_levels(stream_key, shape, shards, -0.22, 0.18) * array
    return jnp.clip(array, min=-limit, max=limit).astype(kind)


def setup_inputs(seed: int = 0, part: int = 0) -> dict:
    streams_of = jax.random.split(jax.random.key(seed), 14)
    part_keys = jax.random.split(jax.random.fold_in(streams_of[13], part), 14)
    queries = draw_queries(jax.random.fold_in(jax.random.fold_in(streams_of[13], part), 71), part)
    keys = draw_keys(jax.random.fold_in(jax.random.fold_in(streams_of[13], part), 71), part)
    values = draw_values(jax.random.fold_in(jax.random.fold_in(streams_of[13], part), 71), part)
    lengths = draw_lengths(jax.random.fold_in(jax.random.fold_in(streams_of[13], part), 71), part)
    owner_counts = uneven(part_keys[4], N_CTX, ROWS, CAP_ROWS, 2).astype(jnp.int32)
    row_order = jax.random.permutation(part_keys[5], ROWS).astype(jnp.int32)
    residual = draw_residual(jax.random.fold_in(jax.random.fold_in(streams_of[13], part), 71), part)
    out_weight = gaussian(streams_of[7], (HQ * HD, D), (HQ * HD) ** -0.5, 0.125, ((0, 16),))
    norm_gain = jnp.clip(1.0 + 0.18 * jax.random.normal(streams_of[8], (D,), jnp.float32), 0.1, 1.9)
    expert_ids_keys = jax.random.split(jax.random.fold_in(part_keys[9], 1), SLOTS // CAP_ROWS)
    expert_ids_turns = jax.random.permutation(jax.random.fold_in(part_keys[9], 3), SLOTS // CAP_ROWS)
    expert_ids = jax.vmap(lambda own, number: assign_block(jax.random.fold_in(part_keys[9], 2), own, number, CAP_ROWS, EXPERTS, TOPK, ROUTE_CAP, 2))(expert_ids_keys, expert_ids_turns).reshape((SLOTS, TOPK))
    route_weights = jnp.clip(jnp.exp(math.log(1.0) - 2.3025851 * jax.random.uniform(part_keys[10], (SLOTS, TOPK), jnp.float32) ** block_levels(part_keys[10], (SLOTS, TOPK), ((0, 16),), -0.2, 0.2)), 0.1, 1.0)
    gate_up = gaussian(streams_of[11], (EXPERTS, D, 2 * EFF), D ** -0.5, 0.125, ((0, 16),))
    expert_down = gaussian(streams_of[12], (EXPERTS, EFF, D), EFF ** -0.5, 0.21875, ((0, 16),))
    return dict(queries=queries, keys=keys, values=values, lengths=lengths, owner_counts=owner_counts, row_order=row_order, residual=residual, out_weight=out_weight, norm_gain=norm_gain, expert_ids=expert_ids, route_weights=route_weights, gate_up=gate_up, expert_down=expert_down)


def slot_table(owner_counts, row_order, total_rows, capacity):
    offsets = jnp.cumsum(owner_counts) - owner_counts
    column = jnp.arange(capacity, dtype=jnp.int32)
    where_at = (offsets[:, None] + column[None, :]).astype(jnp.int32)
    filled = column[None, :] < owner_counts[:, None]
    picked = row_order[jnp.clip(where_at, 0, total_rows - 1)]
    return (jnp.where(filled, picked, total_rows).astype(jnp.int32), filled)

def partial_attention(query_rows, key_block, value_block, lengths, first_key):
    requests = lengths.shape[0]
    groups = HQ // KVH
    span = key_block.shape[1]
    query_grid = query_rows.reshape(requests, STRETCH, KVH, groups, HD).astype(jnp.float32)
    key_grid = key_block.reshape(requests, span, KVH, HD).astype(jnp.float32)
    value_grid = value_block.reshape(requests, span, KVH, HD).astype(jnp.float32)

    def one_request(items):
        query_part, key_part, value_part, length = items
        scores = jnp.einsum('cvgh,pvh->vgcp', query_part, key_part, precision=lax.Precision.HIGHEST) * HD ** (-0.5)
        query_pos = length - STRETCH + jnp.arange(STRETCH, dtype=jnp.int32)
        key_pos = first_key + jnp.arange(span, dtype=jnp.int32)
        allowed = key_pos[None, :] <= query_pos[:, None]
        scores = jnp.where(allowed, scores, -1e+30)
        top = lax.optimization_barrier(jnp.max(scores, axis=-1))
        weights = jnp.where(allowed, jnp.exp(scores - top[..., None]), 0.0)
        total = lax.optimization_barrier(jnp.sum(weights, axis=-1))
        rounded = weights.astype(jnp.bfloat16).astype(jnp.float32)
        mixed = jnp.einsum('vgcp,pvh->cvgh', rounded, value_part, precision=lax.Precision.HIGHEST)
        return (mixed.reshape(STRETCH, HQ * HD), jnp.transpose(top, (2, 0, 1)).reshape(STRETCH, HQ), jnp.transpose(total, (2, 0, 1)).reshape(STRETCH, HQ))
    mixed, top, total = lax.map(one_request, (query_grid, key_grid, value_grid, lengths))
    return (mixed.reshape(-1, HQ * HD), top.reshape(-1, HQ), total.reshape(-1, HQ))

def reference(queries, keys, values, lengths, owner_counts, row_order, residual, out_weight, norm_gain, expert_ids, route_weights, gate_up, expert_down):
    key_shards = jnp.moveaxis(keys.reshape(REQS, N_CTX, CACHE_DEV, KVH * HD), 1, 0)
    value_shards = jnp.moveaxis(values.reshape(REQS, N_CTX, CACHE_DEV, KVH * HD), 1, 0)

    def fold(carry, items):
        best, denom, numer = carry
        shard, key_part, value_part = items
        mixed, top, total = partial_attention(queries, key_part, value_part, lengths, (shard * CACHE_DEV).astype(jnp.int32))
        new_best = jnp.maximum(best, top)
        old_factor = jnp.exp(best - new_best)
        new_factor = jnp.exp(top - new_best)
        denom = denom * old_factor + total * new_factor
        numer = (numer.reshape(ROWS, HQ, HD) * old_factor[..., None] + mixed.reshape(ROWS, HQ, HD) * new_factor[..., None]).reshape(ROWS, HQ * HD)
        return ((new_best, denom, numer), None)
    start = (jnp.full((ROWS, HQ), -1e+30, jnp.float32), jnp.zeros((ROWS, HQ), jnp.float32), jnp.zeros((ROWS, HQ * HD), jnp.float32))
    (best, denom, numer), _ = lax.scan(fold, start, (jnp.arange(N_CTX, dtype=jnp.int32), key_shards, value_shards))
    attn = (numer.reshape(ROWS, HQ, HD) / denom[..., None]).reshape(ROWS, HQ * HD).astype(jnp.bfloat16)
    attn_pad = jnp.concatenate([attn, jnp.zeros((1, HQ * HD), jnp.bfloat16)], axis=0)
    slot_rows, filled = slot_table(owner_counts, row_order, ROWS, CAP_ROWS)
    valid = filled.reshape(-1)
    attn_slots = attn_pad[slot_rows.reshape(-1)]
    projected = jnp.dot(attn_slots, out_weight, preferred_element_type=jnp.float32)
    stream = (residual.astype(jnp.float32) + projected).astype(jnp.bfloat16)
    stream_f = stream.astype(jnp.float32)
    normed = (stream_f * lax.rsqrt(lax.optimization_barrier(jnp.mean(stream_f * stream_f, axis=-1, keepdims=True)) + 1e-06) * norm_gain).astype(jnp.bfloat16)
    normed_pad = jnp.concatenate([normed, jnp.zeros((1, D), jnp.bfloat16)], axis=0)
    weight_norm = route_weights / lax.optimization_barrier(jnp.sum(route_weights, axis=-1, keepdims=True))

    def per_expert(moe, items):
        expert, gate_part, down_part = items
        hit = (expert_ids == expert) & valid[:, None]
        chosen = jnp.any(hit, axis=-1)
        weight = lax.optimization_barrier(jnp.sum(jnp.where(hit, weight_norm, 0.0), axis=-1))
        index = jnp.nonzero(chosen, size=N_CTX * ROUTE_CAP, fill_value=SLOTS)[0].astype(jnp.int32)
        rows = normed_pad[index]
        both = jnp.dot(rows, gate_part, preferred_element_type=jnp.float32)
        hidden = (jax.nn.silu(both[:, :EFF]) * both[:, EFF:]).astype(jnp.bfloat16)
        result = jnp.dot(hidden, down_part, preferred_element_type=jnp.float32).astype(jnp.bfloat16)
        weight_pad = jnp.concatenate([weight, jnp.zeros((1,), weight.dtype)])
        moe = moe.at[index].add(weight_pad[index][:, None] * result.astype(jnp.float32))
        return (moe, None)
    moe, _ = lax.scan(per_expert, jnp.zeros((SLOTS + 1, D), jnp.float32), (jnp.arange(EXPERTS, dtype=jnp.int32), gate_up, expert_down))
    layer_out = jnp.where(valid[:, None], stream_f + moe[:SLOTS], 0.0).astype(jnp.bfloat16)
    return (attn_slots, layer_out)
```

```python
import functools

import jax
import jax.numpy as jnp
from jax import lax
from jax.experimental import pallas as pl
from jax.experimental.pallas import tpu as pltpu
from jax.sharding import PartitionSpec as P

D = 2048
HQ = 16
KVH = 2
HD = 128
EFF = 768
TOPK = 8
STRETCH = 128
BF = jnp.bfloat16
F32 = jnp.float32
STAT = 8


NT = (((1,), (1,)), ((), ()))
NN = (((1,), (0,)), ((), ()))
TN = (((0,), (0,)), ((), ()))


def dot(a, b, dims):
    return lax.dot_general(a, b, dims, preferred_element_type=F32)


def place():
    device = lax.axis_index("ctx")
    return device, device & 1, device >> 1, device >> 2


def hop(x, mask, width):
    return lax.ppermute(x, "ctx", [(i, i ^ mask) for i in range(width)])


def split3(x):
    hi = x.astype(BF)
    rest = x - hi.astype(F32)
    mid = rest.astype(BF)
    return hi, mid, (rest - mid.astype(F32)).astype(BF)


def row_ids(count, per, core, axis, shape):
    i = lax.broadcasted_iota(jnp.int32, shape, axis)
    return (i // per) * (2 * per) + core * per + i % per


def owner_start(counts, owner, width):
    total = jnp.int32(0)
    for o in range(width):
        total = total + jnp.where(o < owner, counts[o], 0)
    return total


def owner_picks(counts, owner, start, cap, rows):
    p = lax.broadcasted_iota(jnp.int32, (cap, rows), 1)
    j = lax.broadcasted_iota(jnp.int32, (cap, rows), 0)
    return ((p - start == j) & (j < counts[owner])).astype(F32).astype(BF)


def attention_kernel(nz, lengths, *refs):
    pieces, (k_own, v_own, k_oth, v_oth, out, rows) = refs[:nz], refs[nz:]
    device, core, chip, z = place()
    per = pieces[0].shape[1]
    requests, span = k_own.shape[0], k_own.shape[1]
    count = rows.shape[0]
    seat = count // requests
    chips, depth = out.shape[0], out.shape[1] - STAT
    cols = HQ * HD // chips
    heads = max(1, cols // HD)
    for kz in range(nz):
        both = pieces[kz][...].astype(F32)
        for ky in range(2):
            spot = (chip ^ (2 * kz + ky)) * per
            rows[pl.ds(pl.multiple_of(spot, per), per), :] = both[ky]
    key = lax.broadcasted_iota(jnp.int32, (span, 2 * seat), 0)
    lane = lax.broadcasted_iota(jnp.int32, (1, 2 * seat), 1) % seat
    ahead = (lane // per) * (2 * per) + core * per + lane % per - STRETCH
    first_own, first_oth = device * span, (device ^ 1) * span
    for q in range(requests):
        last = lengths[q] + ahead
        see_own, see_oth = key <= last - first_own, key <= last - first_oth
        for j in range(HQ // 2):
            v = 2 * j // (HQ // KVH)
            kv = slice(v * HD, (v + 1) * HD)
            pair = jnp.concatenate(
                [
                    rows[q * seat : (q + 1) * seat, (2 * j + e) * HD : (2 * j + e + 1) * HD]
                    for e in range(2)
                ],
                axis=0,
            ).astype(BF)
            s_own = dot(k_own[q, :, kv], pair, NT) * HD ** (-0.5)
            s_oth = dot(k_oth[q, :, kv], pair, NT) * HD ** (-0.5)
            s_own = jnp.where(see_own, s_own, -1e30)
            s_oth = jnp.where(see_oth, s_oth, -1e30)
            top = jnp.maximum(
                jnp.max(s_own, axis=0, keepdims=True), jnp.max(s_oth, axis=0, keepdims=True)
            )
            w_own = jnp.where(see_own, jnp.exp(s_own - top), 0.0)
            w_oth = jnp.where(see_oth, jnp.exp(s_oth - top), 0.0)
            total = jnp.sum(w_own, axis=0, keepdims=True) + jnp.sum(w_oth, axis=0, keepdims=True)
            mixed = dot(v_own[q, :, kv], w_own.astype(BF), TN) + dot(
                v_oth[q, :, kv], w_oth.astype(BF), TN
            )
            some = total > 0.0
            safe = jnp.where(some, total, 1.0)
            mixed = (mixed / safe).astype(BF)
            lse = jnp.where(some, top + jnp.log(safe), -1e30)
            hi, mid, low = split3(lse)
            stat = jnp.concatenate(
                [hi.astype(F32), mid.astype(F32), low.astype(F32)]
                + [jnp.zeros((STAT - 3, 2 * seat), F32)],
                axis=0,
            ).astype(BF)
            if heads == 2 and requests == 1:
                out[j, :depth, :] = mixed
                out[j, depth:, :] = stat
            else:
                for e in range(2):
                    mine = slice(e * seat, (e + 1) * seat)
                    head = 2 * j + e
                    lo = (head % heads) * count + q * seat
                    for part in range(HD // depth):
                        dest = (head * HD + part * depth) // cols
                        out[dest, :depth, lo : lo + seat] = mixed[
                            part * depth : (part + 1) * depth, mine
                        ]
                        out[dest, depth:, lo : lo + seat] = stat[:, mine]


def attention(pieces, k_own, v_own, k_oth, v_oth, lengths, chips):
    nz = len(pieces)
    per = pieces[0].shape[1]
    count = chips * per
    cols = HQ * HD // chips
    heads = max(1, cols // HD)
    shape = (chips, min(cols, HD) + STAT, heads * count)
    work = 4 * k_own.size * (HQ // KVH) * 2 * count
    return pl.pallas_call(
        functools.partial(attention_kernel, nz),
        out_shape=jax.ShapeDtypeStruct(shape, BF),
        in_specs=[pl.BlockSpec(memory_space=pltpu.SMEM)]
        + [pl.BlockSpec(memory_space=pltpu.VMEM)] * (nz + 4),
        out_specs=pl.BlockSpec(memory_space=pltpu.VMEM),
        scratch_shapes=[pltpu.VMEM((count, HQ * HD), F32)],
        cost_estimate=pl.CostEstimate(
            flops=work, bytes_accessed=8 * k_own.size, transcendentals=work // (4 * HD)
        ),
        name="attention",
    )(lengths, *pieces, k_own, v_own, k_oth, v_oth)


def project_kernel(per, nz, width, counts, got, w_own, w_oth, res_own, res_oth, order, *refs):
    outs, sent, part = refs[:nz], refs[nz], refs[nz + 1]
    device, core, chip, z = place()
    chips, depth = got.shape[0], got.shape[1] - STAT
    count = part.shape[0]
    rows = order.shape[1]
    cap = res_own.shape[0]
    heads = got.shape[2] // count
    lse = [
        jnp.sum(got[i, depth:, :].astype(F32), axis=0, keepdims=True) for i in range(chips)
    ]
    best = functools.reduce(jnp.maximum, lse)
    factor = [jnp.exp(x - best) for x in lse]
    denom = functools.reduce(lambda a, b: a + b, factor)
    merged = functools.reduce(
        lambda a, b: a + b, [got[i, :depth, :].astype(F32) * factor[i] for i in range(chips)]
    )
    merged = (merged / denom).T.astype(BF)
    if heads == 2:
        first, second = merged[:count], merged[count:]
        attn = jnp.concatenate([first, second], axis=1)
    else:
        first, second = merged[:, : depth // 2], merged[:, depth // 2 :]
        attn = merged
    low = (core == 0).astype(F32)
    first, second = first.astype(F32), second.astype(F32)
    own = (first * low + second * (1.0 - low)).astype(BF)
    oth = (second * low + first * (1.0 - low)).astype(BF)
    ids = row_ids(count, per, core, 0, (count, rows))
    at = (order[...] == ids).astype(F32).astype(BF)
    start = owner_start(counts, device, width)
    start_oth = owner_start(counts, device ^ 1, width)
    take_own = dot(at, owner_picks(counts, device, start, cap, rows), NT).astype(BF)
    take_oth = dot(at, owner_picks(counts, device ^ 1, start_oth, cap, rows), NT).astype(BF)
    part[...] = dot(take_own, res_own[...], NN) + dot(take_oth, res_oth[...], NN)
    part[:, :D] += dot(own, w_own[...], NN) + dot(oth, w_oth[...], NN)
    block = outs[0].shape[0]
    for kz in range(nz):
        spot = pl.multiple_of((z ^ kz) * block, block)
        outs[kz][...] = part[pl.ds(spot, block), :].astype(BF)
    begin = jnp.int32(0)
    for o in range(width):
        take = dot(owner_picks(counts, o, begin, cap, rows), at, NT).astype(BF)
        sent[o] = dot(take, attn, NN).astype(BF)
        begin = begin + counts[o]


def project(got, w_own, w_oth, res_own, res_oth, order, counts, per, nz, width):
    chips = got.shape[0]
    count = chips * per
    cols = D // chips
    wide = res_own.shape[1]
    cap = res_own.shape[0]
    return pl.pallas_call(
        functools.partial(project_kernel, per, nz, width),
        out_shape=[jax.ShapeDtypeStruct((count // nz, wide), BF)] * nz
        + [jax.ShapeDtypeStruct((width, cap, cols), BF)],
        in_specs=[pl.BlockSpec(memory_space=pltpu.SMEM)]
        + [pl.BlockSpec(memory_space=pltpu.VMEM)] * 6,
        out_specs=[pl.BlockSpec(memory_space=pltpu.VMEM)] * (nz + 1),
        scratch_shapes=[pltpu.VMEM((count, wide), F32)],
        cost_estimate=pl.CostEstimate(
            flops=2 * count * cols * D, bytes_accessed=4 * cols * D, transcendentals=0
        ),
        name="project",
    )(counts, got, w_own, w_oth, res_own, res_oth, order)


def expert_kernel(per, nz, width, counts, *refs):
    mine, theirs = refs[:nz], refs[nz : 2 * nz]
    (gain, gate_up, down, order, keep0, keep1, send0, send1, stream_own) = refs[
        2 * nz : 2 * nz + 9
    ]
    x, normed, hidden, scaled = refs[2 * nz + 9 :]
    device, core, chip, z = place()
    block = mine[0].shape[0]
    half = block * nz
    rows = order.shape[1]
    cap = stream_own.shape[0]
    experts = width
    for kz in range(nz):
        spot = (z ^ kz) * block
        x[pl.ds(pl.multiple_of(core * half + spot, block), block), :] = mine[kz][...]
        x[pl.ds(pl.multiple_of((1 - core) * half + spot, block), block), :] = theirs[kz][...]
    stream = x[:, :D].astype(F32)
    scale = lax.rsqrt(jnp.mean(stream * stream, axis=-1, keepdims=True) + 1e-06)
    normed[...] = (stream * scale * gain[...]).astype(BF)
    extra = x[:, D:].astype(F32)
    lane = lax.broadcasted_iota(jnp.int32, extra.shape, 1)
    pick = (lane == device) | (lane == device + experts)
    weight = jnp.sum(jnp.where(pick, extra, 0.0), axis=-1, keepdims=True)
    tile = 256
    def up(n, _):
        lo = pl.multiple_of(n * tile, tile)
        hi = pl.multiple_of(EFF + n * tile, tile)
        g = dot(normed[...], gate_up[0, :, pl.ds(lo, tile)], NN)
        u = dot(normed[...], gate_up[0, :, pl.ds(hi, tile)], NN)
        hidden[:, pl.ds(lo, tile)] = (g / (1.0 + jnp.exp(-g)) * u).astype(BF)
        return 0
    lax.fori_loop(0, EFF // tile, up, 0)
    both = jnp.concatenate(
        [row_ids(half, per, c, 0, (half, rows)) for c in range(2)], axis=0
    )
    at = (order[...] == both).astype(F32).astype(BF)
    starts = [jnp.int32(0)]
    for o in range(width):
        starts.append(starts[-1] + counts[o])
    def picks(owner):
        start = owner_start(counts, owner, width)
        return owner_picks(counts, owner, start, cap, rows)
    def downs(n, _):
        lo = pl.multiple_of(n * tile, tile)
        y = dot(hidden[...], down[0, :, pl.ds(lo, tile)], NN).astype(BF)
        scaled[:, pl.ds(lo, tile)] = (y.astype(F32) * weight).astype(BF)
        return 0
    lax.fori_loop(0, D // tile, downs, 0)
    for kc, ky, target in ((0, 0, keep0), (0, 1, keep1), (1, 0, send0), (1, 1, send1)):
        near = jnp.concatenate(
            [picks(device ^ (kc + 2 * ky + 4 * kz)) for kz in range(nz)], axis=0
        )
        take = dot(near, at, NT).astype(BF)
        target[...] = dot(take, scaled[...], NN).astype(BF)
        if kc == 0 and ky == 0:
            stream_own[...] = dot(take[:cap], x[:, :D], NN).astype(BF)


def experts(mine, theirs, gain, gate_up, down, order, counts, per, width, cap):
    nz = len(mine)
    block, wide = mine[0].shape
    total = 2 * nz * block
    wide_out = jax.ShapeDtypeStruct((nz * cap, D), BF)
    return pl.pallas_call(
        functools.partial(expert_kernel, per, nz, width),
        out_shape=[wide_out] * 4 + [jax.ShapeDtypeStruct((cap, D), BF)],
        in_specs=[pl.BlockSpec(memory_space=pltpu.SMEM)]
        + [pl.BlockSpec(memory_space=pltpu.VMEM)] * (2 * nz + 4),
        out_specs=[pl.BlockSpec(memory_space=pltpu.VMEM)] * 5,
        scratch_shapes=[
            pltpu.VMEM((total, wide), BF),
            pltpu.VMEM((total, D), BF),
            pltpu.VMEM((total, EFF), BF),
            pltpu.VMEM((total, D), BF),
        ],
        cost_estimate=pl.CostEstimate(
            flops=6 * total * D * EFF, bytes_accessed=6 * D * EFF, transcendentals=total * EFF
        ),
        name="experts",
    )(counts, *mine, *theirs, gain, gate_up, down, order)


def route_columns(expert_ids, route_weights, width):
    norm = route_weights / jnp.sum(route_weights, axis=-1, keepdims=True)
    lanes = -(-2 * width // 128) * 128
    lane = jnp.arange(lanes, dtype=jnp.int32)
    hit = expert_ids[:, :, None] == (lane % width)[None, None, :]
    dense = jnp.sum(jnp.where(hit, norm[:, :, None], 0.0), axis=1)
    hi = dense.astype(BF)
    low = (dense - hi.astype(F32)).astype(BF)
    kind = (lane // width)[None, :]
    return jnp.where(kind == 0, hi, jnp.where(kind == 1, low, jnp.zeros_like(hi)))


def body(
    queries,
    keys,
    values,
    lengths,
    owner_counts,
    row_order,
    residual,
    out_weight,
    norm_gain,
    expert_ids,
    route_weights,
    gate_up,
    expert_down,
):
    width = lax.axis_size("ctx")
    chips, nz = width // 2, width // 4
    per = queries.shape[0]
    cap = residual.shape[0]
    order = row_order.reshape(1, -1)
    zs = [4 * kz for kz in range(1, nz)]
    same_core = [[2 * i + c for i in range(chips)] for c in range(2)]

    near = hop(queries, 2, width)
    k_oth, v_oth = hop(keys, 1, width), hop(values, 1, width)
    column = jnp.stack([queries, near])
    pieces = [column] + [hop(column, m, width) for m in zs]
    w_oth = hop(out_weight, 1, width)
    res_own = jnp.concatenate([residual, route_columns(expert_ids, route_weights, width)], axis=1)
    res_oth = hop(res_own, 1, width)

    partial = attention(pieces, keys, values, k_oth, v_oth, lengths, chips)
    got = lax.all_to_all(
        partial, "ctx", split_axis=0, concat_axis=0, tiled=True, axis_index_groups=same_core
    )
    *parts, sent = project(
        got, out_weight, w_oth, res_own, res_oth, order, owner_counts, per, nz, width
    )
    attn = lax.all_to_all(sent, "ctx", split_axis=0, concat_axis=0, tiled=True)

    def add(*terms):
        return functools.reduce(lambda a, b: a + b, [t.astype(F32) for t in terms]).astype(BF)

    chunk = add(parts[0], *[hop(p, m, width) for p, m in zip(parts[1:], zs)])
    chunk = add(chunk, hop(chunk, 2, width))
    mine = [chunk] + [hop(chunk, m, width) for m in zs]
    theirs = [hop(x, 1, width) for x in mine]
    keep0, keep1, send0, send1, stream = experts(
        mine,
        theirs,
        norm_gain.reshape(1, -1),
        gate_up,
        expert_down,
        order,
        owner_counts,
        per,
        width,
        cap,
    )
    far = add(keep1, hop(send1, 1, width))
    close = add(keep0, hop(send0, 1, width))
    close = add(close, hop(far, 2, width)).reshape(nz, cap, D)
    moe = [close[0]] + [hop(close[kz], 4 * kz, width) for kz in range(1, nz)]
    layer_out = add(stream, *moe)

    cols = D // chips
    attn = attn.reshape(chips, 2, cap, cols)
    attn_own = jnp.transpose(attn[:, 0] + attn[:, 1], (1, 0, 2)).reshape(cap, D)
    return (attn_own, layer_out)


def solution(mesh):
    placed = (
        P(("groups", "ctx"), None),
        P("groups", "ctx", None),
        P("groups", "ctx", None),
        P("groups"),
        P("groups"),
        P("groups"),
        P(("groups", "ctx"), None),
        P("ctx", None),
        P(),
        P(("groups", "ctx"), None),
        P(("groups", "ctx"), None),
        P("ctx", None, None),
        P("ctx", None, None),
    )
    return jax.shard_map(
        body,
        mesh=mesh,
        in_specs=placed,
        out_specs=(P(("groups", "ctx"), None), P(("groups", "ctx"), None)),
        check_vma=False,
    )
```

```python
import functools

import jax
import jax.numpy as jnp
from jax import lax
from jax.experimental import pallas as pl
from jax.experimental.pallas import tpu as pltpu
from jax.sharding import PartitionSpec as P

D = 2048
HQ = 16
KVH = 2
HD = 128
EFF = 768
TOPK = 8
STRETCH = 128
BF = jnp.bfloat16
F32 = jnp.float32
MIB = 1 << 20
UPS, DOWNS = 3, 4
STAT = 8


NT = (((1,), (1,)), ((), ()))
NN = (((1,), (0,)), ((), ()))
TN = (((0,), (0,)), ((), ()))


def dot(a, b, dims):
    return lax.dot_general(a, b, dims, preferred_element_type=F32)


def place():
    device = lax.axis_index("ctx")
    return device, device & 1, device >> 1, device >> 2


def hop(x, mask, width):
    return lax.ppermute(x, "ctx", [(i, i ^ mask) for i in range(width)])


def split3(x):
    hi = x.astype(BF)
    rest = x - hi.astype(F32)
    mid = rest.astype(BF)
    return hi, mid, (rest - mid.astype(F32)).astype(BF)


def row_ids(count, per, core, axis, shape):
    i = lax.broadcasted_iota(jnp.int32, shape, axis)
    return (i // per) * (2 * per) + core * per + i % per


def prepare_kernel(per, width, counts, order, ids, weights, residual, res, home, fill, turn, picks, table):
    device, core, chip, z = place()
    cap, rows = residual.shape[0], order.shape[1]
    half = home.shape[0]
    p = lax.broadcasted_iota(jnp.int32, (cap, rows), 1)
    j = lax.broadcasted_iota(jnp.int32, (cap, rows), 0)
    start = jnp.int32(0)
    for o in range(width):
        hit = (p - start == j) & (j < counts[o])
        picks[o * cap : (o + 1) * cap, :] = hit.astype(F32).astype(BF)
        start = start + counts[o]
    seats = [
        (order[...] == row_ids(half, per, c, 0, (half, rows))).astype(F32).astype(BF)
        for c in range(2)
    ]
    mine = (order[...] == row_ids(half, per, core, 0, (half, rows))).astype(F32).astype(BF)
    fill[...] = dot(picks[...], mine, NT).astype(BF)
    table[...] = dot(picks[...], jnp.concatenate(seats, axis=0), NT).astype(BF)
    for kc in range(2):
        for ky in range(2):
            for kz in range(width // 4):
                owner = device ^ (kc + 2 * ky + 4 * kz)
                to = (kc * 2 + ky) * (width // 4) + kz
                turn[to * cap : (to + 1) * cap, :] = table[
                    pl.ds(pl.multiple_of(owner * cap, cap), cap), :
                ]
    chip_picks = [
        picks[pl.ds(pl.multiple_of(o * cap, cap), cap), :] for o in (device, device ^ 1)
    ]
    home[...] = dot(mine, jnp.concatenate(chip_picks, axis=0), NT).astype(BF)
    lanes = res.shape[1] - D
    lane = lax.broadcasted_iota(jnp.int32, (cap, lanes), 1)
    norm = weights[...] / jnp.sum(weights[...], axis=-1, keepdims=True)
    dense = jnp.zeros((cap, lanes), F32)
    for k in range(TOPK):
        hit = ids[:, k : k + 1] == lane % width
        dense = dense + jnp.where(hit, norm[:, k : k + 1], 0.0)
    high = dense.astype(BF).astype(F32)
    low = jnp.where(lane < 2 * width, dense - high, 0.0)
    res[:, :D] = residual[...]
    res[:, D:] = jnp.where(lane < width, high, low).astype(BF)


def prepare(counts, order, ids, weights, residual, per, width):
    cap, rows = residual.shape[0], order.shape[1]
    half = width // 2 * per
    lanes = -(-2 * width // 128) * 128
    slots = width * cap
    return pl.pallas_call(
        functools.partial(prepare_kernel, per, width),
        out_shape=[
            jax.ShapeDtypeStruct((cap, D + lanes), BF),
            jax.ShapeDtypeStruct((half, 2 * cap), BF),
            jax.ShapeDtypeStruct((slots, half), BF),
            jax.ShapeDtypeStruct((slots, 2 * half), BF),
        ],
        in_specs=[pl.BlockSpec(memory_space=pltpu.SMEM)]
        + [pl.BlockSpec(memory_space=pltpu.VMEM)] * 4,
        out_specs=[pl.BlockSpec(memory_space=pltpu.VMEM)] * 4,
        scratch_shapes=[pltpu.VMEM((slots, rows), BF), pltpu.VMEM((slots, 2 * half), BF)],
        cost_estimate=pl.CostEstimate(
            flops=6 * slots * rows * half, bytes_accessed=8 * slots * half, transcendentals=0
        ),
        compiler_params=pltpu.CompilerParams(vmem_limit_bytes=8 * MIB),
        name="prepare",
    )(counts, order, ids, weights, residual)


def attention_kernel(nz, lengths, *refs):
    pieces, (k_own, v_own, k_oth, v_oth, out, rows) = refs[:nz], refs[nz:]
    device, core, chip, z = place()
    per = pieces[0].shape[1]
    requests, span = k_own.shape[0], k_own.shape[1]
    count = rows.shape[0]
    seat = count // requests
    chips, depth = out.shape[0], out.shape[1] - STAT
    cols = HQ * HD // chips
    heads = max(1, cols // HD)
    for kz in range(nz):
        both = pieces[kz][...].astype(F32)
        for ky in range(2):
            spot = (chip ^ (2 * kz + ky)) * per
            rows[pl.ds(pl.multiple_of(spot, per), per), :] = both[ky]
    key = lax.broadcasted_iota(jnp.int32, (span, 2 * seat), 0)
    lane = lax.broadcasted_iota(jnp.int32, (1, 2 * seat), 1) % seat
    ahead = (lane // per) * (2 * per) + core * per + lane % per - STRETCH
    first_own, first_oth = device * span, (device ^ 1) * span
    for q in range(requests):
        last = lengths[q] + ahead
        see_own, see_oth = key <= last - first_own, key <= last - first_oth
        for j in range(HQ // 2):
            v = 2 * j // (HQ // KVH)
            kv = slice(v * HD, (v + 1) * HD)
            if 2 * j % (HQ // KVH) == 0:
                vt_own, vt_oth = v_own[q, :, kv].T, v_oth[q, :, kv].T
            pair = jnp.concatenate(
                [
                    rows[q * seat : (q + 1) * seat, (2 * j + e) * HD : (2 * j + e + 1) * HD]
                    for e in range(2)
                ],
                axis=0,
            ).astype(BF)
            s_own = dot(k_own[q, :, kv], pair, NT) * HD ** (-0.5)
            s_oth = dot(k_oth[q, :, kv], pair, NT) * HD ** (-0.5)
            s_own = jnp.where(see_own, s_own, -1e30)
            s_oth = jnp.where(see_oth, s_oth, -1e30)
            top = jnp.maximum(
                jnp.max(s_own, axis=0, keepdims=True), jnp.max(s_oth, axis=0, keepdims=True)
            )
            w_own = jnp.where(see_own, jnp.exp(s_own - top), 0.0)
            w_oth = jnp.where(see_oth, jnp.exp(s_oth - top), 0.0)
            total = jnp.sum(w_own, axis=0, keepdims=True) + jnp.sum(w_oth, axis=0, keepdims=True)
            mixed = dot(vt_own, w_own.astype(BF), NN) + dot(vt_oth, w_oth.astype(BF), NN)
            some = total > 0.0
            safe = jnp.where(some, total, 1.0)
            mixed = (mixed / safe).astype(BF)
            lse = jnp.where(some, top + jnp.log(safe), -1e30)
            hi, mid, low = split3(lse)
            stat = jnp.concatenate(
                [hi.astype(F32), mid.astype(F32), low.astype(F32)]
                + [jnp.zeros((STAT - 3, 2 * seat), F32)],
                axis=0,
            ).astype(BF)
            if heads == 2 and requests == 1:
                out[j, :depth, :] = mixed
                out[j, depth:, :] = stat
            else:
                for e in range(2):
                    mine = slice(e * seat, (e + 1) * seat)
                    head = 2 * j + e
                    lo = (head % heads) * count + q * seat
                    for part in range(HD // depth):
                        dest = (head * HD + part * depth) // cols
                        out[dest, :depth, lo : lo + seat] = mixed[
                            part * depth : (part + 1) * depth, mine
                        ]
                        out[dest, depth:, lo : lo + seat] = stat[:, mine]


def attention(pieces, k_own, v_own, k_oth, v_oth, lengths, chips):
    nz = len(pieces)
    per = pieces[0].shape[1]
    count = chips * per
    cols = HQ * HD // chips
    heads = max(1, cols // HD)
    shape = (chips, min(cols, HD) + STAT, heads * count)
    work = 4 * k_own.size * (HQ // KVH) * 2 * count
    return pl.pallas_call(
        functools.partial(attention_kernel, nz),
        out_shape=jax.ShapeDtypeStruct(shape, BF),
        in_specs=[pl.BlockSpec(memory_space=pltpu.SMEM)]
        + [pl.BlockSpec(memory_space=pltpu.VMEM)] * (nz + 4),
        out_specs=pl.BlockSpec(memory_space=pltpu.VMEM),
        scratch_shapes=[pltpu.VMEM((count, HQ * HD), F32)],
        cost_estimate=pl.CostEstimate(
            flops=work, bytes_accessed=8 * k_own.size, transcendentals=work // (4 * HD)
        ),
        compiler_params=pltpu.CompilerParams(vmem_limit_bytes=16 * MIB),
        name="attention",
    )(lengths, *pieces, k_own, v_own, k_oth, v_oth)


def project_kernel(nz, got, w_own, w_oth, res_own, res_oth, home, *refs):
    outs, attn, part = refs[:nz], refs[nz], refs[nz + 1]
    device, core, chip, z = place()
    chips, depth = got.shape[0], got.shape[1] - STAT
    count = part.shape[0]
    heads = got.shape[2] // count
    lse = [
        jnp.sum(got[i, depth:, :].astype(F32), axis=0, keepdims=True) for i in range(chips)
    ]
    best = functools.reduce(jnp.maximum, lse)
    factor = [jnp.exp(x - best) for x in lse]
    denom = functools.reduce(lambda a, b: a + b, factor)
    merged = functools.reduce(
        lambda a, b: a + b, [got[i, :depth, :].astype(F32) * factor[i] for i in range(chips)]
    )
    merged = (merged / denom).T.astype(BF)
    if heads == 2:
        first, second = merged[:count], merged[count:]
        attn[...] = jnp.concatenate([first, second], axis=1)
    else:
        first, second = merged[:, : depth // 2], merged[:, depth // 2 :]
        attn[...] = merged
    low = (core == 0).astype(F32)
    first, second = first.astype(F32), second.astype(F32)
    own = (first * low + second * (1.0 - low)).astype(BF)
    oth = (second * low + first * (1.0 - low)).astype(BF)
    res = jnp.concatenate([res_own[...], res_oth[...]], axis=0)
    part[:, :D] = (
        dot(home[...], res[:, :D], NN) + dot(own, w_own[...], NN) + dot(oth, w_oth[...], NN)
    )
    part[:, D:] = dot(home[...], res[:, D:], NN)
    block = outs[0].shape[0]
    for kz in range(nz):
        spot = pl.multiple_of((z ^ kz) * block, block)
        outs[kz][...] = part[pl.ds(spot, block), :].astype(BF)


def project(got, w_own, w_oth, res_own, res_oth, home, nz):
    chips = got.shape[0]
    count = home.shape[0]
    cols = D // chips
    wide = res_own.shape[1]
    return pl.pallas_call(
        functools.partial(project_kernel, nz),
        out_shape=[jax.ShapeDtypeStruct((count // nz, wide), BF)] * nz
        + [jax.ShapeDtypeStruct((count, cols), BF)],
        in_specs=[pl.BlockSpec(memory_space=pltpu.VMEM)] * 6,
        out_specs=[pl.BlockSpec(memory_space=pltpu.VMEM)] * (nz + 1),
        scratch_shapes=[pltpu.VMEM((count, wide), F32)],
        cost_estimate=pl.CostEstimate(
            flops=2 * count * cols * D, bytes_accessed=4 * cols * D, transcendentals=0
        ),
        compiler_params=pltpu.CompilerParams(vmem_limit_bytes=12 * MIB),
        name="project",
    )(got, w_own, w_oth, res_own, res_oth, home)


def expert_kernel(nz, width, *refs):
    mine, theirs = refs[:nz], refs[nz : 2 * nz]
    (gain, gate_up, down, turn, keep0, keep1, send0, send1, stream_own) = refs[
        2 * nz : 2 * nz + 9
    ]
    x, normed, hidden, scaled, up_buf, down_buf, up_sem, down_sem = refs[2 * nz + 9 :]
    device, core, chip, z = place()
    tile = EFF // up_buf.shape[0] * 2
    wide = D // down_buf.shape[0]
    ups, downs = [], []
    for n in range(up_buf.shape[0]):
        lo = n // 2 * tile + n % 2 * EFF
        ups.append(
            pltpu.make_async_copy(gate_up.at[0, :, pl.ds(lo, tile)], up_buf.at[n], up_sem.at[n])
        )
    for n in range(down_buf.shape[0]):
        downs.append(
            pltpu.make_async_copy(
                down.at[0, :, pl.ds(n * wide, wide)], down_buf.at[n], down_sem.at[n]
            )
        )
    for copy in ups + downs:
        copy.start()
    block = mine[0].shape[0]
    half = block * nz
    cap = stream_own.shape[0]
    for kz in range(nz):
        spot = (z ^ kz) * block
        x[pl.ds(pl.multiple_of(core * half + spot, block), block), :] = mine[kz][...]
        x[pl.ds(pl.multiple_of((1 - core) * half + spot, block), block), :] = theirs[kz][...]
    stream = x[:, :D].astype(F32)
    scale = lax.rsqrt(jnp.mean(stream * stream, axis=-1, keepdims=True) + 1e-06)
    normed[...] = (stream * scale * gain[...]).astype(BF)
    extra = x[:, D:].astype(F32)
    lane = lax.broadcasted_iota(jnp.int32, extra.shape, 1)
    pick = (lane == device) | (lane == device + width)
    weight = jnp.sum(jnp.where(pick, extra, 0.0), axis=-1, keepdims=True)
    for n in range(0, len(ups), 2):
        lo = n // 2 * tile
        ups[n].wait()
        g = dot(normed[...], up_buf[n], NN)
        ups[n + 1].wait()
        u = dot(normed[...], up_buf[n + 1], NN)
        hidden[:, lo : lo + tile] = (g / (1.0 + jnp.exp(-g)) * u).astype(BF)
    for n in range(len(downs)):
        downs[n].wait()
        y = dot(hidden[...], down_buf[n], NN).astype(BF)
        scaled[:, n * wide : (n + 1) * wide] = (y.astype(F32) * weight).astype(BF)
    for k, target in enumerate((keep0, keep1, send0, send1)):
        size = target.shape[0]
        target[...] = dot(turn[k * size : (k + 1) * size, :], scaled[...], NN).astype(BF)
    stream_own[...] = dot(turn[:cap, :], x[:, :D], NN).astype(BF)


def experts(mine, theirs, gain, gate_up, down, turn, width, cap):
    nz = len(mine)
    block, wide = mine[0].shape
    total = 2 * nz * block
    wide_out = jax.ShapeDtypeStruct((nz * cap, D), BF)
    return pl.pallas_call(
        functools.partial(expert_kernel, nz, width),
        out_shape=[wide_out] * 4 + [jax.ShapeDtypeStruct((cap, D), BF)],
        in_specs=[pl.BlockSpec(memory_space=pltpu.VMEM)] * (2 * nz + 1)
        + [pl.BlockSpec(memory_space=pltpu.HBM)] * 2
        + [pl.BlockSpec(memory_space=pltpu.VMEM)],
        out_specs=[pl.BlockSpec(memory_space=pltpu.VMEM)] * 5,
        scratch_shapes=[
            pltpu.VMEM((total, wide), BF),
            pltpu.VMEM((total, D), BF),
            pltpu.VMEM((total, EFF), BF),
            pltpu.VMEM((total, D), BF),
            pltpu.VMEM((2 * UPS, D, EFF // UPS), BF),
            pltpu.VMEM((DOWNS, EFF, D // DOWNS), BF),
            pltpu.SemaphoreType.DMA((2 * UPS,)),
            pltpu.SemaphoreType.DMA((DOWNS,)),
        ],
        cost_estimate=pl.CostEstimate(
            flops=6 * total * D * EFF, bytes_accessed=6 * D * EFF, transcendentals=total * EFF
        ),
        compiler_params=pltpu.CompilerParams(vmem_limit_bytes=53_500_000),
        name="experts",
    )(*mine, *theirs, gain, gate_up, down, turn)


def body(
    queries,
    keys,
    values,
    lengths,
    owner_counts,
    row_order,
    residual,
    out_weight,
    norm_gain,
    expert_ids,
    route_weights,
    gate_up,
    expert_down,
):
    width = lax.axis_size("ctx")
    chips, nz = width // 2, width // 4
    per = queries.shape[0]
    cap = residual.shape[0]
    order = row_order.reshape(1, -1)
    zs = [4 * kz for kz in range(1, nz)]
    same_core = [[2 * i + c for i in range(chips)] for c in range(2)]

    near = hop(queries, 2, width)
    k_oth, v_oth = hop(keys, 1, width), hop(values, 1, width)
    column = jnp.stack([queries, near])
    pieces = [column] + [hop(column, m, width) for m in zs]
    w_oth = hop(out_weight, 1, width)
    res_own, home, fill, turn = prepare(
        owner_counts, order, expert_ids, route_weights, residual, per, width
    )
    res_oth = hop(res_own, 1, width)

    partial = attention(pieces, keys, values, k_oth, v_oth, lengths, chips)
    got = lax.all_to_all(
        partial, "ctx", split_axis=0, concat_axis=0, tiled=True, axis_index_groups=same_core
    )
    *parts, mixed = project(got, out_weight, w_oth, res_own, res_oth, home, nz)
    sent = jnp.dot(fill, mixed, preferred_element_type=F32).astype(BF)
    attn = lax.all_to_all(sent, "ctx", split_axis=0, concat_axis=0, tiled=True)

    def add(*terms):
        return functools.reduce(lambda a, b: a + b, [t.astype(F32) for t in terms]).astype(BF)

    chunk = add(parts[0], *[hop(p, m, width) for p, m in zip(parts[1:], zs)])
    chunk = add(chunk, hop(chunk, 2, width))
    mine = [chunk] + [hop(chunk, m, width) for m in zs]
    theirs = [hop(x, 1, width) for x in mine]
    keep0, keep1, send0, send1, stream = experts(
        mine,
        theirs,
        norm_gain.reshape(1, -1),
        gate_up,
        expert_down,
        turn,
        width,
        cap,
    )
    far = add(keep1, hop(send1, 1, width))
    close = add(keep0, hop(send0, 1, width))
    close = add(close, hop(far, 2, width)).reshape(nz, cap, D)
    moe = [close[0]] + [hop(close[kz], 4 * kz, width) for kz in range(1, nz)]
    layer_out = add(stream, *moe)

    cols = D // chips
    attn = attn.reshape(chips, 2, cap, cols)
    attn_own = jnp.transpose(attn[:, 0] + attn[:, 1], (1, 0, 2)).reshape(cap, D)
    return (attn_own, layer_out)


def solution(mesh):
    placed = (
        P(("groups", "ctx"), None),
        P("groups", "ctx", None),
        P("groups", "ctx", None),
        P("groups"),
        P("groups"),
        P("groups"),
        P(("groups", "ctx"), None),
        P("ctx", None),
        P(),
        P(("groups", "ctx"), None),
        P(("groups", "ctx"), None),
        P("ctx", None, None),
        P("ctx", None, None),
    )
    return jax.shard_map(
        body,
        mesh=mesh,
        in_specs=placed,
        out_specs=(P(("groups", "ctx"), None), P(("groups", "ctx"), None)),
        check_vma=False,
    )
```

```python
import functools

import jax
import jax.numpy as jnp
from jax import lax
from jax.experimental import pallas as pl
from jax.experimental.pallas import tpu as pltpu
from jax.sharding import PartitionSpec as P


D = 2048
HQ = 16
KVH = 2
HD = 128
EFF = 768
TOPK = 8
STRETCH = 128
BF = jnp.bfloat16
F32 = jnp.float32
MIB = 1 << 20
STAT = 8


NT = (((1,), (1,)), ((), ()))
NN = (((1,), (0,)), ((), ()))


def dot(a, b, dims):
    return lax.dot_general(a, b, dims, preferred_element_type=F32)


def place():
    device = lax.axis_index("ctx")
    return device, device & 1, device >> 1, device >> 2


def hop(x, mask, width):
    return lax.ppermute(x, "ctx", [(i, i ^ mask) for i in range(width)])


def split3(x):
    hi = x.astype(BF)
    rest = x - hi.astype(F32)
    mid = rest.astype(BF)
    return hi, mid, (rest - mid.astype(F32)).astype(BF)


def row_ids(per, core, axis, shape):
    i = lax.broadcasted_iota(jnp.int32, shape, axis)
    return (i // per) * (2 * per) + core * per + i % per


def fetch_kernel(count, *refs):
    sems = refs[2 * count]
    copies = [
        pltpu.make_async_copy(refs[i], refs[count + i], sems.at[i]) for i in range(count)
    ]
    for copy in copies:
        copy.start()
    for copy in copies:
        copy.wait()


def in_hbm(x):
    return pltpu.with_memory_space_constraint(x, pltpu.HBM)


def fetch(*arrays):
    count = len(arrays)
    size = sum(a.size * a.dtype.itemsize for a in arrays)
    return pl.pallas_call(
        functools.partial(fetch_kernel, count),
        out_shape=[pltpu.VMEM(a.shape, a.dtype) for a in arrays],
        in_specs=[pl.BlockSpec(memory_space=pltpu.HBM)] * count,
        out_specs=[pl.BlockSpec(memory_space=pltpu.VMEM)] * count,
        scratch_shapes=[pltpu.SemaphoreType.DMA((count,))],
        cost_estimate=pl.CostEstimate(flops=0, bytes_accessed=2 * size, transcendentals=0),
        compiler_params=pltpu.CompilerParams(vmem_limit_bytes=16 * MIB),
        name="fetch",
    )(*[in_hbm(a) for a in arrays])


def prepare_kernel(per, width, counts, order, ids, weights, residual, res, home, fill, turn, picks, table, own):
    device, core, _, _ = place()
    cap, rows = residual.shape[0], order.shape[1]
    half = home.shape[0]
    p = lax.broadcasted_iota(jnp.int32, (cap, rows), 1)
    j = lax.broadcasted_iota(jnp.int32, (cap, rows), 0)
    start = jnp.int32(0)
    for o in range(width):
        hit = (p - start == j) & (j < counts[o])
        picks[o * cap : (o + 1) * cap, :] = hit.astype(F32).astype(BF)
        start = start + counts[o]
    seats = [
        (order[...] == row_ids(per, c, 0, (half, rows))).astype(F32).astype(BF)
        for c in range(2)
    ]
    mine = (order[...] == row_ids(per, core, 0, (half, rows))).astype(F32).astype(BF)
    own[...] = dot(picks[...], mine, NT).astype(BF)
    table[...] = dot(picks[...], jnp.concatenate(seats, axis=0), NT).astype(BF)
    for kc in range(2):
        for ky in range(2):
            for kz in range(width // 4):
                owner = device ^ (kc + 2 * ky + 4 * kz)
                to = (kc * 2 + ky) * (width // 4) + kz
                there = pl.ds(pl.multiple_of(owner * cap, cap), cap)
                turn[to * cap : (to + 1) * cap, :] = table[there, :]
                fill[to * cap : (to + 1) * cap, :] = own[there, :]
    chip_picks = [
        picks[pl.ds(pl.multiple_of(o * cap, cap), cap), :] for o in (device, device ^ 1)
    ]
    home[...] = dot(mine, jnp.concatenate(chip_picks, axis=0), NT).astype(BF)
    lanes = res.shape[1] - D
    lane = lax.broadcasted_iota(jnp.int32, (cap, lanes), 1)
    norm = weights[...] / jnp.sum(weights[...], axis=-1, keepdims=True)
    dense = jnp.zeros((cap, lanes), F32)
    for k in range(TOPK):
        hit = ids[:, k : k + 1] == lane % width
        dense = dense + jnp.where(hit, norm[:, k : k + 1], 0.0)
    high = dense.astype(BF).astype(F32)
    low = jnp.where(lane < 2 * width, dense - high, 0.0)
    res[:, :D] = residual[...]
    res[:, D:] = jnp.where(lane < width, high, low).astype(BF)


def prepare(counts, order, ids, weights, residual, per, width):
    cap, rows = residual.shape[0], order.shape[1]
    half = width // 2 * per
    lanes = -(-2 * width // 128) * 128
    slots = width * cap
    return pl.pallas_call(
        functools.partial(prepare_kernel, per, width),
        out_shape=[
            jax.ShapeDtypeStruct((cap, D + lanes), BF),
            jax.ShapeDtypeStruct((half, 2 * cap), BF),
            jax.ShapeDtypeStruct((slots, half), BF),
            jax.ShapeDtypeStruct((slots, 2 * half), BF),
        ],
        in_specs=[pl.BlockSpec(memory_space=pltpu.SMEM)]
        + [pl.BlockSpec(memory_space=pltpu.VMEM)] * 4,
        out_specs=[pl.BlockSpec(memory_space=pltpu.VMEM)] * 4,
        scratch_shapes=[
            pltpu.VMEM((slots, rows), BF),
            pltpu.VMEM((slots, 2 * half), BF),
            pltpu.VMEM((slots, half), BF),
        ],
        cost_estimate=pl.CostEstimate(
            flops=6 * slots * rows * half, bytes_accessed=8 * slots * half, transcendentals=0
        ),
        compiler_params=pltpu.CompilerParams(vmem_limit_bytes=8 * MIB),
        name="prepare",
    )(counts, in_hbm(order), ids, weights, in_hbm(residual))


def attention_kernel(nz, lengths, *refs):
    pieces, (k_own, v_own, k_oth, v_oth, out, rows) = refs[:nz], refs[nz:]
    device, core, chip, _ = place()
    per = pieces[0].shape[1]
    requests, span = k_own.shape[0], k_own.shape[1]
    count = rows.shape[0]
    seat = count // requests
    chips, depth = out.shape[0], out.shape[1] - STAT
    cols = HQ * HD // chips
    heads = max(1, cols // HD)
    for kz in range(nz):
        both = pieces[kz][...].astype(F32)
        for ky in range(2):
            spot = (chip ^ (2 * kz + ky)) * per
            rows[pl.ds(pl.multiple_of(spot, per), per), :] = both[ky]
    key = lax.broadcasted_iota(jnp.int32, (span, 2 * seat), 0)
    lane = lax.broadcasted_iota(jnp.int32, (1, 2 * seat), 1) % seat
    ahead = (lane // per) * (2 * per) + core * per + lane % per - STRETCH
    first_own, first_oth = device * span, (device ^ 1) * span
    for q in range(requests):
        last = lengths[q] + ahead
        see_own, see_oth = key <= last - first_own, key <= last - first_oth
        for j in range(HQ // 2):
            v = 2 * j // (HQ // KVH)
            kv = slice(v * HD, (v + 1) * HD)
            if 2 * j % (HQ // KVH) == 0:
                vt_own, vt_oth = v_own[q, :, kv].T, v_oth[q, :, kv].T
            pair = jnp.concatenate(
                [
                    rows[q * seat : (q + 1) * seat, (2 * j + e) * HD : (2 * j + e + 1) * HD]
                    for e in range(2)
                ],
                axis=0,
            ).astype(BF)
            s_own = dot(k_own[q, :, kv], pair, NT) * HD ** (-0.5)
            s_oth = dot(k_oth[q, :, kv], pair, NT) * HD ** (-0.5)
            s_own = jnp.where(see_own, s_own, -1e30)
            s_oth = jnp.where(see_oth, s_oth, -1e30)
            top = jnp.maximum(
                jnp.max(s_own, axis=0, keepdims=True), jnp.max(s_oth, axis=0, keepdims=True)
            )
            w_own = jnp.where(see_own, jnp.exp(s_own - top), 0.0)
            w_oth = jnp.where(see_oth, jnp.exp(s_oth - top), 0.0)
            total = jnp.sum(w_own, axis=0, keepdims=True) + jnp.sum(w_oth, axis=0, keepdims=True)
            mixed = dot(vt_own, w_own.astype(BF), NN) + dot(vt_oth, w_oth.astype(BF), NN)
            some = total > 0.0
            safe = jnp.where(some, total, 1.0)
            mixed = (mixed / safe).astype(BF)
            lse = jnp.where(some, top + jnp.log(safe), -1e30)
            hi, mid, low = split3(lse)
            stat = jnp.concatenate(
                [hi.astype(F32), mid.astype(F32), low.astype(F32)]
                + [jnp.zeros((STAT - 3, 2 * seat), F32)],
                axis=0,
            ).astype(BF)
            if heads == 2 and requests == 1:
                out[j, :depth, :] = mixed
                out[j, depth:, :] = stat
            else:
                for e in range(2):
                    mine = slice(e * seat, (e + 1) * seat)
                    head = 2 * j + e
                    lo = (head % heads) * count + q * seat
                    for part in range(HD // depth):
                        dest = (head * HD + part * depth) // cols
                        out[dest, :depth, lo : lo + seat] = mixed[
                            part * depth : (part + 1) * depth, mine
                        ]
                        out[dest, depth:, lo : lo + seat] = stat[:, mine]


def attention(pieces, k_own, v_own, k_oth, v_oth, lengths, chips):
    nz = len(pieces)
    per = pieces[0].shape[1]
    count = chips * per
    cols = HQ * HD // chips
    heads = max(1, cols // HD)
    shape = (chips, min(cols, HD) + STAT, heads * count)
    work = 4 * k_own.size * (HQ // KVH) * 2 * count
    return pl.pallas_call(
        functools.partial(attention_kernel, nz),
        out_shape=jax.ShapeDtypeStruct(shape, BF),
        in_specs=[pl.BlockSpec(memory_space=pltpu.SMEM)]
        + [pl.BlockSpec(memory_space=pltpu.VMEM)] * (nz + 4),
        out_specs=pl.BlockSpec(memory_space=pltpu.VMEM),
        scratch_shapes=[pltpu.VMEM((count, HQ * HD), F32)],
        cost_estimate=pl.CostEstimate(
            flops=work, bytes_accessed=8 * k_own.size, transcendentals=work // (4 * HD)
        ),
        compiler_params=pltpu.CompilerParams(vmem_limit_bytes=16 * MIB),
        name="attention",
    )(lengths, *pieces, k_own, v_own, k_oth, v_oth)


def project_kernel(nz, got, w_own, w_oth, res_own, res_oth, home, *refs):
    outs, attn, part = refs[:nz], refs[nz], refs[nz + 1]
    _, core, _, z = place()
    chips, depth = got.shape[0], got.shape[1] - STAT
    count = part.shape[0]
    heads = got.shape[2] // count
    lse = [
        jnp.sum(got[i, depth:, :].astype(F32), axis=0, keepdims=True) for i in range(chips)
    ]
    best = functools.reduce(jnp.maximum, lse)
    factor = [jnp.exp(x - best) for x in lse]
    denom = functools.reduce(lambda a, b: a + b, factor)
    merged = functools.reduce(
        lambda a, b: a + b, [got[i, :depth, :].astype(F32) * factor[i] for i in range(chips)]
    )
    merged = (merged / denom).T.astype(BF)
    if heads == 2:
        first, second = merged[:count], merged[count:]
        attn[...] = jnp.concatenate([first, second], axis=1)
    else:
        first, second = merged[:, : depth // 2], merged[:, depth // 2 :]
        attn[...] = merged
    low = (core == 0).astype(F32)
    first, second = first.astype(F32), second.astype(F32)
    own = (first * low + second * (1.0 - low)).astype(BF)
    oth = (second * low + first * (1.0 - low)).astype(BF)
    res = jnp.concatenate([res_own[...], res_oth[...]], axis=0)
    part[:, :D] = (
        dot(home[...], res[:, :D], NN) + dot(own, w_own[...], NN) + dot(oth, w_oth[...], NN)
    )
    part[:, D:] = dot(home[...], res[:, D:], NN)
    block = outs[0].shape[0]
    for kz in range(nz):
        spot = pl.multiple_of((z ^ kz) * block, block)
        outs[kz][...] = part[pl.ds(spot, block), :].astype(BF)


def project(got, w_own, w_oth, res_own, res_oth, home, nz):
    chips = got.shape[0]
    count = home.shape[0]
    cols = D // chips
    wide = res_own.shape[1]
    return pl.pallas_call(
        functools.partial(project_kernel, nz),
        out_shape=[jax.ShapeDtypeStruct((count // nz, wide), BF)] * nz
        + [jax.ShapeDtypeStruct((count, cols), BF)],
        in_specs=[pl.BlockSpec(memory_space=pltpu.VMEM)] * 6,
        out_specs=[pl.BlockSpec(memory_space=pltpu.VMEM)] * (nz + 1),
        scratch_shapes=[pltpu.VMEM((count, wide), F32)],
        cost_estimate=pl.CostEstimate(
            flops=2 * count * cols * D, bytes_accessed=4 * cols * D, transcendentals=0
        ),
        compiler_params=pltpu.CompilerParams(vmem_limit_bytes=12 * MIB),
        name="project",
    )(got, w_own, w_oth, res_own, res_oth, home)


def expert_kernel(nz, width, *refs):
    mine, theirs = refs[:nz], refs[nz : 2 * nz]
    (gain, gate_up, down, turn, fill, mixed, keep0, keep1, send0, send1, stream_own) = refs[
        2 * nz : 2 * nz + 11
    ]
    x, normed, hidden, scaled = refs[2 * nz + 11 :]
    device, core, _, z = place()
    block = mine[0].shape[0]
    half = block * nz
    cap = stream_own.shape[0]
    for kz in range(nz):
        spot = (z ^ kz) * block
        x[pl.ds(pl.multiple_of(core * half + spot, block), block), :] = mine[kz][...]
        x[pl.ds(pl.multiple_of((1 - core) * half + spot, block), block), :] = theirs[kz][...]
    stream = x[:, :D].astype(F32)
    scale = lax.rsqrt(jnp.mean(stream * stream, axis=-1, keepdims=True) + 1e-06)
    normed[...] = (stream * scale * gain[...]).astype(BF)
    extra = x[:, D:].astype(F32)
    lane = lax.broadcasted_iota(jnp.int32, extra.shape, 1)
    pick = (lane == device) | (lane == device + width)
    weight = jnp.sum(jnp.where(pick, extra, 0.0), axis=-1, keepdims=True)
    tile = 256
    for lo in range(0, EFF, tile):
        g = dot(normed[...], gate_up[0, :, lo : lo + tile], NN)
        u = dot(normed[...], gate_up[0, :, EFF + lo : EFF + lo + tile], NN)
        hidden[:, lo : lo + tile] = (g / (1.0 + jnp.exp(-g)) * u).astype(BF)
    for lo in range(0, D, tile):
        y = dot(hidden[...], down[0, :, lo : lo + tile], NN).astype(BF)
        scaled[:, lo : lo + tile] = (y.astype(F32) * weight).astype(BF)
    for k, target in enumerate((keep0, keep1, send0, send1)):
        size = target.shape[0]
        some = slice(k * size, (k + 1) * size)
        target[:, :D] = dot(turn[some, :], scaled[...], NN).astype(BF)
        target[:, D:] = dot(fill[some, :], mixed[...], NN).astype(BF)
    stream_own[...] = dot(turn[:cap, :], x[:, :D], NN).astype(BF)


def experts(mine, theirs, gain, gate_up, down, turn, fill, mixed, width, cap):
    nz = len(mine)
    block, wide = mine[0].shape
    total = 2 * nz * block
    wide_out = jax.ShapeDtypeStruct((nz * cap, D + mixed.shape[1]), BF)
    return pl.pallas_call(
        functools.partial(expert_kernel, nz, width),
        out_shape=[wide_out] * 4 + [jax.ShapeDtypeStruct((cap, D), BF)],
        in_specs=[pl.BlockSpec(memory_space=pltpu.VMEM)] * (2 * nz + 6),
        out_specs=[pl.BlockSpec(memory_space=pltpu.VMEM)] * 5,
        scratch_shapes=[
            pltpu.VMEM((total, wide), BF),
            pltpu.VMEM((total, D), BF),
            pltpu.VMEM((total, EFF), BF),
            pltpu.VMEM((total, D), BF),
        ],
        cost_estimate=pl.CostEstimate(
            flops=6 * total * D * EFF, bytes_accessed=6 * D * EFF, transcendentals=total * EFF
        ),
        compiler_params=pltpu.CompilerParams(vmem_limit_bytes=32 * MIB),
        name="experts",
    )(*mine, *theirs, gain, gate_up, down, turn, fill, mixed)


def mix_kernel(keep, near, far, *outs):
    cap = outs[0].shape[0]
    for kz, out in enumerate(outs):
        some = slice(kz * cap, (kz + 1) * cap)
        own = keep[some, :].astype(F32) + near[some, :].astype(F32)
        other = far[some, :].astype(F32)
        out[:, :D] = (own[:, :D] + other[:, :D]).astype(BF)
        out[:, D:] = jnp.concatenate([own[:, D:], other[:, D:]], axis=1).astype(BF)


def mix(keep, near, far, nz):
    cap = keep.shape[0] // nz
    cols = keep.shape[1] - D
    return pl.pallas_call(
        mix_kernel,
        out_shape=[jax.ShapeDtypeStruct((cap, D + 2 * cols), BF)] * nz,
        in_specs=[pl.BlockSpec(memory_space=pltpu.VMEM)] * 3,
        out_specs=[pl.BlockSpec(memory_space=pltpu.VMEM)] * nz,
        cost_estimate=pl.CostEstimate(
            flops=3 * keep.size, bytes_accessed=8 * keep.size, transcendentals=0
        ),
        compiler_params=pltpu.CompilerParams(vmem_limit_bytes=16 * MIB),
        name="mix",
    )(keep, near, far)


def finish_kernel(nz, stream, *refs):
    pieces, (attn, out) = refs[:nz], refs[nz:]
    _, _, chip, _ = place()
    cols = (pieces[0].shape[1] - D) // 2
    total = stream[...].astype(F32)
    for kz in range(nz):
        total = total + pieces[kz][:, :D].astype(F32)
    out[...] = total.astype(BF)
    if cols % 128 == 0:
        for kz in range(nz):
            for ky in range(2):
                spot = pl.multiple_of((chip ^ (2 * kz + ky)) * cols, cols)
                attn[:, pl.ds(spot, cols)] = pieces[kz][:, D + ky * cols : D + (ky + 1) * cols]
    else:
        whole = jnp.zeros(attn.shape, F32)
        lane = lax.broadcasted_iota(jnp.int32, (cols, D), 1)
        line = lax.broadcasted_iota(jnp.int32, (cols, D), 0)
        for kz in range(nz):
            for ky in range(2):
                spot = (chip ^ (2 * kz + ky)) * cols
                put = (lane == line + spot).astype(F32).astype(BF)
                part = pieces[kz][:, D + ky * cols : D + (ky + 1) * cols]
                whole = whole + dot(part, put, NN)
        attn[...] = whole.astype(BF)


def finish(stream, pieces):
    shape = jax.ShapeDtypeStruct(stream.shape, BF)
    nz = len(pieces)
    return pl.pallas_call(
        functools.partial(finish_kernel, nz),
        out_shape=[shape, shape],
        in_specs=[pl.BlockSpec(memory_space=pltpu.VMEM)] * (nz + 1),
        out_specs=[pl.BlockSpec(memory_space=pltpu.VMEM)] * 2,
        cost_estimate=pl.CostEstimate(
            flops=nz * stream.size, bytes_accessed=4 * nz * stream.size, transcendentals=0
        ),
        compiler_params=pltpu.CompilerParams(vmem_limit_bytes=16 * MIB),
        name="finish",
    )(stream, *pieces)


def body(
    queries,
    keys,
    values,
    lengths,
    owner_counts,
    row_order,
    residual,
    out_weight,
    norm_gain,
    expert_ids,
    route_weights,
    gate_up,
    expert_down,
):
    width = lax.axis_size("ctx")
    chips, nz = width // 2, width // 4
    per = queries.shape[0]
    cap = residual.shape[0]
    order = row_order.reshape(1, -1)
    same_core = [[2 * i + c for i in range(chips)] for c in range(2)]

    def along_z(terms):
        out = [terms[0]]
        for kz in range(1, nz):
            out.append(hop(terms[kz], 4 * kz, width))
        return out

    def add(*terms):
        return functools.reduce(lambda a, b: a + b, [t.astype(F32) for t in terms]).astype(BF)

    near = hop(queries, 2, width)
    k_oth, v_oth = hop(keys, 1, width), hop(values, 1, width)
    column = jnp.stack([queries, near])
    pieces = along_z([column] * nz)
    k_own, v_own = fetch(keys, values)
    w_oth = hop(out_weight, 1, width)
    res_own, home, fill, turn = prepare(
        owner_counts, order, expert_ids, route_weights, residual, per, width
    )
    res_oth = hop(res_own, 1, width)

    partial = attention(pieces, k_own, v_own, k_oth, v_oth, lengths, chips)
    got = lax.all_to_all(
        partial, "ctx", split_axis=0, concat_axis=0, tiled=True, axis_index_groups=same_core
    )
    w_own, gain = fetch(out_weight, norm_gain.reshape(1, -1))
    *parts, mixed = project(got, w_own, w_oth, res_own, res_oth, home, nz)
    chunk = add(*along_z(parts))
    chunk = add(chunk, hop(chunk, 2, width))
    mine = along_z([chunk] * nz)
    theirs = [hop(x, 1, width) for x in mine]
    up, down = fetch(gate_up, lax.optimization_barrier((expert_down, chunk))[0])
    keep0, keep1, send0, send1, stream = experts(
        mine, theirs, gain, up, down, turn, fill, mixed, width, cap
    )
    far = hop(add(keep1, hop(send1, 1, width)), 2, width)
    sums = mix(keep0, hop(send0, 1, width), far, nz)
    attn, layer_out = finish(stream, along_z(sums))
    return (attn, layer_out)


def solution(mesh):
    placed = (
        P(("groups", "ctx"), None),
        P("groups", "ctx", None),
        P("groups", "ctx", None),
        P("groups"),
        P("groups"),
        P("groups"),
        P(("groups", "ctx"), None),
        P("ctx", None),
        P(),
        P(("groups", "ctx"), None),
        P(("groups", "ctx"), None),
        P("ctx", None, None),
        P("ctx", None, None),
    )

    return jax.shard_map(
        body,
        mesh=mesh,
        in_specs=placed,
        out_specs=(P(("groups", "ctx"), None), P(("groups", "ctx"), None)),
        check_vma=False,
    )
```

```python
import functools

import jax
import jax.numpy as jnp
from jax import lax
from jax.experimental import pallas as pl
from jax.experimental.pallas import tpu as pltpu
from jax.sharding import PartitionSpec as P


D = 2048
HQ = 16
KVH = 2
HD = 128
EFF = 768
TOPK = 8
STRETCH = 128
BF = jnp.bfloat16
F32 = jnp.float32
MIB = 1 << 20
LOG2E = 1.4426950408889634
STAT = 8


NT = (((1,), (1,)), ((), ()))
NN = (((1,), (0,)), ((), ()))


def dot(a, b, dims):
    return lax.dot_general(a, b, dims, preferred_element_type=F32)


def place():
    device = lax.axis_index("ctx")
    return device, device & 1, device >> 1, device >> 2


def hop(x, mask, width):
    return lax.ppermute(x, "ctx", [(i, i ^ mask) for i in range(width)])


def split3(x):
    hi = x.astype(BF)
    rest = x - hi.astype(F32)
    mid = rest.astype(BF)
    return hi, mid, (rest - mid.astype(F32)).astype(BF)


def row_ids(per, core, axis, shape):
    i = lax.broadcasted_iota(jnp.int32, shape, axis)
    return (i // per) * (2 * per) + core * per + i % per


def fetch_kernel(count, *refs):
    sems = refs[2 * count]
    copies = [
        pltpu.make_async_copy(refs[i], refs[count + i], sems.at[i]) for i in range(count)
    ]
    for copy in copies:
        copy.start()
    for copy in copies:
        copy.wait()


def in_hbm(x):
    return pltpu.with_memory_space_constraint(x, pltpu.HBM)


def fetch(*arrays):
    count = len(arrays)
    size = sum(a.size * a.dtype.itemsize for a in arrays)
    return pl.pallas_call(
        functools.partial(fetch_kernel, count),
        out_shape=[pltpu.VMEM(a.shape, a.dtype) for a in arrays],
        in_specs=[pl.BlockSpec(memory_space=pltpu.HBM)] * count,
        out_specs=[pl.BlockSpec(memory_space=pltpu.VMEM)] * count,
        scratch_shapes=[pltpu.SemaphoreType.DMA((count,))],
        cost_estimate=pl.CostEstimate(flops=0, bytes_accessed=2 * size, transcendentals=0),
        compiler_params=pltpu.CompilerParams(vmem_limit_bytes=16 * MIB),
        name="fetch",
    )(*[in_hbm(a) for a in arrays])


def prepare_kernel(per, width, *refs):
    (counts, order, ids, weights, residual, weight_in, gain_in) = refs[:7]
    (res, home, fill, turn, weight_out, gain_out) = refs[7:13]
    picks, table, own, sems = refs[13:]
    copies = [
        pltpu.make_async_copy(weight_in, weight_out, sems.at[0]),
        pltpu.make_async_copy(gain_in, gain_out, sems.at[1]),
    ]
    for copy in copies:
        copy.start()
    device, core, _, _ = place()
    cap, rows = residual.shape[0], order.shape[1]
    half = home.shape[0]
    slots = picks.shape[0]
    lane = lax.broadcasted_iota(jnp.int32, (width, width), 1)
    line = lax.broadcasted_iota(jnp.int32, (width, width), 0)
    many = counts[...].astype(F32)
    end = jnp.sum(jnp.where(lane <= line, many, 0.0), axis=1, keepdims=True)
    size = jnp.sum(jnp.where(lane == line, many, 0.0), axis=1, keepdims=True)
    p = lax.broadcasted_iota(jnp.int32, (width, rows), 1).astype(F32)
    past = (p >= end).astype(F32)
    owner = jnp.sum(past, axis=0, keepdims=True)
    start = jnp.sum(past * size, axis=0, keepdims=True)
    slot = owner * cap + p[:1] - start
    at = lax.broadcasted_iota(jnp.int32, (slots, rows), 0).astype(F32)
    picks[...] = (at == slot).astype(F32).astype(BF)
    seats = [
        (order[...] == row_ids(per, c, 0, (half, rows))).astype(F32).astype(BF)
        for c in range(2)
    ]
    mine = (order[...] == row_ids(per, core, 0, (half, rows))).astype(F32).astype(BF)
    own[...] = dot(picks[...], mine, NT).astype(BF)
    table[...] = dot(picks[...], jnp.concatenate(seats, axis=0), NT).astype(BF)
    for kc in range(2):
        for ky in range(2):
            for kz in range(width // 4):
                there = device ^ (kc + 2 * ky + 4 * kz)
                there = pl.ds(pl.multiple_of(there * cap, cap), cap)
                to = (kc * 2 + ky) * (width // 4) + kz
                turn[to * cap : (to + 1) * cap, :] = table[there, :]
                fill[to * cap : (to + 1) * cap, :] = own[there, :]
    chip_picks = [
        picks[pl.ds(pl.multiple_of(o * cap, cap), cap), :] for o in (device, device ^ 1)
    ]
    home[...] = dot(mine, jnp.concatenate(chip_picks, axis=0), NT).astype(BF)
    lanes = res.shape[1] - D
    kind = lax.broadcasted_iota(jnp.int32, (lanes, cap), 0)
    norm = weights[...] / jnp.sum(weights[...], axis=0, keepdims=True)
    dense = jnp.zeros((lanes, cap), F32)
    for k in range(TOPK):
        dense = dense + jnp.where(ids[k : k + 1, :] == kind % width, norm[k : k + 1, :], 0.0)
    high = dense.astype(BF).astype(F32)
    low = jnp.where(kind < 2 * width, dense - high, 0.0)
    both = jnp.where(kind < width, high, low).astype(BF)
    i = lax.broadcasted_iota(jnp.int32, (cap, cap), 0)
    j = lax.broadcasted_iota(jnp.int32, (cap, cap), 1)
    res[:, :D] = residual[...]
    res[:, D:] = dot((i == j).astype(F32).astype(BF), both, NT).astype(BF)
    for copy in copies:
        copy.wait()


def prepare(counts, order, ids, weights, residual, out_weight, gain, per, width):
    cap, rows = residual.shape[0], order.shape[1]
    half = width // 2 * per
    lanes = -(-2 * width // 128) * 128
    slots = width * cap
    given = (counts, order, ids, weights, residual, out_weight, gain)
    return pl.pallas_call(
        functools.partial(prepare_kernel, per, width),
        out_shape=[
            jax.ShapeDtypeStruct((cap, D + lanes), BF),
            jax.ShapeDtypeStruct((half, 2 * cap), BF),
            jax.ShapeDtypeStruct((slots, half), BF),
            jax.ShapeDtypeStruct((slots, 2 * half), BF),
            pltpu.VMEM(out_weight.shape, out_weight.dtype),
            pltpu.VMEM(gain.shape, gain.dtype),
        ],
        in_specs=[pl.BlockSpec(memory_space=pltpu.VMEM)] * 5
        + [pl.BlockSpec(memory_space=pltpu.HBM)] * 2,
        out_specs=[pl.BlockSpec(memory_space=pltpu.VMEM)] * 6,
        scratch_shapes=[
            pltpu.VMEM((slots, rows), BF),
            pltpu.VMEM((slots, 2 * half), BF),
            pltpu.VMEM((slots, half), BF),
            pltpu.SemaphoreType.DMA((2,)),
        ],
        cost_estimate=pl.CostEstimate(
            flops=6 * slots * rows * half, bytes_accessed=8 * slots * half, transcendentals=0
        ),
        compiler_params=pltpu.CompilerParams(vmem_limit_bytes=12 * MIB),
        name="prepare",
    )(*[in_hbm(a) for a in given])


def total_kernel(*refs):
    terms, out = refs[:-1], refs[-1]
    out[...] = functools.reduce(lambda a, b: a + b, [t[...].astype(F32) for t in terms]).astype(BF)


def pair_kernel(first, second, out):
    out[0] = first[...]
    out[1] = second[...]


def small(kernel, shape, *terms):
    return pl.pallas_call(
        kernel,
        out_shape=jax.ShapeDtypeStruct(shape, BF),
        in_specs=[pl.BlockSpec(memory_space=pltpu.VMEM)] * len(terms),
        out_specs=pl.BlockSpec(memory_space=pltpu.VMEM),
        cost_estimate=pl.CostEstimate(
            flops=len(terms) * terms[0].size,
            bytes_accessed=2 * (len(terms) + 1) * terms[0].size,
            transcendentals=0,
        ),
        compiler_params=pltpu.CompilerParams(vmem_limit_bytes=16 * MIB),
    )(*terms)


def attention_kernel(nz, lengths, *refs):
    pieces, (k_own, v_own, k_oth, v_oth, out, rows) = refs[:nz], refs[nz:]
    device, core, chip, _ = place()
    per = pieces[0].shape[1]
    requests, span = k_own.shape[0], k_own.shape[1]
    count = rows.shape[0]
    seat = count // requests
    chips, depth = out.shape[0], out.shape[1] - STAT
    cols = HQ * HD // chips
    heads = max(1, cols // HD)
    for kz in range(nz):
        both = pieces[kz][...].astype(F32)
        for ky in range(2):
            spot = (chip ^ (2 * kz + ky)) * per
            rows[pl.ds(pl.multiple_of(spot, per), per), :] = both[ky]
    key = lax.broadcasted_iota(jnp.int32, (span, 2 * seat), 0)
    lane = lax.broadcasted_iota(jnp.int32, (1, 2 * seat), 1) % seat
    ahead = (lane // per) * (2 * per) + core * per + lane % per - STRETCH
    first_own, first_oth = device * span, (device ^ 1) * span
    for q in range(requests):
        last = lengths[q] + ahead
        see_own, see_oth = key <= last - first_own, key <= last - first_oth
        for j in range(HQ // 2):
            v = 2 * j // (HQ // KVH)
            kv = slice(v * HD, (v + 1) * HD)
            if 2 * j % (HQ // KVH) == 0:
                vt_own, vt_oth = v_own[q, :, kv].T, v_oth[q, :, kv].T
            pair = jnp.concatenate(
                [
                    rows[q * seat : (q + 1) * seat, (2 * j + e) * HD : (2 * j + e + 1) * HD]
                    for e in range(2)
                ],
                axis=0,
            ).astype(BF)
            s_own = dot(k_own[q, :, kv], pair, NT) * (HD ** (-0.5) * LOG2E)
            s_oth = dot(k_oth[q, :, kv], pair, NT) * (HD ** (-0.5) * LOG2E)
            s_own = jnp.where(see_own, s_own, -1e30)
            s_oth = jnp.where(see_oth, s_oth, -1e30)
            top = jnp.maximum(
                jnp.max(s_own, axis=0, keepdims=True), jnp.max(s_oth, axis=0, keepdims=True)
            )
            top = jnp.maximum(top, -1e29)
            w_own = jnp.exp2(s_own - top)
            w_oth = jnp.exp2(s_oth - top)
            total = jnp.sum(w_own, axis=0, keepdims=True) + jnp.sum(w_oth, axis=0, keepdims=True)
            mixed = dot(vt_own, w_own.astype(BF), NN) + dot(vt_oth, w_oth.astype(BF), NN)
            some = total > 0.0
            safe = jnp.where(some, total, 1.0)
            mixed = (mixed / safe).astype(BF)
            lse = jnp.where(some, top * (1.0 / LOG2E) + jnp.log(safe), -1e30)
            hi, mid, low = split3(lse)
            stat = jnp.concatenate(
                [hi.astype(F32), mid.astype(F32), low.astype(F32)]
                + [jnp.zeros((STAT - 3, 2 * seat), F32)],
                axis=0,
            ).astype(BF)
            if heads == 2 and requests == 1:
                out[j, :depth, :] = mixed
                out[j, depth:, :] = stat
            else:
                for e in range(2):
                    mine = slice(e * seat, (e + 1) * seat)
                    head = 2 * j + e
                    lo = (head % heads) * count + q * seat
                    for part in range(HD // depth):
                        dest = (head * HD + part * depth) // cols
                        out[dest, :depth, lo : lo + seat] = mixed[
                            part * depth : (part + 1) * depth, mine
                        ]
                        out[dest, depth:, lo : lo + seat] = stat[:, mine]


def attention(pieces, k_own, v_own, k_oth, v_oth, lengths, chips):
    nz = len(pieces)
    per = pieces[0].shape[1]
    count = chips * per
    cols = HQ * HD // chips
    heads = max(1, cols // HD)
    shape = (chips, min(cols, HD) + STAT, heads * count)
    work = 4 * k_own.size * (HQ // KVH) * 2 * count
    return pl.pallas_call(
        functools.partial(attention_kernel, nz),
        out_shape=jax.ShapeDtypeStruct(shape, BF),
        in_specs=[pl.BlockSpec(memory_space=pltpu.SMEM)]
        + [pl.BlockSpec(memory_space=pltpu.VMEM)] * (nz + 4),
        out_specs=pl.BlockSpec(memory_space=pltpu.VMEM),
        scratch_shapes=[pltpu.VMEM((count, HQ * HD), F32)],
        cost_estimate=pl.CostEstimate(
            flops=work, bytes_accessed=8 * k_own.size, transcendentals=work // (4 * HD)
        ),
        compiler_params=pltpu.CompilerParams(vmem_limit_bytes=16 * MIB),
        name="attention",
    )(lengths, *pieces, k_own, v_own, k_oth, v_oth)


def project_kernel(nz, got, w_own, w_oth, res_own, res_oth, home, *refs):
    outs, attn, part = refs[:nz], refs[nz], refs[nz + 1]
    _, core, _, z = place()
    chips, depth = got.shape[0], got.shape[1] - STAT
    count = part.shape[0]
    heads = got.shape[2] // count
    lse = [
        jnp.sum(got[i, depth:, :].astype(F32), axis=0, keepdims=True) for i in range(chips)
    ]
    best = functools.reduce(jnp.maximum, lse)
    factor = [jnp.exp(x - best) for x in lse]
    denom = functools.reduce(lambda a, b: a + b, factor)
    merged = functools.reduce(
        lambda a, b: a + b, [got[i, :depth, :].astype(F32) * factor[i] for i in range(chips)]
    )
    merged = (merged / denom).T.astype(BF)
    if heads == 2:
        first, second = merged[:count], merged[count:]
        attn[...] = jnp.concatenate([first, second], axis=1)
    else:
        first, second = merged[:, : depth // 2], merged[:, depth // 2 :]
        attn[...] = merged
    low = (core == 0).astype(F32)
    first, second = first.astype(F32), second.astype(F32)
    own = (first * low + second * (1.0 - low)).astype(BF)
    oth = (second * low + first * (1.0 - low)).astype(BF)
    res = jnp.concatenate([res_own[...], res_oth[...]], axis=0)
    part[:, :D] = (
        dot(home[...], res[:, :D], NN) + dot(own, w_own[...], NN) + dot(oth, w_oth[...], NN)
    )
    part[:, D:] = dot(home[...], res[:, D:], NN)
    block = outs[0].shape[0]
    for kz in range(nz):
        spot = pl.multiple_of((z ^ kz) * block, block)
        outs[kz][...] = part[pl.ds(spot, block), :].astype(BF)


def project(got, w_own, w_oth, res_own, res_oth, home, nz):
    chips = got.shape[0]
    count = home.shape[0]
    cols = D // chips
    wide = res_own.shape[1]
    return pl.pallas_call(
        functools.partial(project_kernel, nz),
        out_shape=[jax.ShapeDtypeStruct((count // nz, wide), BF)] * nz
        + [jax.ShapeDtypeStruct((count, cols), BF)],
        in_specs=[pl.BlockSpec(memory_space=pltpu.VMEM)] * 6,
        out_specs=[pl.BlockSpec(memory_space=pltpu.VMEM)] * (nz + 1),
        scratch_shapes=[pltpu.VMEM((count, wide), F32)],
        cost_estimate=pl.CostEstimate(
            flops=2 * count * cols * D, bytes_accessed=4 * cols * D, transcendentals=0
        ),
        compiler_params=pltpu.CompilerParams(vmem_limit_bytes=12 * MIB),
        name="project",
    )(got, w_own, w_oth, res_own, res_oth, home)


def expert_kernel(nz, width, *refs):
    mine, theirs = refs[:nz], refs[nz : 2 * nz]
    (gain, gate_up, down, turn, fill, mixed, keep0, keep1, send0, send1, stream_own) = refs[
        2 * nz : 2 * nz + 11
    ]
    x, normed, hidden, scaled = refs[2 * nz + 11 :]
    device, core, _, z = place()
    block = mine[0].shape[0]
    half = block * nz
    cap = stream_own.shape[0]
    for kz in range(nz):
        spot = (z ^ kz) * block
        x[pl.ds(pl.multiple_of(core * half + spot, block), block), :] = mine[kz][...]
        x[pl.ds(pl.multiple_of((1 - core) * half + spot, block), block), :] = theirs[kz][...]
    stream = x[:, :D].astype(F32)
    scale = lax.rsqrt(jnp.mean(stream * stream, axis=-1, keepdims=True) + 1e-06)
    normed[...] = (stream * scale * gain[...]).astype(BF)
    extra = x[:, D:].astype(F32)
    lane = lax.broadcasted_iota(jnp.int32, extra.shape, 1)
    pick = (lane == device) | (lane == device + width)
    weight = jnp.sum(jnp.where(pick, extra, 0.0), axis=-1, keepdims=True)
    tile = 256
    for lo in range(0, EFF, tile):
        g = dot(normed[...], gate_up[0, :, lo : lo + tile], NN)
        u = dot(normed[...], gate_up[0, :, EFF + lo : EFF + lo + tile], NN)
        hidden[:, lo : lo + tile] = (g / (1.0 + jnp.exp(-g)) * u).astype(BF)
    for lo in range(0, D, tile):
        y = dot(hidden[...], down[0, :, lo : lo + tile], NN).astype(BF)
        scaled[:, lo : lo + tile] = (y.astype(F32) * weight).astype(BF)
    for k, target in enumerate((keep0, keep1, send0, send1)):
        size = target.shape[0]
        some = slice(k * size, (k + 1) * size)
        target[:, :D] = dot(turn[some, :], scaled[...], NN).astype(BF)
        target[:, D:] = dot(fill[some, :], mixed[...], NN).astype(BF)
    stream_own[...] = dot(turn[:cap, :], x[:, :D], NN).astype(BF)


def experts(mine, theirs, gain, gate_up, down, turn, fill, mixed, width, cap):
    nz = len(mine)
    block, wide = mine[0].shape
    total = 2 * nz * block
    wide_out = jax.ShapeDtypeStruct((nz * cap, D + mixed.shape[1]), BF)
    return pl.pallas_call(
        functools.partial(expert_kernel, nz, width),
        out_shape=[wide_out] * 4 + [jax.ShapeDtypeStruct((cap, D), BF)],
        in_specs=[pl.BlockSpec(memory_space=pltpu.VMEM)] * (2 * nz + 6),
        out_specs=[pl.BlockSpec(memory_space=pltpu.VMEM)] * 5,
        scratch_shapes=[
            pltpu.VMEM((total, wide), BF),
            pltpu.VMEM((total, D), BF),
            pltpu.VMEM((total, EFF), BF),
            pltpu.VMEM((total, D), BF),
        ],
        cost_estimate=pl.CostEstimate(
            flops=6 * total * D * EFF, bytes_accessed=6 * D * EFF, transcendentals=total * EFF
        ),
        compiler_params=pltpu.CompilerParams(vmem_limit_bytes=32 * MIB),
        name="experts",
    )(*mine, *theirs, gain, gate_up, down, turn, fill, mixed)


def mix_kernel(keep, near, far, *outs):
    cap = outs[0].shape[0]
    for kz, out in enumerate(outs):
        some = slice(kz * cap, (kz + 1) * cap)
        own = keep[some, :].astype(F32) + near[some, :].astype(F32)
        other = far[some, :].astype(F32)
        out[:, :D] = (own[:, :D] + other[:, :D]).astype(BF)
        out[:, D:] = jnp.concatenate([own[:, D:], other[:, D:]], axis=1).astype(BF)


def mix(keep, near, far, nz):
    cap = keep.shape[0] // nz
    cols = keep.shape[1] - D
    return pl.pallas_call(
        mix_kernel,
        out_shape=[jax.ShapeDtypeStruct((cap, D + 2 * cols), BF)] * nz,
        in_specs=[pl.BlockSpec(memory_space=pltpu.VMEM)] * 3,
        out_specs=[pl.BlockSpec(memory_space=pltpu.VMEM)] * nz,
        cost_estimate=pl.CostEstimate(
            flops=3 * keep.size, bytes_accessed=8 * keep.size, transcendentals=0
        ),
        compiler_params=pltpu.CompilerParams(vmem_limit_bytes=16 * MIB),
        name="mix",
    )(keep, near, far)


def finish_kernel(nz, stream, *refs):
    pieces, (attn, out) = refs[:nz], refs[nz:]
    _, _, chip, _ = place()
    cols = (pieces[0].shape[1] - D) // 2
    total = stream[...].astype(F32)
    for kz in range(nz):
        total = total + pieces[kz][:, :D].astype(F32)
    out[...] = total.astype(BF)
    if cols % 128 == 0:
        for kz in range(nz):
            for ky in range(2):
                spot = pl.multiple_of((chip ^ (2 * kz + ky)) * cols, cols)
                attn[:, pl.ds(spot, cols)] = pieces[kz][:, D + ky * cols : D + (ky + 1) * cols]
    else:
        whole = jnp.zeros(attn.shape, F32)
        lane = lax.broadcasted_iota(jnp.int32, (cols, D), 1)
        line = lax.broadcasted_iota(jnp.int32, (cols, D), 0)
        for kz in range(nz):
            for ky in range(2):
                spot = (chip ^ (2 * kz + ky)) * cols
                put = (lane == line + spot).astype(F32).astype(BF)
                part = pieces[kz][:, D + ky * cols : D + (ky + 1) * cols]
                whole = whole + dot(part, put, NN)
        attn[...] = whole.astype(BF)


def finish(stream, pieces):
    shape = jax.ShapeDtypeStruct(stream.shape, BF)
    nz = len(pieces)
    return pl.pallas_call(
        functools.partial(finish_kernel, nz),
        out_shape=[shape, shape],
        in_specs=[pl.BlockSpec(memory_space=pltpu.VMEM)] * (nz + 1),
        out_specs=[pl.BlockSpec(memory_space=pltpu.VMEM)] * 2,
        cost_estimate=pl.CostEstimate(
            flops=nz * stream.size, bytes_accessed=4 * nz * stream.size, transcendentals=0
        ),
        compiler_params=pltpu.CompilerParams(vmem_limit_bytes=16 * MIB),
        name="finish",
    )(stream, *pieces)


def body(
    queries,
    keys,
    values,
    lengths,
    owner_counts,
    row_order,
    residual,
    out_weight,
    norm_gain,
    expert_ids,
    route_weights,
    gate_up,
    expert_down,
):
    width = lax.axis_size("ctx")
    chips, nz = width // 2, width // 4
    per = queries.shape[0]
    cap = residual.shape[0]
    order = row_order.reshape(1, -1)
    same_core = [[2 * i + c for i in range(chips)] for c in range(2)]

    def along_z(terms):
        out = [terms[0]]
        for kz in range(1, nz):
            out.append(hop(terms[kz], 4 * kz, width))
        return out

    def add(*terms):
        return small(total_kernel, terms[0].shape, *terms)

    near = hop(queries, 2, width)
    k_oth = hop(keys, 1, width)
    v_oth = hop(values, 1, width)
    q_own, k_own, v_own = fetch(queries, keys, values)
    column = small(pair_kernel, (2,) + queries.shape, q_own, near)
    pieces = along_z([column] * nz)
    w_oth = hop(out_weight, 1, width)
    res_own, home, fill, turn, w_own, gain = prepare(
        owner_counts.reshape(1, -1),
        order,
        expert_ids.T,
        route_weights.T,
        residual,
        out_weight,
        norm_gain.reshape(1, -1),
        per,
        width,
    )
    res_oth = hop(res_own, 1, width)

    partial = attention(pieces, k_own, v_own, k_oth, v_oth, lengths, chips)
    got = lax.all_to_all(
        partial, "ctx", split_axis=0, concat_axis=0, tiled=True, axis_index_groups=same_core
    )
    *parts, mixed = project(got, w_own, w_oth, res_own, res_oth, home, nz)
    chunk = add(*along_z(parts))
    (up,) = fetch(gate_up)
    other = hop(chunk, 2, width)
    chunk = add(chunk, other)
    mine = along_z([chunk] * nz)
    theirs = [hop(x, 1, width) for x in mine]
    (down,) = fetch(expert_down)
    keep0, keep1, send0, send1, stream = experts(
        mine, theirs, gain, up, down, turn, fill, mixed, width, cap
    )
    far = hop(add(keep1, hop(send1, 1, width)), 2, width)
    sums = mix(keep0, hop(send0, 1, width), far, nz)
    attn, layer_out = finish(stream, along_z(sums))
    return (attn, layer_out)


def solution(mesh):
    placed = (
        P(("groups", "ctx"), None),
        P("groups", "ctx", None),
        P("groups", "ctx", None),
        P("groups"),
        P("groups"),
        P("groups"),
        P(("groups", "ctx"), None),
        P("ctx", None),
        P(),
        P(("groups", "ctx"), None),
        P(("groups", "ctx"), None),
        P("ctx", None, None),
        P("ctx", None, None),
    )

    return jax.shard_map(
        body,
        mesh=mesh,
        in_specs=placed,
        out_specs=(P(("groups", "ctx"), None), P(("groups", "ctx"), None)),
        check_vma=False,
    )
```

```python
import functools

import jax
import jax.numpy as jnp
from jax import lax
from jax.experimental import pallas as pl
from jax.experimental.pallas import tpu as pltpu
from jax.sharding import PartitionSpec as P


D = 2048
HQ = 16
KVH = 2
HD = 128
EFF = 768
TOPK = 8
STRETCH = 128
BF = jnp.bfloat16
F32 = jnp.float32
MIB = 1 << 20
LOG2E = 1.4426950408889634
STAT = 8


NT = (((1,), (1,)), ((), ()))
NN = (((1,), (0,)), ((), ()))


def dot(a, b, dims):
    return lax.dot_general(a, b, dims, preferred_element_type=F32)


def place():
    device = lax.axis_index("ctx")
    return device, device & 1, device >> 1, device >> 2


def hop(x, mask, width):
    return lax.ppermute(x, "ctx", [(i, i ^ mask) for i in range(width)])


def split3(x):
    hi = x.astype(BF)
    rest = x - hi.astype(F32)
    mid = rest.astype(BF)
    return hi, mid, (rest - mid.astype(F32)).astype(BF)


def row_ids(per, core, axis, shape):
    i = lax.broadcasted_iota(jnp.int32, shape, axis)
    return (i // per) * (2 * per) + core * per + i % per


def fetch_kernel(count, *refs):
    sems = refs[2 * count]
    copies = [
        pltpu.make_async_copy(refs[i], refs[count + i], sems.at[i]) for i in range(count)
    ]
    for copy in copies:
        copy.start()
    for copy in copies:
        copy.wait()


def in_hbm(x):
    return pltpu.with_memory_space_constraint(x, pltpu.HBM)


def fetch(*arrays):
    count = len(arrays)
    size = sum(a.size * a.dtype.itemsize for a in arrays)
    return pl.pallas_call(
        functools.partial(fetch_kernel, count),
        out_shape=[pltpu.VMEM(a.shape, a.dtype) for a in arrays],
        in_specs=[pl.BlockSpec(memory_space=pltpu.HBM)] * count,
        out_specs=[pl.BlockSpec(memory_space=pltpu.VMEM)] * count,
        scratch_shapes=[pltpu.SemaphoreType.DMA((count,))],
        cost_estimate=pl.CostEstimate(flops=0, bytes_accessed=2 * size, transcendentals=0),
        compiler_params=pltpu.CompilerParams(vmem_limit_bytes=16 * MIB),
        name="fetch",
    )(*[in_hbm(a) for a in arrays])


def prepare_kernel(per, width, *refs):
    (counts, order, ids, weights, residual, weight_in, gain_in) = refs[:7]
    (res, home, fill, turn, weight_out, gain_out) = refs[7:13]
    picks, table, own, sems = refs[13:]
    copies = [
        pltpu.make_async_copy(weight_in, weight_out, sems.at[0]),
        pltpu.make_async_copy(gain_in, gain_out, sems.at[1]),
    ]
    for copy in copies:
        copy.start()
    device, core, _, _ = place()
    cap, rows = residual.shape[0], order.shape[1]
    half = home.shape[0]
    slots = picks.shape[0]
    lane = lax.broadcasted_iota(jnp.int32, (width, width), 1)
    line = lax.broadcasted_iota(jnp.int32, (width, width), 0)
    many = counts[...].astype(F32)
    end = jnp.sum(jnp.where(lane <= line, many, 0.0), axis=1, keepdims=True)
    size = jnp.sum(jnp.where(lane == line, many, 0.0), axis=1, keepdims=True)
    p = lax.broadcasted_iota(jnp.int32, (width, rows), 1).astype(F32)
    past = (p >= end).astype(F32)
    owner = jnp.sum(past, axis=0, keepdims=True)
    start = jnp.sum(past * size, axis=0, keepdims=True)
    slot = owner * cap + p[:1] - start
    at = lax.broadcasted_iota(jnp.int32, (slots, rows), 0).astype(F32)
    picks[...] = (at == slot).astype(F32).astype(BF)
    seats = [
        (order[...] == row_ids(per, c, 0, (half, rows))).astype(F32).astype(BF)
        for c in range(2)
    ]
    mine = (order[...] == row_ids(per, core, 0, (half, rows))).astype(F32).astype(BF)
    own[...] = dot(picks[...], mine, NT).astype(BF)
    table[...] = dot(picks[...], jnp.concatenate(seats, axis=0), NT).astype(BF)
    for kc in range(2):
        for ky in range(2):
            for kz in range(width // 4):
                there = device ^ (kc + 2 * ky + 4 * kz)
                there = pl.ds(pl.multiple_of(there * cap, cap), cap)
                to = (kc * 2 + ky) * (width // 4) + kz
                turn[to * cap : (to + 1) * cap, :] = table[there, :]
                fill[to * cap : (to + 1) * cap, :] = own[there, :]
    chip_picks = [
        picks[pl.ds(pl.multiple_of(o * cap, cap), cap), :] for o in (device, device ^ 1)
    ]
    home[...] = dot(mine, jnp.concatenate(chip_picks, axis=0), NT).astype(BF)
    lanes = res.shape[1] - D
    kind = lax.broadcasted_iota(jnp.int32, (lanes, cap), 0)
    norm = weights[...] / jnp.sum(weights[...], axis=0, keepdims=True)
    dense = jnp.zeros((lanes, cap), F32)
    for k in range(TOPK):
        dense = dense + jnp.where(ids[k : k + 1, :] == kind % width, norm[k : k + 1, :], 0.0)
    high = dense.astype(BF).astype(F32)
    low = jnp.where(kind < 2 * width, dense - high, 0.0)
    both = jnp.where(kind < width, high, low).astype(BF)
    i = lax.broadcasted_iota(jnp.int32, (cap, cap), 0)
    j = lax.broadcasted_iota(jnp.int32, (cap, cap), 1)
    res[:, :D] = residual[...]
    res[:, D:] = dot((i == j).astype(F32).astype(BF), both, NT).astype(BF)
    for copy in copies:
        copy.wait()


def prepare(counts, order, ids, weights, residual, out_weight, gain, per, width):
    cap, rows = residual.shape[0], order.shape[1]
    half = width // 2 * per
    lanes = -(-2 * width // 128) * 128
    slots = width * cap
    given = (counts, order, ids, weights, residual, out_weight, gain)
    return pl.pallas_call(
        functools.partial(prepare_kernel, per, width),
        out_shape=[
            jax.ShapeDtypeStruct((cap, D + lanes), BF),
            jax.ShapeDtypeStruct((half, 2 * cap), BF),
            jax.ShapeDtypeStruct((slots, half), BF),
            jax.ShapeDtypeStruct((slots, 2 * half), BF),
            pltpu.VMEM(out_weight.shape, out_weight.dtype),
            pltpu.VMEM(gain.shape, gain.dtype),
        ],
        in_specs=[pl.BlockSpec(memory_space=pltpu.VMEM)] * 5
        + [pl.BlockSpec(memory_space=pltpu.HBM)] * 2,
        out_specs=[pl.BlockSpec(memory_space=pltpu.VMEM)] * 6,
        scratch_shapes=[
            pltpu.VMEM((slots, rows), BF),
            pltpu.VMEM((slots, 2 * half), BF),
            pltpu.VMEM((slots, half), BF),
            pltpu.SemaphoreType.DMA((2,)),
        ],
        cost_estimate=pl.CostEstimate(
            flops=6 * slots * rows * half, bytes_accessed=8 * slots * half, transcendentals=0
        ),
        compiler_params=pltpu.CompilerParams(vmem_limit_bytes=12 * MIB),
        name="prepare",
    )(*[in_hbm(a) for a in given])


def total_kernel(*refs):
    terms, out = refs[:-1], refs[-1]
    out[...] = functools.reduce(lambda a, b: a + b, [t[...].astype(F32) for t in terms]).astype(BF)


def pair_kernel(first, second, out):
    out[0] = first[...]
    out[1] = second[...]


def small(kernel, shape, *terms):
    return pl.pallas_call(
        kernel,
        out_shape=jax.ShapeDtypeStruct(shape, BF),
        in_specs=[pl.BlockSpec(memory_space=pltpu.VMEM)] * len(terms),
        out_specs=pl.BlockSpec(memory_space=pltpu.VMEM),
        cost_estimate=pl.CostEstimate(
            flops=len(terms) * terms[0].size,
            bytes_accessed=2 * (len(terms) + 1) * terms[0].size,
            transcendentals=0,
        ),
        compiler_params=pltpu.CompilerParams(vmem_limit_bytes=16 * MIB),
    )(*terms)


def attention_kernel(nz, lengths, *refs):
    pieces, (k_own, v_own, k_oth, v_oth) = refs[:nz], refs[nz : nz + 4]
    outs, (rows, ready) = refs[nz + 4 : 2 * nz + 4], refs[2 * nz + 4 :]
    device, core, chip, _ = place()
    per = pieces[0].shape[1]
    requests, span = k_own.shape[0], k_own.shape[1]
    count = rows.shape[0]
    seat = count // requests
    chips, depth = ready.shape[0], ready.shape[1] - STAT
    cols = HQ * HD // chips
    heads = max(1, cols // HD)
    group = HQ // KVH
    for kz in range(nz):
        both = pieces[kz][...].astype(F32)
        for ky in range(2):
            spot = (chip ^ (2 * kz + ky)) * per
            rows[pl.ds(pl.multiple_of(spot, per), per), :] = both[ky]
    wide = group * seat
    key = lax.broadcasted_iota(jnp.int32, (span, wide), 0)
    lane = lax.broadcasted_iota(jnp.int32, (1, wide), 1) % seat
    ahead = (lane // per) * (2 * per) + core * per + lane % per - STRETCH
    first_own, first_oth = device * span, (device ^ 1) * span
    for q in range(requests):
        last = lengths[q] + ahead
        see_own, see_oth = key <= last - first_own, key <= last - first_oth
        for v in range(KVH):
            kv = slice(v * HD, (v + 1) * HD)
            asked = jnp.concatenate(
                [
                    rows[q * seat : (q + 1) * seat, h * HD : (h + 1) * HD]
                    for h in range(v * group, (v + 1) * group)
                ],
                axis=0,
            ).astype(BF)
            s_own = dot(k_own[q, :, kv], asked, NT) * (HD ** (-0.5) * LOG2E)
            s_oth = dot(k_oth[q, :, kv], asked, NT) * (HD ** (-0.5) * LOG2E)
            s_own = jnp.where(see_own, s_own, -1e30)
            s_oth = jnp.where(see_oth, s_oth, -1e30)
            top = jnp.maximum(
                jnp.max(s_own, axis=0, keepdims=True), jnp.max(s_oth, axis=0, keepdims=True)
            )
            top = jnp.maximum(top, -1e29)
            w_own = jnp.exp2(s_own - top)
            w_oth = jnp.exp2(s_oth - top)
            total = jnp.sum(w_own, axis=0, keepdims=True) + jnp.sum(w_oth, axis=0, keepdims=True)
            mixed = dot(v_own[q, :, kv].T, w_own.astype(BF), NN) + dot(
                v_oth[q, :, kv].T, w_oth.astype(BF), NN
            )
            some = total > 0.0
            safe = jnp.where(some, total, 1.0)
            mixed = (mixed * (1.0 / safe)).astype(BF)
            lse = jnp.where(some, top * (1.0 / LOG2E) + jnp.log(safe), -1e30)
            stat = with_lse(lse)
            if heads == 2 and requests == 1:
                for g in range(group // 2):
                    dest = (v * group // 2 + g) ^ chip
                    mine = slice(2 * g * seat, 2 * (g + 1) * seat)
                    ready[dest, :depth, :] = mixed[:, mine]
                    ready[dest, depth:, :] = stat[:, mine]
            else:
                for e in range(group):
                    mine = slice(e * seat, (e + 1) * seat)
                    head = v * group + e
                    lo = (head % heads) * count + q * seat
                    for part in range(HD // depth):
                        dest = ((head * HD + part * depth) // cols) ^ chip
                        some_rows = slice(part * depth, (part + 1) * depth)
                        ready[dest, :depth, lo : lo + seat] = mixed[some_rows, mine]
                        ready[dest, depth:, lo : lo + seat] = stat[:, mine]
    for kz in range(nz):
        outs[kz][...] = ready[2 * kz : 2 * kz + 2]


def with_lse(lse):
    parts = [x.astype(F32) for x in split3(lse)]
    return jnp.concatenate(parts + [jnp.zeros((STAT - 3, lse.shape[1]), F32)], axis=0).astype(BF)


def attention(pieces, k_own, v_own, k_oth, v_oth, lengths, chips):
    nz = len(pieces)
    per = pieces[0].shape[1]
    count = chips * per
    cols = HQ * HD // chips
    heads = max(1, cols // HD)
    shape = (2, min(cols, HD) + STAT, heads * count)
    work = 4 * k_own.size * (HQ // KVH) * 2 * count
    return pl.pallas_call(
        functools.partial(attention_kernel, nz),
        out_shape=[jax.ShapeDtypeStruct(shape, BF)] * nz,
        in_specs=[pl.BlockSpec(memory_space=pltpu.SMEM)]
        + [pl.BlockSpec(memory_space=pltpu.VMEM)] * (nz + 4),
        out_specs=[pl.BlockSpec(memory_space=pltpu.VMEM)] * nz,
        scratch_shapes=[
            pltpu.VMEM((count, HQ * HD), F32),
            pltpu.VMEM((chips,) + shape[1:], BF),
        ],
        cost_estimate=pl.CostEstimate(
            flops=work, bytes_accessed=8 * k_own.size, transcendentals=work // (4 * HD)
        ),
        compiler_params=pltpu.CompilerParams(vmem_limit_bytes=24 * MIB),
        name="attention",
    )(lengths, *pieces, k_own, v_own, k_oth, v_oth)


def merged(blocks):
    depth = blocks[0].shape[0] - STAT
    lse = [jnp.sum(x[depth:].astype(F32), axis=0, keepdims=True) for x in blocks]
    best = functools.reduce(jnp.maximum, lse)
    factor = [jnp.exp(x - best) for x in lse]
    denom = functools.reduce(lambda a, b: a + b, factor)
    mixed = functools.reduce(
        lambda a, b: a + b, [x[:depth].astype(F32) * f for x, f in zip(blocks, factor)]
    )
    return mixed * (1.0 / denom), best + jnp.log(denom)


def fold_kernel(nz, *refs):
    pieces, outs = refs[:nz], refs[nz:]
    depth = outs[0].shape[0] - STAT
    for ky, out in enumerate(outs):
        mixed, lse = merged([p[ky] for p in pieces])
        out[:depth, :] = mixed.astype(BF)
        out[depth:, :] = with_lse(lse)


def fold(pieces):
    nz = len(pieces)
    shape = pieces[0].shape[1:]
    return pl.pallas_call(
        functools.partial(fold_kernel, nz),
        out_shape=[jax.ShapeDtypeStruct(shape, BF)] * 2,
        in_specs=[pl.BlockSpec(memory_space=pltpu.VMEM)] * nz,
        out_specs=[pl.BlockSpec(memory_space=pltpu.VMEM)] * 2,
        cost_estimate=pl.CostEstimate(
            flops=4 * nz * pieces[0].size, bytes_accessed=4 * nz * pieces[0].size, transcendentals=0
        ),
        compiler_params=pltpu.CompilerParams(vmem_limit_bytes=16 * MIB),
        name="fold",
    )(*pieces)


def project_kernel(nz, near, far, w_own, w_oth, res_own, res_oth, home, *refs):
    outs, attn, part = refs[:nz], refs[nz], refs[nz + 1]
    _, core, _, z = place()
    depth = near.shape[0] - STAT
    count = part.shape[0]
    heads = near.shape[1] // count
    mixed, _ = merged([near[...], far[...]])
    mixed = mixed.T.astype(BF)
    if heads == 2:
        first, second = mixed[:count], mixed[count:]
        attn[...] = jnp.concatenate([first, second], axis=1)
    else:
        first, second = mixed[:, : depth // 2], mixed[:, depth // 2 :]
        attn[...] = mixed
    low = (core == 0).astype(F32)
    first, second = first.astype(F32), second.astype(F32)
    own = (first * low + second * (1.0 - low)).astype(BF)
    oth = (second * low + first * (1.0 - low)).astype(BF)
    res = jnp.concatenate([res_own[...], res_oth[...]], axis=0)
    part[:, :D] = (
        dot(home[...], res[:, :D], NN) + dot(own, w_own[...], NN) + dot(oth, w_oth[...], NN)
    )
    part[:, D:] = dot(home[...], res[:, D:], NN)
    block = outs[0].shape[0]
    for kz in range(nz):
        spot = pl.multiple_of((z ^ kz) * block, block)
        outs[kz][...] = part[pl.ds(spot, block), :].astype(BF)


def project(near, far, w_own, w_oth, res_own, res_oth, home, nz):
    count = home.shape[0]
    cols = D // (2 * nz)
    wide = res_own.shape[1]
    return pl.pallas_call(
        functools.partial(project_kernel, nz),
        out_shape=[jax.ShapeDtypeStruct((count // nz, wide), BF)] * nz
        + [jax.ShapeDtypeStruct((count, cols), BF)],
        in_specs=[pl.BlockSpec(memory_space=pltpu.VMEM)] * 7,
        out_specs=[pl.BlockSpec(memory_space=pltpu.VMEM)] * (nz + 1),
        scratch_shapes=[pltpu.VMEM((count, wide), F32)],
        cost_estimate=pl.CostEstimate(
            flops=2 * count * cols * D, bytes_accessed=4 * cols * D, transcendentals=0
        ),
        compiler_params=pltpu.CompilerParams(vmem_limit_bytes=12 * MIB),
        name="project",
    )(near, far, w_own, w_oth, res_own, res_oth, home)


def expert_kernel(nz, width, *refs):
    mine, theirs = refs[:nz], refs[nz : 2 * nz]
    (gain, gate_up, down, turn, fill, mixed, keep0, keep1, send0, send1, stream_own) = refs[
        2 * nz : 2 * nz + 11
    ]
    x, normed, hidden, scaled = refs[2 * nz + 11 :]
    device, core, _, z = place()
    block = mine[0].shape[0]
    half = block * nz
    cap = stream_own.shape[0]
    for kz in range(nz):
        spot = (z ^ kz) * block
        x[pl.ds(pl.multiple_of(core * half + spot, block), block), :] = mine[kz][...]
        x[pl.ds(pl.multiple_of((1 - core) * half + spot, block), block), :] = theirs[kz][...]
    stream = x[:, :D].astype(F32)
    scale = lax.rsqrt(jnp.mean(stream * stream, axis=-1, keepdims=True) + 1e-06)
    normed[...] = (stream * scale * gain[...]).astype(BF)
    extra = x[:, D:].astype(F32)
    lane = lax.broadcasted_iota(jnp.int32, extra.shape, 1)
    pick = (lane == device) | (lane == device + width)
    weight = jnp.sum(jnp.where(pick, extra, 0.0), axis=-1, keepdims=True)
    tile = 256
    for lo in range(0, EFF, tile):
        g = dot(normed[...], gate_up[0, :, lo : lo + tile], NN)
        u = dot(normed[...], gate_up[0, :, EFF + lo : EFF + lo + tile], NN)
        hidden[:, lo : lo + tile] = (g / (1.0 + jnp.exp(-g)) * u).astype(BF)
    for lo in range(0, D, tile):
        y = dot(hidden[...], down[0, :, lo : lo + tile], NN).astype(BF)
        scaled[:, lo : lo + tile] = (y.astype(F32) * weight).astype(BF)
    for k, target in enumerate((keep0, keep1, send0, send1)):
        size = target.shape[0]
        some = slice(k * size, (k + 1) * size)
        target[:, :D] = dot(turn[some, :], scaled[...], NN).astype(BF)
        target[:, D:] = dot(fill[some, :], mixed[...], NN).astype(BF)
    stream_own[...] = dot(turn[:cap, :], x[:, :D], NN).astype(BF)


def experts(mine, theirs, gain, gate_up, down, turn, fill, mixed, width, cap):
    nz = len(mine)
    block, wide = mine[0].shape
    total = 2 * nz * block
    wide_out = jax.ShapeDtypeStruct((nz * cap, D + mixed.shape[1]), BF)
    return pl.pallas_call(
        functools.partial(expert_kernel, nz, width),
        out_shape=[wide_out] * 4 + [jax.ShapeDtypeStruct((cap, D), BF)],
        in_specs=[pl.BlockSpec(memory_space=pltpu.VMEM)] * (2 * nz + 6),
        out_specs=[pl.BlockSpec(memory_space=pltpu.VMEM)] * 5,
        scratch_shapes=[
            pltpu.VMEM((total, wide), BF),
            pltpu.VMEM((total, D), BF),
            pltpu.VMEM((total, EFF), BF),
            pltpu.VMEM((total, D), BF),
        ],
        cost_estimate=pl.CostEstimate(
            flops=6 * total * D * EFF, bytes_accessed=6 * D * EFF, transcendentals=total * EFF
        ),
        compiler_params=pltpu.CompilerParams(vmem_limit_bytes=32 * MIB),
        name="experts",
    )(*mine, *theirs, gain, gate_up, down, turn, fill, mixed)


def mix_kernel(keep, near, far, *outs):
    cap = outs[0].shape[0]
    for kz, out in enumerate(outs):
        some = slice(kz * cap, (kz + 1) * cap)
        own = keep[some, :].astype(F32) + near[some, :].astype(F32)
        other = far[some, :].astype(F32)
        out[:, :D] = (own[:, :D] + other[:, :D]).astype(BF)
        out[:, D:] = jnp.concatenate([own[:, D:], other[:, D:]], axis=1).astype(BF)


def mix(keep, near, far, nz):
    cap = keep.shape[0] // nz
    cols = keep.shape[1] - D
    return pl.pallas_call(
        mix_kernel,
        out_shape=[jax.ShapeDtypeStruct((cap, D + 2 * cols), BF)] * nz,
        in_specs=[pl.BlockSpec(memory_space=pltpu.VMEM)] * 3,
        out_specs=[pl.BlockSpec(memory_space=pltpu.VMEM)] * nz,
        cost_estimate=pl.CostEstimate(
            flops=3 * keep.size, bytes_accessed=8 * keep.size, transcendentals=0
        ),
        compiler_params=pltpu.CompilerParams(vmem_limit_bytes=16 * MIB),
        name="mix",
    )(keep, near, far)


def finish_kernel(nz, stream, *refs):
    pieces, (attn, out) = refs[:nz], refs[nz:]
    _, _, chip, _ = place()
    cols = (pieces[0].shape[1] - D) // 2
    total = stream[...].astype(F32)
    for kz in range(nz):
        total = total + pieces[kz][:, :D].astype(F32)
    out[...] = total.astype(BF)
    if cols % 128 == 0:
        for kz in range(nz):
            for ky in range(2):
                spot = pl.multiple_of((chip ^ (2 * kz + ky)) * cols, cols)
                attn[:, pl.ds(spot, cols)] = pieces[kz][:, D + ky * cols : D + (ky + 1) * cols]
    else:
        whole = jnp.zeros(attn.shape, F32)
        lane = lax.broadcasted_iota(jnp.int32, (cols, D), 1)
        line = lax.broadcasted_iota(jnp.int32, (cols, D), 0)
        for kz in range(nz):
            for ky in range(2):
                spot = (chip ^ (2 * kz + ky)) * cols
                put = (lane == line + spot).astype(F32).astype(BF)
                part = pieces[kz][:, D + ky * cols : D + (ky + 1) * cols]
                whole = whole + dot(part, put, NN)
        attn[...] = whole.astype(BF)


def finish(stream, pieces):
    shape = jax.ShapeDtypeStruct(stream.shape, BF)
    nz = len(pieces)
    return pl.pallas_call(
        functools.partial(finish_kernel, nz),
        out_shape=[shape, shape],
        in_specs=[pl.BlockSpec(memory_space=pltpu.VMEM)] * (nz + 1),
        out_specs=[pl.BlockSpec(memory_space=pltpu.VMEM)] * 2,
        cost_estimate=pl.CostEstimate(
            flops=nz * stream.size, bytes_accessed=4 * nz * stream.size, transcendentals=0
        ),
        compiler_params=pltpu.CompilerParams(vmem_limit_bytes=16 * MIB),
        name="finish",
    )(stream, *pieces)


def body(
    queries,
    keys,
    values,
    lengths,
    owner_counts,
    row_order,
    residual,
    out_weight,
    norm_gain,
    expert_ids,
    route_weights,
    gate_up,
    expert_down,
):
    width = lax.axis_size("ctx")
    chips, nz = width // 2, width // 4
    per = queries.shape[0]
    cap = residual.shape[0]
    order = row_order.reshape(1, -1)

    def along_z(terms):
        out = [terms[0]]
        for kz in range(1, nz):
            out.append(hop(terms[kz], 4 * kz, width))
        return out

    def add(*terms):
        return small(total_kernel, terms[0].shape, *terms)

    near = hop(queries, 2, width)
    k_oth = hop(keys, 1, width)
    v_oth = hop(values, 1, width)
    q_own, k_own, v_own = fetch(queries, keys, values)
    column = small(pair_kernel, (2,) + queries.shape, q_own, near)
    pieces = along_z([column] * nz)
    w_oth = hop(out_weight, 1, width)
    res_own, home, fill, turn, w_own, gain = prepare(
        owner_counts.reshape(1, -1),
        order,
        expert_ids.T,
        route_weights.T,
        residual,
        out_weight,
        norm_gain.reshape(1, -1),
        per,
        width,
    )
    res_oth = hop(res_own, 1, width)

    blocks = along_z(attention(pieces, k_own, v_own, k_oth, v_oth, lengths, chips))
    mine, theirs = fold(blocks)
    theirs = hop(theirs, 2, width)
    *parts, mixed = project(mine, theirs, w_own, w_oth, res_own, res_oth, home, nz)
    chunk = add(*along_z(parts))
    (up,) = fetch(gate_up)
    other = hop(chunk, 2, width)
    chunk = add(chunk, other)
    mine = along_z([chunk] * nz)
    theirs = [hop(x, 1, width) for x in mine]
    (down,) = fetch(expert_down)
    keep0, keep1, send0, send1, stream = experts(
        mine, theirs, gain, up, down, turn, fill, mixed, width, cap
    )
    far = hop(add(keep1, hop(send1, 1, width)), 2, width)
    sums = mix(keep0, hop(send0, 1, width), far, nz)
    attn, layer_out = finish(stream, along_z(sums))
    return (attn, layer_out)


def solution(mesh):
    placed = (
        P(("groups", "ctx"), None),
        P("groups", "ctx", None),
        P("groups", "ctx", None),
        P("groups"),
        P("groups"),
        P("groups"),
        P(("groups", "ctx"), None),
        P("ctx", None),
        P(),
        P(("groups", "ctx"), None),
        P(("groups", "ctx"), None),
        P("ctx", None, None),
        P("ctx", None, None),
    )

    return jax.shard_map(
        body,
        mesh=mesh,
        in_specs=placed,
        out_specs=(P(("groups", "ctx"), None), P(("groups", "ctx"), None)),
        check_vma=False,
    )
```

```python
import functools

import jax
import jax.numpy as jnp
from jax import lax
from jax.experimental import pallas as pl
from jax.experimental.pallas import tpu as pltpu
from jax.sharding import PartitionSpec as P


D = 2048
HQ = 16
KVH = 2
HD = 128
EFF = 768
TOPK = 8
STRETCH = 128
BF = jnp.bfloat16
F32 = jnp.float32
MIB = 1 << 20
LOG2E = 1.4426950408889634
STAT = 8


NT = (((1,), (1,)), ((), ()))
NN = (((1,), (0,)), ((), ()))


def dot(a, b, dims):
    return lax.dot_general(a, b, dims, preferred_element_type=F32)


def place():
    device = lax.axis_index("ctx")
    return device, device & 1, device >> 1, device >> 2


def hop(x, mask, width):
    return lax.ppermute(x, "ctx", [(i, i ^ mask) for i in range(width)])


def sequence(nz):
    return [nz - 1] + list(range(1, nz - 1)) + [0]


def split3(x):
    hi = x.astype(BF)
    rest = x - hi.astype(F32)
    mid = rest.astype(BF)
    return hi, mid, (rest - mid.astype(F32)).astype(BF)


def row_ids(per, core, axis, shape):
    i = lax.broadcasted_iota(jnp.int32, shape, axis)
    return (i // per) * (2 * per) + core * per + i % per


def fetch_kernel(count, *refs):
    sems = refs[2 * count]
    copies = [
        pltpu.make_async_copy(refs[i], refs[count + i], sems.at[i]) for i in range(count)
    ]
    for copy in copies:
        copy.start()
    for copy in copies:
        copy.wait()


def in_hbm(x):
    return pltpu.with_memory_space_constraint(x, pltpu.HBM)


def fetch(*arrays):
    count = len(arrays)
    size = sum(a.size * a.dtype.itemsize for a in arrays)
    return pl.pallas_call(
        functools.partial(fetch_kernel, count),
        out_shape=[pltpu.VMEM(a.shape, a.dtype) for a in arrays],
        in_specs=[pl.BlockSpec(memory_space=pltpu.HBM)] * count,
        out_specs=[pl.BlockSpec(memory_space=pltpu.VMEM)] * count,
        scratch_shapes=[pltpu.SemaphoreType.DMA((count,))],
        cost_estimate=pl.CostEstimate(flops=0, bytes_accessed=2 * size, transcendentals=0),
        compiler_params=pltpu.CompilerParams(vmem_limit_bytes=16 * MIB),
        name="fetch",
    )(*[in_hbm(a) for a in arrays])


def prepare_kernel(per, width, *refs):
    (counts, order, ids, weights, residual, weight_in, gain_in) = refs[:7]
    (res, home, fill, turn, weight_out, gain_out) = refs[7:13]
    picks, table, own, sems = refs[13:]
    copies = [
        pltpu.make_async_copy(weight_in, weight_out, sems.at[0]),
        pltpu.make_async_copy(gain_in, gain_out, sems.at[1]),
    ]
    for copy in copies:
        copy.start()
    device, core, _, _ = place()
    cap, rows = residual.shape[0], order.shape[1]
    half = home.shape[0]
    slots = picks.shape[0]
    lane = lax.broadcasted_iota(jnp.int32, (width, width), 1)
    line = lax.broadcasted_iota(jnp.int32, (width, width), 0)
    many = counts[...].astype(F32)
    end = jnp.sum(jnp.where(lane <= line, many, 0.0), axis=1, keepdims=True)
    size = jnp.sum(jnp.where(lane == line, many, 0.0), axis=1, keepdims=True)
    p = lax.broadcasted_iota(jnp.int32, (width, rows), 1).astype(F32)
    past = (p >= end).astype(F32)
    owner = jnp.sum(past, axis=0, keepdims=True)
    start = jnp.sum(past * size, axis=0, keepdims=True)
    slot = owner * cap + p[:1] - start
    at = lax.broadcasted_iota(jnp.int32, (slots, rows), 0).astype(F32)
    picks[...] = (at == slot).astype(F32).astype(BF)
    seats = [
        (order[...] == row_ids(per, c, 0, (half, rows))).astype(F32).astype(BF)
        for c in range(2)
    ]
    mine = (order[...] == row_ids(per, core, 0, (half, rows))).astype(F32).astype(BF)
    own[...] = dot(picks[...], mine, NT).astype(BF)
    table[...] = dot(picks[...], jnp.concatenate(seats, axis=0), NT).astype(BF)
    for kc in range(2):
        for ky in range(2):
            for spot, kz in enumerate(sequence(width // 4)):
                there = device ^ (kc + 2 * ky + 4 * kz)
                there = pl.ds(pl.multiple_of(there * cap, cap), cap)
                to = (kc * 2 + ky) * (width // 4) + spot
                turn[to * cap : (to + 1) * cap, :] = table[there, :]
                fill[to * cap : (to + 1) * cap, :] = own[there, :]
    chip_picks = [
        picks[pl.ds(pl.multiple_of(o * cap, cap), cap), :] for o in (device, device ^ 1)
    ]
    home[...] = dot(mine, jnp.concatenate(chip_picks, axis=0), NT).astype(BF)
    lanes = res.shape[1] - D
    kind = lax.broadcasted_iota(jnp.int32, (lanes, cap), 0)
    norm = weights[...] / jnp.sum(weights[...], axis=0, keepdims=True)
    dense = jnp.zeros((lanes, cap), F32)
    for k in range(TOPK):
        dense = dense + jnp.where(ids[k : k + 1, :] == kind % width, norm[k : k + 1, :], 0.0)
    high = dense.astype(BF).astype(F32)
    low = jnp.where(kind < 2 * width, dense - high, 0.0)
    both = jnp.where(kind < width, high, low).astype(BF)
    i = lax.broadcasted_iota(jnp.int32, (cap, cap), 0)
    j = lax.broadcasted_iota(jnp.int32, (cap, cap), 1)
    res[:, :D] = residual[...]
    res[:, D:] = dot((i == j).astype(F32).astype(BF), both, NT).astype(BF)
    for copy in copies:
        copy.wait()


def prepare(counts, order, ids, weights, residual, out_weight, gain, per, width):
    cap, rows = residual.shape[0], order.shape[1]
    half = width // 2 * per
    lanes = -(-2 * width // 128) * 128
    slots = width * cap
    given = (counts, order, ids, weights, residual, out_weight, gain)
    return pl.pallas_call(
        functools.partial(prepare_kernel, per, width),
        out_shape=[
            jax.ShapeDtypeStruct((cap, D + lanes), BF),
            jax.ShapeDtypeStruct((half, 2 * cap), BF),
            jax.ShapeDtypeStruct((slots, half), BF),
            jax.ShapeDtypeStruct((slots, 2 * half), BF),
            pltpu.VMEM(out_weight.shape, out_weight.dtype),
            pltpu.VMEM(gain.shape, gain.dtype),
        ],
        in_specs=[pl.BlockSpec(memory_space=pltpu.VMEM)] * 5
        + [pl.BlockSpec(memory_space=pltpu.HBM)] * 2,
        out_specs=[pl.BlockSpec(memory_space=pltpu.VMEM)] * 6,
        scratch_shapes=[
            pltpu.VMEM((slots, rows), BF),
            pltpu.VMEM((slots, 2 * half), BF),
            pltpu.VMEM((slots, half), BF),
            pltpu.SemaphoreType.DMA((2,)),
        ],
        cost_estimate=pl.CostEstimate(
            flops=6 * slots * rows * half, bytes_accessed=8 * slots * half, transcendentals=0
        ),
        compiler_params=pltpu.CompilerParams(vmem_limit_bytes=12 * MIB),
        name="prepare",
    )(*[in_hbm(a) for a in given])


def total_kernel(*refs):
    terms, out = refs[:-1], refs[-1]
    out[...] = functools.reduce(lambda a, b: a + b, [t[...].astype(F32) for t in terms]).astype(BF)


def pair_kernel(first, second, out):
    out[0] = first[...]
    out[1] = second[...]


def small(kernel, shape, *terms):
    return pl.pallas_call(
        kernel,
        out_shape=jax.ShapeDtypeStruct(shape, BF),
        in_specs=[pl.BlockSpec(memory_space=pltpu.VMEM)] * len(terms),
        out_specs=pl.BlockSpec(memory_space=pltpu.VMEM),
        cost_estimate=pl.CostEstimate(
            flops=len(terms) * terms[0].size,
            bytes_accessed=2 * (len(terms) + 1) * terms[0].size,
            transcendentals=0,
        ),
        compiler_params=pltpu.CompilerParams(vmem_limit_bytes=16 * MIB),
    )(*terms)


def attention_kernel(nz, lengths, *refs):
    pieces, (k_own, v_own, k_oth, v_oth) = refs[:nz], refs[nz : nz + 4]
    outs, (rows, ready) = refs[nz + 4 : nz + 8], refs[nz + 8 :]
    device, core, chip, _ = place()
    per = pieces[0].shape[1]
    requests, span = k_own.shape[0], k_own.shape[1]
    count = rows.shape[0]
    seat = count // requests
    chips, depth = ready.shape[0], ready.shape[1] - STAT
    cols = HQ * HD // chips
    heads = max(1, cols // HD)
    group = HQ // KVH
    for kz in range(nz):
        both = pieces[kz][...].astype(F32)
        for ky in range(2):
            spot = (chip ^ (2 * kz + ky)) * per
            rows[pl.ds(pl.multiple_of(spot, per), per), :] = both[ky]
    wide = group * seat
    key = lax.broadcasted_iota(jnp.int32, (span, wide), 0)
    lane = lax.broadcasted_iota(jnp.int32, (1, wide), 1) % seat
    ahead = (lane // per) * (2 * per) + core * per + lane % per - STRETCH
    first_own, first_oth = device * span, (device ^ 1) * span
    for q in range(requests):
        last = lengths[q] + ahead
        see_own, see_oth = key <= last - first_own, key <= last - first_oth
        for v in range(KVH):
            kv = slice(v * HD, (v + 1) * HD)
            asked = jnp.concatenate(
                [
                    rows[q * seat : (q + 1) * seat, h * HD : (h + 1) * HD]
                    for h in range(v * group, (v + 1) * group)
                ],
                axis=0,
            ).astype(BF)
            s_own = dot(k_own[q, :, kv], asked, NT) * (HD ** (-0.5) * LOG2E)
            s_oth = dot(k_oth[q, :, kv], asked, NT) * (HD ** (-0.5) * LOG2E)
            s_own = jnp.where(see_own, s_own, -1e30)
            s_oth = jnp.where(see_oth, s_oth, -1e30)
            top = jnp.maximum(
                jnp.max(s_own, axis=0, keepdims=True), jnp.max(s_oth, axis=0, keepdims=True)
            )
            top = jnp.maximum(top, -1e29)
            w_own = jnp.exp2(s_own - top)
            w_oth = jnp.exp2(s_oth - top)
            total = jnp.sum(w_own, axis=0, keepdims=True) + jnp.sum(w_oth, axis=0, keepdims=True)
            mixed = dot(v_own[q, :, kv].T, w_own.astype(BF), NN) + dot(
                v_oth[q, :, kv].T, w_oth.astype(BF), NN
            )
            some = total > 0.0
            safe = jnp.where(some, total, 1.0)
            mixed = (mixed * (1.0 / safe)).astype(BF)
            lse = jnp.where(some, top * (1.0 / LOG2E) + jnp.log(safe), -1e30)
            stat = with_lse(lse)
            if heads == 2 and requests == 1:
                for g in range(group // 2):
                    dest = (v * group // 2 + g) ^ chip
                    mine = slice(2 * g * seat, 2 * (g + 1) * seat)
                    ready[dest, :depth, :] = mixed[:, mine]
                    ready[dest, depth:, :] = stat[:, mine]
            else:
                for e in range(group):
                    mine = slice(e * seat, (e + 1) * seat)
                    head = v * group + e
                    lo = (head % heads) * count + q * seat
                    for part in range(HD // depth):
                        dest = ((head * HD + part * depth) // cols) ^ chip
                        some_rows = slice(part * depth, (part + 1) * depth)
                        ready[dest, :depth, lo : lo + seat] = mixed[some_rows, mine]
                        ready[dest, depth:, lo : lo + seat] = stat[:, mine]
    order = sequence(nz)
    for ky in range(2):
        for spot, kz in enumerate(order):
            outs[2 * ky + spot // (nz // 2)][spot % (nz // 2)] = ready[2 * kz + ky]


def with_lse(lse):
    parts = [x.astype(F32) for x in split3(lse)]
    return jnp.concatenate(parts + [jnp.zeros((STAT - 3, lse.shape[1]), F32)], axis=0).astype(BF)


def attention(pieces, k_own, v_own, k_oth, v_oth, lengths, chips):
    nz = len(pieces)
    per = pieces[0].shape[1]
    count = chips * per
    cols = HQ * HD // chips
    heads = max(1, cols // HD)
    shape = (nz // 2, min(cols, HD) + STAT, heads * count)
    work = 4 * k_own.size * (HQ // KVH) * 2 * count
    return pl.pallas_call(
        functools.partial(attention_kernel, nz),
        out_shape=[jax.ShapeDtypeStruct(shape, BF)] * 4,
        in_specs=[pl.BlockSpec(memory_space=pltpu.SMEM)]
        + [pl.BlockSpec(memory_space=pltpu.VMEM)] * (nz + 4),
        out_specs=[pl.BlockSpec(memory_space=pltpu.VMEM)] * 4,
        scratch_shapes=[
            pltpu.VMEM((count, HQ * HD), F32),
            pltpu.VMEM((chips,) + shape[1:], BF),
        ],
        cost_estimate=pl.CostEstimate(
            flops=work, bytes_accessed=8 * k_own.size, transcendentals=work // (4 * HD)
        ),
        compiler_params=pltpu.CompilerParams(vmem_limit_bytes=24 * MIB),
        name="attention",
    )(lengths, *pieces, k_own, v_own, k_oth, v_oth)


def merged(blocks):
    depth = blocks[0].shape[0] - STAT
    lse = [jnp.sum(x[depth:].astype(F32), axis=0, keepdims=True) for x in blocks]
    best = functools.reduce(jnp.maximum, lse)
    factor = [jnp.exp(x - best) for x in lse]
    denom = functools.reduce(lambda a, b: a + b, factor)
    mixed = functools.reduce(
        lambda a, b: a + b, [x[:depth].astype(F32) * f for x, f in zip(blocks, factor)]
    )
    return mixed * (1.0 / denom), best + jnp.log(denom)


def fold_kernel(near, far, *outs):
    depth = outs[0].shape[0] - STAT
    for i, out in enumerate(outs):
        mixed, lse = merged([near[i], far[i]])
        out[:depth, :] = mixed.astype(BF)
        out[depth:, :] = with_lse(lse)


def fold(near, far):
    count = near.shape[0]
    return pl.pallas_call(
        fold_kernel,
        out_shape=[jax.ShapeDtypeStruct(near.shape[1:], BF)] * count,
        in_specs=[pl.BlockSpec(memory_space=pltpu.VMEM)] * 2,
        out_specs=[pl.BlockSpec(memory_space=pltpu.VMEM)] * count,
        cost_estimate=pl.CostEstimate(
            flops=8 * near.size, bytes_accessed=8 * near.size, transcendentals=0
        ),
        compiler_params=pltpu.CompilerParams(vmem_limit_bytes=16 * MIB),
        name="fold",
    )(near, far)


def project_kernel(nz, *refs):
    blocks, (w_own, w_oth, res_own, res_oth, home) = refs[:nz], refs[nz : nz + 5]
    outs, attn, part = refs[nz + 5 : 2 * nz + 5], refs[2 * nz + 5], refs[2 * nz + 6]
    _, core, _, z = place()
    depth = blocks[0].shape[0] - STAT
    count = part.shape[0]
    heads = blocks[0].shape[1] // count
    mixed, _ = merged([b[...] for b in blocks])
    mixed = mixed.T.astype(BF)
    if heads == 2:
        first, second = mixed[:count], mixed[count:]
        attn[...] = jnp.concatenate([first, second], axis=1)
    else:
        first, second = mixed[:, : depth // 2], mixed[:, depth // 2 :]
        attn[...] = mixed
    low = (core == 0).astype(F32)
    first, second = first.astype(F32), second.astype(F32)
    own = (first * low + second * (1.0 - low)).astype(BF)
    oth = (second * low + first * (1.0 - low)).astype(BF)
    res = jnp.concatenate([res_own[...], res_oth[...]], axis=0)
    part[:, :D] = (
        dot(home[...], res[:, :D], NN) + dot(own, w_own[...], NN) + dot(oth, w_oth[...], NN)
    )
    part[:, D:] = dot(home[...], res[:, D:], NN)
    block = outs[0].shape[0]
    for kz in range(nz):
        spot = pl.multiple_of((z ^ kz) * block, block)
        outs[kz][...] = part[pl.ds(spot, block), :].astype(BF)


def project(blocks, w_own, w_oth, res_own, res_oth, home):
    nz = len(blocks)
    count = home.shape[0]
    cols = D // (2 * nz)
    wide = res_own.shape[1]
    return pl.pallas_call(
        functools.partial(project_kernel, nz),
        out_shape=[jax.ShapeDtypeStruct((count // nz, wide), BF)] * nz
        + [jax.ShapeDtypeStruct((count, cols), BF)],
        in_specs=[pl.BlockSpec(memory_space=pltpu.VMEM)] * (nz + 5),
        out_specs=[pl.BlockSpec(memory_space=pltpu.VMEM)] * (nz + 1),
        scratch_shapes=[pltpu.VMEM((count, wide), F32)],
        cost_estimate=pl.CostEstimate(
            flops=2 * count * cols * D, bytes_accessed=4 * cols * D, transcendentals=0
        ),
        compiler_params=pltpu.CompilerParams(vmem_limit_bytes=12 * MIB),
        name="project",
    )(*blocks, w_own, w_oth, res_own, res_oth, home)


def expert_kernel(nz, width, *refs):
    mine, theirs = refs[:nz], refs[nz : 2 * nz]
    (gain, gate_up, down, turn, fill, mixed) = refs[2 * nz : 2 * nz + 6]
    outs, stream_own = refs[2 * nz + 6 : 2 * nz + 12], refs[2 * nz + 12]
    x, normed, hidden, scaled = refs[2 * nz + 13 :]
    device, core, _, z = place()
    block = mine[0].shape[0]
    half = block * nz
    cap = stream_own.shape[0]
    for kz in range(nz):
        spot = (z ^ kz) * block
        x[pl.ds(pl.multiple_of(core * half + spot, block), block), :] = mine[kz][...]
        x[pl.ds(pl.multiple_of((1 - core) * half + spot, block), block), :] = theirs[kz][...]
    stream = x[:, :D].astype(F32)
    scale = lax.rsqrt(jnp.mean(stream * stream, axis=-1, keepdims=True) + 1e-06)
    normed[...] = (stream * scale * gain[...]).astype(BF)
    extra = x[:, D:].astype(F32)
    lane = lax.broadcasted_iota(jnp.int32, extra.shape, 1)
    pick = (lane == device) | (lane == device + width)
    weight = jnp.sum(jnp.where(pick, extra, 0.0), axis=-1, keepdims=True)
    tile = 256
    for lo in range(0, EFF, tile):
        g = dot(normed[...], gate_up[0, :, lo : lo + tile], NN)
        u = dot(normed[...], gate_up[0, :, EFF + lo : EFF + lo + tile], NN)
        hidden[:, lo : lo + tile] = (g / (1.0 + jnp.exp(-g)) * u).astype(BF)
    for lo in range(0, D, tile):
        y = dot(hidden[...], down[0, :, lo : lo + tile], NN).astype(BF)
        scaled[:, lo : lo + tile] = (y.astype(F32) * weight).astype(BF)
    done = 0
    for target in outs:
        some = slice(done, done + target.shape[0])
        target[:, :D] = dot(turn[some, :], scaled[...], NN).astype(BF)
        target[:, D:] = dot(fill[some, :], mixed[...], NN).astype(BF)
        done = done + target.shape[0]
    stream_own[...] = dot(turn[(nz - 1) * cap : nz * cap, :], x[:, :D], NN).astype(BF)


def experts(mine, theirs, gain, gate_up, down, turn, fill, mixed, width, cap):
    nz = len(mine)
    block, wide = mine[0].shape
    total = 2 * nz * block
    whole = jax.ShapeDtypeStruct((nz * cap, D + mixed.shape[1]), BF)
    half = jax.ShapeDtypeStruct((nz // 2 * cap, D + mixed.shape[1]), BF)
    return pl.pallas_call(
        functools.partial(expert_kernel, nz, width),
        out_shape=[whole, half, half] * 2 + [jax.ShapeDtypeStruct((cap, D), BF)],
        in_specs=[pl.BlockSpec(memory_space=pltpu.VMEM)] * (2 * nz + 6),
        out_specs=[pl.BlockSpec(memory_space=pltpu.VMEM)] * 7,
        scratch_shapes=[
            pltpu.VMEM((total, wide), BF),
            pltpu.VMEM((total, D), BF),
            pltpu.VMEM((total, EFF), BF),
            pltpu.VMEM((total, D), BF),
        ],
        cost_estimate=pl.CostEstimate(
            flops=6 * total * D * EFF, bytes_accessed=6 * D * EFF, transcendentals=total * EFF
        ),
        compiler_params=pltpu.CompilerParams(vmem_limit_bytes=32 * MIB),
        name="experts",
    )(*mine, *theirs, gain, gate_up, down, turn, fill, mixed)


def mix_kernel(first, keep, near, far, *outs):
    cap = outs[0].shape[0]
    for i, out in enumerate(outs):
        here = slice((first + i) * cap, (first + i + 1) * cap)
        own = keep[here, :].astype(F32) + near[here, :].astype(F32)
        other = far[i * cap : (i + 1) * cap, :].astype(F32)
        out[:, :D] = (own[:, :D] + other[:, :D]).astype(BF)
        out[:, D:] = jnp.concatenate([own[:, D:], other[:, D:]], axis=1).astype(BF)


def mix(keep, near, far, cap, first):
    count = far.shape[0] // cap
    cols = keep.shape[1] - D
    return pl.pallas_call(
        functools.partial(mix_kernel, first),
        out_shape=[jax.ShapeDtypeStruct((cap, D + 2 * cols), BF)] * count,
        in_specs=[pl.BlockSpec(memory_space=pltpu.VMEM)] * 3,
        out_specs=[pl.BlockSpec(memory_space=pltpu.VMEM)] * count,
        cost_estimate=pl.CostEstimate(
            flops=3 * far.size, bytes_accessed=8 * far.size, transcendentals=0
        ),
        compiler_params=pltpu.CompilerParams(vmem_limit_bytes=16 * MIB),
        name="mix",
    )(keep, near, far)


def finish_kernel(nz, stream, *refs):
    pieces, (attn, out) = refs[:nz], refs[nz:]
    _, _, chip, _ = place()
    cols = (pieces[0].shape[1] - D) // 2
    total = stream[...].astype(F32)
    for kz in range(nz):
        total = total + pieces[kz][:, :D].astype(F32)
    out[...] = total.astype(BF)
    if cols % 128 == 0:
        for kz in range(nz):
            for ky in range(2):
                spot = pl.multiple_of((chip ^ (2 * kz + ky)) * cols, cols)
                attn[:, pl.ds(spot, cols)] = pieces[kz][:, D + ky * cols : D + (ky + 1) * cols]
    else:
        whole = jnp.zeros(attn.shape, F32)
        lane = lax.broadcasted_iota(jnp.int32, (cols, D), 1)
        line = lax.broadcasted_iota(jnp.int32, (cols, D), 0)
        for kz in range(nz):
            for ky in range(2):
                spot = (chip ^ (2 * kz + ky)) * cols
                put = (lane == line + spot).astype(F32).astype(BF)
                part = pieces[kz][:, D + ky * cols : D + (ky + 1) * cols]
                whole = whole + dot(part, put, NN)
        attn[...] = whole.astype(BF)


def finish(stream, pieces):
    shape = jax.ShapeDtypeStruct(stream.shape, BF)
    nz = len(pieces)
    return pl.pallas_call(
        functools.partial(finish_kernel, nz),
        out_shape=[shape, shape],
        in_specs=[pl.BlockSpec(memory_space=pltpu.VMEM)] * (nz + 1),
        out_specs=[pl.BlockSpec(memory_space=pltpu.VMEM)] * 2,
        cost_estimate=pl.CostEstimate(
            flops=nz * stream.size, bytes_accessed=4 * nz * stream.size, transcendentals=0
        ),
        compiler_params=pltpu.CompilerParams(vmem_limit_bytes=16 * MIB),
        name="finish",
    )(stream, *pieces)


def body(
    queries,
    keys,
    values,
    lengths,
    owner_counts,
    row_order,
    residual,
    out_weight,
    norm_gain,
    expert_ids,
    route_weights,
    gate_up,
    expert_down,
):
    width = lax.axis_size("ctx")
    chips, nz = width // 2, width // 4
    per = queries.shape[0]
    cap = residual.shape[0]
    order = row_order.reshape(1, -1)

    def along_z(terms):
        out = [terms[0]]
        for kz in range(1, nz):
            out.append(hop(terms[kz], 4 * kz, width))
        return out

    def by_distance(blocks):
        return [blocks[sequence(nz).index(kz)] for kz in range(nz)]

    def add(*terms):
        return small(total_kernel, terms[0].shape, *terms)

    near = hop(queries, 2, width)
    k_oth = hop(keys, 1, width)
    v_oth = hop(values, 1, width)
    q_own, k_own, v_own = fetch(queries, keys, values)
    column = small(pair_kernel, (2,) + queries.shape, q_own, near)
    pieces = along_z([column] * nz)
    w_oth = hop(out_weight, 1, width)
    res_own, home, fill, turn, w_own, gain = prepare(
        owner_counts.reshape(1, -1),
        order,
        expert_ids.T,
        route_weights.T,
        residual,
        out_weight,
        norm_gain.reshape(1, -1),
        per,
        width,
    )
    res_oth = hop(res_own, 1, width)

    near_a, near_b, far_a, far_b = attention(
        pieces, k_own, v_own, k_oth, v_oth, lengths, chips
    )
    far_a = hop(far_a, 2, width)
    far_b = hop(far_b, 2, width)
    first = fold(near_a, far_a)
    second = fold(near_b, far_b)
    blocks = along_z(by_distance(first + second))
    *parts, mixed = project(blocks, w_own, w_oth, res_own, res_oth, home)
    chunk = add(*along_z(parts))
    (up,) = fetch(gate_up)
    other = hop(chunk, 2, width)
    chunk = add(chunk, other)
    mine = along_z([chunk] * nz)
    theirs = [hop(x, 1, width) for x in mine]
    (down,) = fetch(expert_down)
    keep, keep_a, keep_b, send, send_a, send_b, stream = experts(
        mine, theirs, gain, up, down, turn, fill, mixed, width, cap
    )
    got_a = hop(send_a, 1, width)
    got_b = hop(send_b, 1, width)
    got = hop(send, 1, width)
    far_a, far_b = add(keep_a, got_a), add(keep_b, got_b)
    far_a = hop(far_a, 2, width)
    far_b = hop(far_b, 2, width)
    first = mix(keep, got, far_a, cap, 0)
    second = mix(keep, got, far_b, cap, nz // 2)
    attn, layer_out = finish(stream, along_z(by_distance(first + second)))
    return (attn, layer_out)


def solution(mesh):
    placed = (
        P(("groups", "ctx"), None),
        P("groups", "ctx", None),
        P("groups", "ctx", None),
        P("groups"),
        P("groups"),
        P("groups"),
        P(("groups", "ctx"), None),
        P("ctx", None),
        P(),
        P(("groups", "ctx"), None),
        P(("groups", "ctx"), None),
        P("ctx", None, None),
        P("ctx", None, None),
    )

    return jax.shard_map(
        body,
        mesh=mesh,
        in_specs=placed,
        out_specs=(P(("groups", "ctx"), None), P(("groups", "ctx"), None)),
        check_vma=False,
    )
```

```python
import functools

import jax
import jax.numpy as jnp
from jax import lax
from jax.experimental import pallas as pl
from jax.experimental.pallas import tpu as pltpu
from jax.sharding import PartitionSpec as P


D = 2048
HQ = 16
KVH = 2
HD = 128
EFF = 768
TOPK = 8
STRETCH = 128
BF = jnp.bfloat16
F32 = jnp.float32
MIB = 1 << 20
LOG2E = 1.4426950408889634
STAT = 8


NT = (((1,), (1,)), ((), ()))
NN = (((1,), (0,)), ((), ()))


def dot(a, b, dims):
    return lax.dot_general(a, b, dims, preferred_element_type=F32)


def place():
    device = lax.axis_index("ctx")
    return device, device & 1, device >> 1, device >> 2


def hop(x, mask, width):
    return lax.ppermute(x, "ctx", [(i, i ^ mask) for i in range(width)])


def sequence(nz):
    return list(range(nz - 1, -1, -1))


def portions(nz):
    return [1, 1, nz - 2]


def split3(x):
    hi = x.astype(BF)
    rest = x - hi.astype(F32)
    mid = rest.astype(BF)
    return hi, mid, (rest - mid.astype(F32)).astype(BF)


def row_ids(per, core, axis, shape):
    i = lax.broadcasted_iota(jnp.int32, shape, axis)
    return (i // per) * (2 * per) + core * per + i % per


def fetch_kernel(count, *refs):
    sems = refs[2 * count]
    copies = [
        pltpu.make_async_copy(refs[i], refs[count + i], sems.at[i]) for i in range(count)
    ]
    for copy in copies:
        copy.start()
    for copy in copies:
        copy.wait()


def in_hbm(x):
    return pltpu.with_memory_space_constraint(x, pltpu.HBM)


def fetch(*arrays):
    count = len(arrays)
    size = sum(a.size * a.dtype.itemsize for a in arrays)
    return pl.pallas_call(
        functools.partial(fetch_kernel, count),
        out_shape=[pltpu.VMEM(a.shape, a.dtype) for a in arrays],
        in_specs=[pl.BlockSpec(memory_space=pltpu.HBM)] * count,
        out_specs=[pl.BlockSpec(memory_space=pltpu.VMEM)] * count,
        scratch_shapes=[pltpu.SemaphoreType.DMA((count,))],
        cost_estimate=pl.CostEstimate(flops=0, bytes_accessed=2 * size, transcendentals=0),
        compiler_params=pltpu.CompilerParams(vmem_limit_bytes=16 * MIB),
        name="fetch",
    )(*[in_hbm(a) for a in arrays])


def prepare_kernel(per, width, *refs):
    (counts, order, ids, weights, residual, weight_in, gain_in) = refs[:7]
    (res, home, fill, turn, weight_out, gain_out) = refs[7:13]
    picks, table, own, sems = refs[13:]
    copies = [
        pltpu.make_async_copy(weight_in, weight_out, sems.at[0]),
        pltpu.make_async_copy(gain_in, gain_out, sems.at[1]),
    ]
    for copy in copies:
        copy.start()
    device, core, _, _ = place()
    cap, rows = residual.shape[0], order.shape[1]
    half = home.shape[0]
    slots = picks.shape[0]
    lane = lax.broadcasted_iota(jnp.int32, (width, width), 1)
    line = lax.broadcasted_iota(jnp.int32, (width, width), 0)
    many = counts[...].astype(F32)
    end = jnp.sum(jnp.where(lane <= line, many, 0.0), axis=1, keepdims=True)
    size = jnp.sum(jnp.where(lane == line, many, 0.0), axis=1, keepdims=True)
    p = lax.broadcasted_iota(jnp.int32, (width, rows), 1).astype(F32)
    past = (p >= end).astype(F32)
    owner = jnp.sum(past, axis=0, keepdims=True)
    start = jnp.sum(past * size, axis=0, keepdims=True)
    slot = owner * cap + p[:1] - start
    at = lax.broadcasted_iota(jnp.int32, (slots, rows), 0).astype(F32)
    picks[...] = (at == slot).astype(F32).astype(BF)
    seats = [
        (order[...] == row_ids(per, c, 0, (half, rows))).astype(F32).astype(BF)
        for c in range(2)
    ]
    mine = (order[...] == row_ids(per, core, 0, (half, rows))).astype(F32).astype(BF)
    own[...] = dot(picks[...], mine, NT).astype(BF)
    table[...] = dot(picks[...], jnp.concatenate(seats, axis=0), NT).astype(BF)
    for kc in range(2):
        for ky in range(2):
            for spot, kz in enumerate(sequence(width // 4)):
                there = device ^ (kc + 2 * ky + 4 * kz)
                there = pl.ds(pl.multiple_of(there * cap, cap), cap)
                to = (kc * 2 + ky) * (width // 4) + spot
                turn[to * cap : (to + 1) * cap, :] = table[there, :]
                fill[to * cap : (to + 1) * cap, :] = own[there, :]
    chip_picks = [
        picks[pl.ds(pl.multiple_of(o * cap, cap), cap), :] for o in (device, device ^ 1)
    ]
    home[...] = dot(mine, jnp.concatenate(chip_picks, axis=0), NT).astype(BF)
    lanes = res.shape[1] - D
    kind = lax.broadcasted_iota(jnp.int32, (lanes, cap), 0)
    norm = weights[...] / jnp.sum(weights[...], axis=0, keepdims=True)
    dense = jnp.zeros((lanes, cap), F32)
    for k in range(TOPK):
        dense = dense + jnp.where(ids[k : k + 1, :] == kind % width, norm[k : k + 1, :], 0.0)
    high = dense.astype(BF).astype(F32)
    low = jnp.where(kind < 2 * width, dense - high, 0.0)
    both = jnp.where(kind < width, high, low).astype(BF)
    i = lax.broadcasted_iota(jnp.int32, (cap, cap), 0)
    j = lax.broadcasted_iota(jnp.int32, (cap, cap), 1)
    res[:, :D] = residual[...]
    res[:, D:] = dot((i == j).astype(F32).astype(BF), both, NT).astype(BF)
    for copy in copies:
        copy.wait()


def prepare(counts, order, ids, weights, residual, out_weight, gain, per, width):
    cap, rows = residual.shape[0], order.shape[1]
    half = width // 2 * per
    lanes = -(-2 * width // 128) * 128
    slots = width * cap
    given = (counts, order, ids, weights, residual, out_weight, gain)
    return pl.pallas_call(
        functools.partial(prepare_kernel, per, width),
        out_shape=[
            jax.ShapeDtypeStruct((cap, D + lanes), BF),
            jax.ShapeDtypeStruct((half, 2 * cap), BF),
            jax.ShapeDtypeStruct((slots, half), BF),
            jax.ShapeDtypeStruct((slots, 2 * half), BF),
            pltpu.VMEM(out_weight.shape, out_weight.dtype),
            pltpu.VMEM(gain.shape, gain.dtype),
        ],
        in_specs=[pl.BlockSpec(memory_space=pltpu.VMEM)] * 5
        + [pl.BlockSpec(memory_space=pltpu.HBM)] * 2,
        out_specs=[pl.BlockSpec(memory_space=pltpu.VMEM)] * 6,
        scratch_shapes=[
            pltpu.VMEM((slots, rows), BF),
            pltpu.VMEM((slots, 2 * half), BF),
            pltpu.VMEM((slots, half), BF),
            pltpu.SemaphoreType.DMA((2,)),
        ],
        cost_estimate=pl.CostEstimate(
            flops=6 * slots * rows * half, bytes_accessed=8 * slots * half, transcendentals=0
        ),
        compiler_params=pltpu.CompilerParams(vmem_limit_bytes=12 * MIB),
        name="prepare",
    )(*[in_hbm(a) for a in given])


def total_kernel(*refs):
    terms, out = refs[:-1], refs[-1]
    out[...] = functools.reduce(lambda a, b: a + b, [t[...].astype(F32) for t in terms]).astype(BF)


def pair_kernel(first, second, out):
    out[0] = first[...]
    out[1] = second[...]


def small(kernel, shape, *terms):
    return pl.pallas_call(
        kernel,
        out_shape=jax.ShapeDtypeStruct(shape, BF),
        in_specs=[pl.BlockSpec(memory_space=pltpu.VMEM)] * len(terms),
        out_specs=pl.BlockSpec(memory_space=pltpu.VMEM),
        cost_estimate=pl.CostEstimate(
            flops=len(terms) * terms[0].size,
            bytes_accessed=2 * (len(terms) + 1) * terms[0].size,
            transcendentals=0,
        ),
        compiler_params=pltpu.CompilerParams(vmem_limit_bytes=16 * MIB),
    )(*terms)


def attention_kernel(nz, lengths, *refs):
    pieces, (k_own, v_own, k_oth, v_oth) = refs[:nz], refs[nz : nz + 4]
    outs, (rows, ready) = refs[nz + 4 : nz + 8], refs[nz + 8 :]
    device, core, chip, _ = place()
    per = pieces[0].shape[1]
    requests, span = k_own.shape[0], k_own.shape[1]
    count = rows.shape[0]
    seat = count // requests
    chips, depth = ready.shape[0], ready.shape[1] - STAT
    cols = HQ * HD // chips
    heads = max(1, cols // HD)
    group = HQ // KVH
    for kz in range(nz):
        both = pieces[kz][...].astype(F32)
        for ky in range(2):
            spot = (chip ^ (2 * kz + ky)) * per
            rows[pl.ds(pl.multiple_of(spot, per), per), :] = both[ky]
    wide = group * seat
    key = lax.broadcasted_iota(jnp.int32, (span, wide), 0)
    lane = lax.broadcasted_iota(jnp.int32, (1, wide), 1) % seat
    ahead = (lane // per) * (2 * per) + core * per + lane % per - STRETCH
    first_own, first_oth = device * span, (device ^ 1) * span
    for q in range(requests):
        last = lengths[q] + ahead
        see_own, see_oth = key <= last - first_own, key <= last - first_oth
        for v in range(KVH):
            kv = slice(v * HD, (v + 1) * HD)
            asked = jnp.concatenate(
                [
                    rows[q * seat : (q + 1) * seat, h * HD : (h + 1) * HD]
                    for h in range(v * group, (v + 1) * group)
                ],
                axis=0,
            ).astype(BF)
            s_own = dot(k_own[q, :, kv], asked, NT) * (HD ** (-0.5) * LOG2E)
            s_oth = dot(k_oth[q, :, kv], asked, NT) * (HD ** (-0.5) * LOG2E)
            s_own = jnp.where(see_own, s_own, -1e30)
            s_oth = jnp.where(see_oth, s_oth, -1e30)
            top = jnp.maximum(
                jnp.max(s_own, axis=0, keepdims=True), jnp.max(s_oth, axis=0, keepdims=True)
            )
            top = jnp.maximum(top, -1e29)
            w_own = jnp.exp2(s_own - top)
            w_oth = jnp.exp2(s_oth - top)
            total = jnp.sum(w_own, axis=0, keepdims=True) + jnp.sum(w_oth, axis=0, keepdims=True)
            mixed = dot(v_own[q, :, kv].T, w_own.astype(BF), NN) + dot(
                v_oth[q, :, kv].T, w_oth.astype(BF), NN
            )
            some = total > 0.0
            safe = jnp.where(some, total, 1.0)
            mixed = (mixed * (1.0 / safe)).astype(BF)
            lse = jnp.where(some, top * (1.0 / LOG2E) + jnp.log(safe), -1e30)
            stat = with_lse(lse)
            if heads == 2 and requests == 1:
                for g in range(group // 2):
                    dest = (v * group // 2 + g) ^ chip
                    mine = slice(2 * g * seat, 2 * (g + 1) * seat)
                    ready[dest, :depth, :] = mixed[:, mine]
                    ready[dest, depth:, :] = stat[:, mine]
            else:
                for e in range(group):
                    mine = slice(e * seat, (e + 1) * seat)
                    head = v * group + e
                    lo = (head % heads) * count + q * seat
                    for part in range(HD // depth):
                        dest = ((head * HD + part * depth) // cols) ^ chip
                        some_rows = slice(part * depth, (part + 1) * depth)
                        ready[dest, :depth, lo : lo + seat] = mixed[some_rows, mine]
                        ready[dest, depth:, lo : lo + seat] = stat[:, mine]
    order = sequence(nz)
    for ky in range(2):
        for spot, kz in enumerate(order):
            outs[2 * ky + spot // (nz // 2)][spot % (nz // 2)] = ready[2 * kz + ky]


def with_lse(lse):
    parts = [x.astype(F32) for x in split3(lse)]
    return jnp.concatenate(parts + [jnp.zeros((STAT - 3, lse.shape[1]), F32)], axis=0).astype(BF)


def attention(pieces, k_own, v_own, k_oth, v_oth, lengths, chips):
    nz = len(pieces)
    per = pieces[0].shape[1]
    count = chips * per
    cols = HQ * HD // chips
    heads = max(1, cols // HD)
    shape = (nz // 2, min(cols, HD) + STAT, heads * count)
    work = 4 * k_own.size * (HQ // KVH) * 2 * count
    return pl.pallas_call(
        functools.partial(attention_kernel, nz),
        out_shape=[jax.ShapeDtypeStruct(shape, BF)] * 4,
        in_specs=[pl.BlockSpec(memory_space=pltpu.SMEM)]
        + [pl.BlockSpec(memory_space=pltpu.VMEM)] * (nz + 4),
        out_specs=[pl.BlockSpec(memory_space=pltpu.VMEM)] * 4,
        scratch_shapes=[
            pltpu.VMEM((count, HQ * HD), F32),
            pltpu.VMEM((chips,) + shape[1:], BF),
        ],
        cost_estimate=pl.CostEstimate(
            flops=work, bytes_accessed=8 * k_own.size, transcendentals=work // (4 * HD)
        ),
        compiler_params=pltpu.CompilerParams(vmem_limit_bytes=24 * MIB),
        name="attention",
    )(lengths, *pieces, k_own, v_own, k_oth, v_oth)


def merged(blocks):
    depth = blocks[0].shape[0] - STAT
    lse = [jnp.sum(x[depth:].astype(F32), axis=0, keepdims=True) for x in blocks]
    best = functools.reduce(jnp.maximum, lse)
    factor = [jnp.exp(x - best) for x in lse]
    denom = functools.reduce(lambda a, b: a + b, factor)
    mixed = functools.reduce(
        lambda a, b: a + b, [x[:depth].astype(F32) * f for x, f in zip(blocks, factor)]
    )
    return mixed * (1.0 / denom), best + jnp.log(denom)


def fold_kernel(near, far, *outs):
    depth = outs[0].shape[0] - STAT
    for i, out in enumerate(outs):
        mixed, lse = merged([near[i], far[i]])
        out[:depth, :] = mixed.astype(BF)
        out[depth:, :] = with_lse(lse)


def fold(near, far):
    count = near.shape[0]
    return pl.pallas_call(
        fold_kernel,
        out_shape=[jax.ShapeDtypeStruct(near.shape[1:], BF)] * count,
        in_specs=[pl.BlockSpec(memory_space=pltpu.VMEM)] * 2,
        out_specs=[pl.BlockSpec(memory_space=pltpu.VMEM)] * count,
        cost_estimate=pl.CostEstimate(
            flops=8 * near.size, bytes_accessed=8 * near.size, transcendentals=0
        ),
        compiler_params=pltpu.CompilerParams(vmem_limit_bytes=16 * MIB),
        name="fold",
    )(near, far)


def project_kernel(nz, *refs):
    blocks, (w_own, w_oth, res_own, res_oth, home) = refs[:nz], refs[nz : nz + 5]
    outs, attn, part = refs[nz + 5 : 2 * nz + 5], refs[2 * nz + 5], refs[2 * nz + 6]
    _, core, _, z = place()
    depth = blocks[0].shape[0] - STAT
    count = part.shape[0]
    heads = blocks[0].shape[1] // count
    mixed, _ = merged([b[...] for b in blocks])
    mixed = mixed.T.astype(BF)
    if heads == 2:
        first, second = mixed[:count], mixed[count:]
        attn[...] = jnp.concatenate([first, second], axis=1)
    else:
        first, second = mixed[:, : depth // 2], mixed[:, depth // 2 :]
        attn[...] = mixed
    low = (core == 0).astype(F32)
    first, second = first.astype(F32), second.astype(F32)
    own = (first * low + second * (1.0 - low)).astype(BF)
    oth = (second * low + first * (1.0 - low)).astype(BF)
    res = jnp.concatenate([res_own[...], res_oth[...]], axis=0)
    part[:, :D] = (
        dot(home[...], res[:, :D], NN) + dot(own, w_own[...], NN) + dot(oth, w_oth[...], NN)
    )
    part[:, D:] = dot(home[...], res[:, D:], NN)
    block = outs[0].shape[0]
    for kz in range(nz):
        spot = pl.multiple_of((z ^ kz) * block, block)
        outs[kz][...] = part[pl.ds(spot, block), :].astype(BF)


def project(blocks, w_own, w_oth, res_own, res_oth, home):
    nz = len(blocks)
    count = home.shape[0]
    cols = D // (2 * nz)
    wide = res_own.shape[1]
    return pl.pallas_call(
        functools.partial(project_kernel, nz),
        out_shape=[jax.ShapeDtypeStruct((count // nz, wide), BF)] * nz
        + [jax.ShapeDtypeStruct((count, cols), BF)],
        in_specs=[pl.BlockSpec(memory_space=pltpu.VMEM)] * (nz + 5),
        out_specs=[pl.BlockSpec(memory_space=pltpu.VMEM)] * (nz + 1),
        scratch_shapes=[pltpu.VMEM((count, wide), F32)],
        cost_estimate=pl.CostEstimate(
            flops=2 * count * cols * D, bytes_accessed=4 * cols * D, transcendentals=0
        ),
        compiler_params=pltpu.CompilerParams(vmem_limit_bytes=12 * MIB),
        name="project",
    )(*blocks, w_own, w_oth, res_own, res_oth, home)


def expert_kernel(nz, width, *refs):
    mine, theirs = refs[:nz], refs[nz : 2 * nz]
    (gain, gate_up, down, turn, fill, mixed) = refs[2 * nz : 2 * nz + 6]
    *outs, stream_own, x, normed, hidden, scaled = refs[2 * nz + 6 :]
    device, core, _, z = place()
    block = mine[0].shape[0]
    half = block * nz
    cap = stream_own.shape[0]
    for kz in range(nz):
        spot = (z ^ kz) * block
        x[pl.ds(pl.multiple_of(core * half + spot, block), block), :] = mine[kz][...]
        x[pl.ds(pl.multiple_of((1 - core) * half + spot, block), block), :] = theirs[kz][...]
    stream = x[:, :D].astype(F32)
    scale = lax.rsqrt(jnp.mean(stream * stream, axis=-1, keepdims=True) + 1e-06)
    normed[...] = (stream * scale * gain[...]).astype(BF)
    extra = x[:, D:].astype(F32)
    lane = lax.broadcasted_iota(jnp.int32, extra.shape, 1)
    pick = (lane == device) | (lane == device + width)
    weight = jnp.sum(jnp.where(pick, extra, 0.0), axis=-1, keepdims=True)
    tile = 256
    for lo in range(0, EFF, tile):
        g = dot(normed[...], gate_up[0, :, lo : lo + tile], NN)
        u = dot(normed[...], gate_up[0, :, EFF + lo : EFF + lo + tile], NN)
        hidden[:, lo : lo + tile] = (g / (1.0 + jnp.exp(-g)) * u).astype(BF)
    for lo in range(0, D, tile):
        y = dot(hidden[...], down[0, :, lo : lo + tile], NN).astype(BF)
        scaled[:, lo : lo + tile] = (y.astype(F32) * weight).astype(BF)
    done = 0
    for target in outs:
        some = slice(done, done + target.shape[0])
        target[:, :D] = dot(turn[some, :], scaled[...], NN).astype(BF)
        target[:, D:] = dot(fill[some, :], mixed[...], NN).astype(BF)
        done = done + target.shape[0]
    stream_own[...] = dot(turn[(nz - 1) * cap : nz * cap, :], x[:, :D], NN).astype(BF)


def experts(mine, theirs, gain, gate_up, down, turn, fill, mixed, width, cap):
    nz = len(mine)
    block, wide = mine[0].shape
    total = 2 * nz * block
    shapes = [
        jax.ShapeDtypeStruct((blocks * cap, D + mixed.shape[1]), BF)
        for blocks in [nz] + portions(nz)
    ]
    return pl.pallas_call(
        functools.partial(expert_kernel, nz, width),
        out_shape=shapes * 2 + [jax.ShapeDtypeStruct((cap, D), BF)],
        in_specs=[pl.BlockSpec(memory_space=pltpu.VMEM)] * (2 * nz + 6),
        out_specs=[pl.BlockSpec(memory_space=pltpu.VMEM)] * (2 * len(shapes) + 1),
        scratch_shapes=[
            pltpu.VMEM((total, wide), BF),
            pltpu.VMEM((total, D), BF),
            pltpu.VMEM((total, EFF), BF),
            pltpu.VMEM((total, D), BF),
        ],
        cost_estimate=pl.CostEstimate(
            flops=6 * total * D * EFF, bytes_accessed=6 * D * EFF, transcendentals=total * EFF
        ),
        compiler_params=pltpu.CompilerParams(vmem_limit_bytes=32 * MIB),
        name="experts",
    )(*mine, *theirs, gain, gate_up, down, turn, fill, mixed)


def mix_kernel(first, keep, near, far, *outs):
    cap = outs[0].shape[0]
    for i, out in enumerate(outs):
        here = slice((first + i) * cap, (first + i + 1) * cap)
        own = keep[here, :].astype(F32) + near[here, :].astype(F32)
        other = far[i * cap : (i + 1) * cap, :].astype(F32)
        out[:, :D] = (own[:, :D] + other[:, :D]).astype(BF)
        out[:, D:] = jnp.concatenate([own[:, D:], other[:, D:]], axis=1).astype(BF)


def mix(keep, near, far, cap, first):
    count = far.shape[0] // cap
    cols = keep.shape[1] - D
    return pl.pallas_call(
        functools.partial(mix_kernel, first),
        out_shape=[jax.ShapeDtypeStruct((cap, D + 2 * cols), BF)] * count,
        in_specs=[pl.BlockSpec(memory_space=pltpu.VMEM)] * 3,
        out_specs=[pl.BlockSpec(memory_space=pltpu.VMEM)] * count,
        cost_estimate=pl.CostEstimate(
            flops=3 * far.size, bytes_accessed=8 * far.size, transcendentals=0
        ),
        compiler_params=pltpu.CompilerParams(vmem_limit_bytes=16 * MIB),
        name="mix",
    )(keep, near, far)


def finish_kernel(nz, stream, *refs):
    pieces, (attn, out) = refs[:nz], refs[nz:]
    _, _, chip, _ = place()
    cols = (pieces[0].shape[1] - D) // 2
    total = stream[...].astype(F32)
    for kz in range(nz):
        total = total + pieces[kz][:, :D].astype(F32)
    out[...] = total.astype(BF)
    if cols % 128 == 0:
        for kz in range(nz):
            for ky in range(2):
                spot = pl.multiple_of((chip ^ (2 * kz + ky)) * cols, cols)
                attn[:, pl.ds(spot, cols)] = pieces[kz][:, D + ky * cols : D + (ky + 1) * cols]
    else:
        whole = jnp.zeros(attn.shape, F32)
        lane = lax.broadcasted_iota(jnp.int32, (cols, D), 1)
        line = lax.broadcasted_iota(jnp.int32, (cols, D), 0)
        for kz in range(nz):
            for ky in range(2):
                spot = (chip ^ (2 * kz + ky)) * cols
                put = (lane == line + spot).astype(F32).astype(BF)
                part = pieces[kz][:, D + ky * cols : D + (ky + 1) * cols]
                whole = whole + dot(part, put, NN)
        attn[...] = whole.astype(BF)


def finish(stream, pieces):
    shape = jax.ShapeDtypeStruct(stream.shape, BF)
    nz = len(pieces)
    return pl.pallas_call(
        functools.partial(finish_kernel, nz),
        out_shape=[shape, shape],
        in_specs=[pl.BlockSpec(memory_space=pltpu.VMEM)] * (nz + 1),
        out_specs=[pl.BlockSpec(memory_space=pltpu.VMEM)] * 2,
        cost_estimate=pl.CostEstimate(
            flops=nz * stream.size, bytes_accessed=4 * nz * stream.size, transcendentals=0
        ),
        compiler_params=pltpu.CompilerParams(vmem_limit_bytes=16 * MIB),
        name="finish",
    )(stream, *pieces)


def body(
    queries,
    keys,
    values,
    lengths,
    owner_counts,
    row_order,
    residual,
    out_weight,
    norm_gain,
    expert_ids,
    route_weights,
    gate_up,
    expert_down,
):
    width = lax.axis_size("ctx")
    chips, nz = width // 2, width // 4
    per = queries.shape[0]
    cap = residual.shape[0]
    order = row_order.reshape(1, -1)

    def along_z(terms):
        out = [terms[0]]
        for kz in range(1, nz):
            out.append(hop(terms[kz], 4 * kz, width))
        return out

    def by_distance(blocks):
        return [blocks[sequence(nz).index(kz)] for kz in range(nz)]

    def add(*terms):
        return small(total_kernel, terms[0].shape, *terms)

    near = hop(queries, 2, width)
    k_oth = hop(keys, 1, width)
    v_oth = hop(values, 1, width)
    q_own, k_own, v_own = fetch(queries, keys, values)
    column = small(pair_kernel, (2,) + queries.shape, q_own, near)
    pieces = along_z([column] * nz)
    w_oth = hop(out_weight, 1, width)
    res_own, home, fill, turn, w_own, gain = prepare(
        owner_counts.reshape(1, -1),
        order,
        expert_ids.T,
        route_weights.T,
        residual,
        out_weight,
        norm_gain.reshape(1, -1),
        per,
        width,
    )
    res_oth = hop(res_own, 1, width)

    near_a, near_b, far_a, far_b = attention(
        pieces, k_own, v_own, k_oth, v_oth, lengths, chips
    )
    far_a = hop(far_a, 2, width)
    far_b = hop(far_b, 2, width)
    first = fold(near_a, far_a)
    second = fold(near_b, far_b)
    blocks = along_z(by_distance(first + second))
    *parts, mixed = project(blocks, w_own, w_oth, res_own, res_oth, home)
    chunk = add(*along_z(parts))
    (up,) = fetch(gate_up)
    other = hop(chunk, 2, width)
    chunk = add(chunk, other)
    mine = along_z([chunk] * nz)
    theirs = [hop(x, 1, width) for x in mine]
    (down,) = fetch(expert_down)
    *halves, stream = experts(
        mine, theirs, gain, up, down, turn, fill, mixed, width, cap
    )
    count = len(portions(nz))
    keep, *keeps = halves[: count + 1]
    send, *sends = halves[count + 1 :]
    gots, fars, blocks = [], [], []
    for i in range(count):
        gots.append(hop(sends[i], 1, width))
    got = hop(send, 1, width)
    for i in range(count):
        term = add(keeps[i], gots[i])
        fars.append(hop(term, 2, width))
    for i in range(count):
        blocks += mix(keep, got, fars[i], cap, len(blocks))
    attn, layer_out = finish(stream, along_z(by_distance(blocks)))
    return (attn, layer_out)


def solution(mesh):
    placed = (
        P(("groups", "ctx"), None),
        P("groups", "ctx", None),
        P("groups", "ctx", None),
        P("groups"),
        P("groups"),
        P("groups"),
        P(("groups", "ctx"), None),
        P("ctx", None),
        P(),
        P(("groups", "ctx"), None),
        P(("groups", "ctx"), None),
        P("ctx", None, None),
        P("ctx", None, None),
    )

    return jax.shard_map(
        body,
        mesh=mesh,
        in_specs=placed,
        out_specs=(P(("groups", "ctx"), None), P(("groups", "ctx"), None)),
        check_vma=False,
    )
```

```python
import functools

import jax
import jax.numpy as jnp
from jax import lax
from jax.experimental import pallas as pl
from jax.experimental.pallas import tpu as pltpu
from jax.sharding import PartitionSpec as P


D = 2048
HQ = 16
KVH = 2
HD = 128
EFF = 768
TOPK = 8
STRETCH = 128
BF = jnp.bfloat16
F32 = jnp.float32
MIB = 1 << 20
LOG2E = 1.4426950408889634
STAT = 8


NT = (((1,), (1,)), ((), ()))
NN = (((1,), (0,)), ((), ()))


def dot(a, b, dims):
    return lax.dot_general(a, b, dims, preferred_element_type=F32)


def place():
    device = lax.axis_index("ctx")
    return device, device & 1, device >> 1, device >> 2


def hop(x, mask, width):
    return lax.ppermute(x, "ctx", [(i, i ^ mask) for i in range(width)])


def sequence(nz):
    return list(range(nz - 1, -1, -1))


def portions(nz):
    return [1, nz // 2 - 1, nz // 2]


def split3(x):
    hi = x.astype(BF)
    rest = x - hi.astype(F32)
    mid = rest.astype(BF)
    return hi, mid, (rest - mid.astype(F32)).astype(BF)


def row_ids(per, core, axis, shape):
    i = lax.broadcasted_iota(jnp.int32, shape, axis)
    return (i // per) * (2 * per) + core * per + i % per


def fetch_kernel(count, *refs):
    sems = refs[2 * count]
    copies = [
        pltpu.make_async_copy(refs[i], refs[count + i], sems.at[i]) for i in range(count)
    ]
    for copy in copies:
        copy.start()
    for copy in copies:
        copy.wait()


def in_hbm(x):
    return pltpu.with_memory_space_constraint(x, pltpu.HBM)


def fetch(*arrays):
    count = len(arrays)
    size = sum(a.size * a.dtype.itemsize for a in arrays)
    return pl.pallas_call(
        functools.partial(fetch_kernel, count),
        out_shape=[pltpu.VMEM(a.shape, a.dtype) for a in arrays],
        in_specs=[pl.BlockSpec(memory_space=pltpu.HBM)] * count,
        out_specs=[pl.BlockSpec(memory_space=pltpu.VMEM)] * count,
        scratch_shapes=[pltpu.SemaphoreType.DMA((count,))],
        cost_estimate=pl.CostEstimate(flops=0, bytes_accessed=2 * size, transcendentals=0),
        compiler_params=pltpu.CompilerParams(vmem_limit_bytes=16 * MIB),
        name="fetch",
    )(*[in_hbm(a) for a in arrays])


def prepare_kernel(per, width, *refs):
    (counts, order, ids, weights, residual, weight_in, gain_in) = refs[:7]
    (res, home, fill, turn, weight_out, gain_out) = refs[7:13]
    picks, table, own, sems = refs[13:]
    copies = [
        pltpu.make_async_copy(weight_in, weight_out, sems.at[0]),
        pltpu.make_async_copy(gain_in, gain_out, sems.at[1]),
    ]
    for copy in copies:
        copy.start()
    device, core, _, _ = place()
    cap, rows = residual.shape[0], order.shape[1]
    half = home.shape[0]
    slots = picks.shape[0]
    lane = lax.broadcasted_iota(jnp.int32, (width, width), 1)
    line = lax.broadcasted_iota(jnp.int32, (width, width), 0)
    many = counts[...].astype(F32)
    end = jnp.sum(jnp.where(lane <= line, many, 0.0), axis=1, keepdims=True)
    size = jnp.sum(jnp.where(lane == line, many, 0.0), axis=1, keepdims=True)
    p = lax.broadcasted_iota(jnp.int32, (width, rows), 1).astype(F32)
    past = (p >= end).astype(F32)
    owner = jnp.sum(past, axis=0, keepdims=True)
    start = jnp.sum(past * size, axis=0, keepdims=True)
    slot = owner * cap + p[:1] - start
    at = lax.broadcasted_iota(jnp.int32, (slots, rows), 0).astype(F32)
    picks[...] = (at == slot).astype(F32).astype(BF)
    seats = [
        (order[...] == row_ids(per, c, 0, (half, rows))).astype(F32).astype(BF)
        for c in range(2)
    ]
    mine = (order[...] == row_ids(per, core, 0, (half, rows))).astype(F32).astype(BF)
    own[...] = dot(picks[...], mine, NT).astype(BF)
    table[...] = dot(picks[...], jnp.concatenate(seats, axis=0), NT).astype(BF)
    for kc in range(2):
        for ky in range(2):
            for spot, kz in enumerate(sequence(width // 4)):
                there = device ^ (kc + 2 * ky + 4 * kz)
                there = pl.ds(pl.multiple_of(there * cap, cap), cap)
                to = (kc * 2 + ky) * (width // 4) + spot
                turn[to * cap : (to + 1) * cap, :] = table[there, :]
                fill[to * cap : (to + 1) * cap, :] = own[there, :]
    chip_picks = [
        picks[pl.ds(pl.multiple_of(o * cap, cap), cap), :] for o in (device, device ^ 1)
    ]
    home[...] = dot(mine, jnp.concatenate(chip_picks, axis=0), NT).astype(BF)
    lanes = res.shape[1] - D
    kind = lax.broadcasted_iota(jnp.int32, (lanes, cap), 0)
    norm = weights[...] / jnp.sum(weights[...], axis=0, keepdims=True)
    dense = jnp.zeros((lanes, cap), F32)
    for k in range(TOPK):
        dense = dense + jnp.where(ids[k : k + 1, :] == kind % width, norm[k : k + 1, :], 0.0)
    high = dense.astype(BF).astype(F32)
    low = jnp.where(kind < 2 * width, dense - high, 0.0)
    both = jnp.where(kind < width, high, low).astype(BF)
    i = lax.broadcasted_iota(jnp.int32, (cap, cap), 0)
    j = lax.broadcasted_iota(jnp.int32, (cap, cap), 1)
    res[:, :D] = residual[...]
    res[:, D:] = dot((i == j).astype(F32).astype(BF), both, NT).astype(BF)
    for copy in copies:
        copy.wait()


def prepare(counts, order, ids, weights, residual, out_weight, gain, per, width):
    cap, rows = residual.shape[0], order.shape[1]
    half = width // 2 * per
    lanes = -(-2 * width // 128) * 128
    slots = width * cap
    given = (counts, order, ids, weights, residual, out_weight, gain)
    return pl.pallas_call(
        functools.partial(prepare_kernel, per, width),
        out_shape=[
            jax.ShapeDtypeStruct((cap, D + lanes), BF),
            jax.ShapeDtypeStruct((half, 2 * cap), BF),
            jax.ShapeDtypeStruct((slots, half), BF),
            jax.ShapeDtypeStruct((slots, 2 * half), BF),
            pltpu.VMEM(out_weight.shape, out_weight.dtype),
            pltpu.VMEM(gain.shape, gain.dtype),
        ],
        in_specs=[pl.BlockSpec(memory_space=pltpu.VMEM)] * 5
        + [pl.BlockSpec(memory_space=pltpu.HBM)] * 2,
        out_specs=[pl.BlockSpec(memory_space=pltpu.VMEM)] * 6,
        scratch_shapes=[
            pltpu.VMEM((slots, rows), BF),
            pltpu.VMEM((slots, 2 * half), BF),
            pltpu.VMEM((slots, half), BF),
            pltpu.SemaphoreType.DMA((2,)),
        ],
        cost_estimate=pl.CostEstimate(
            flops=6 * slots * rows * half, bytes_accessed=8 * slots * half, transcendentals=0
        ),
        compiler_params=pltpu.CompilerParams(vmem_limit_bytes=12 * MIB),
        name="prepare",
    )(*[in_hbm(a) for a in given])


def total_kernel(*refs):
    terms, out = refs[:-1], refs[-1]
    out[...] = functools.reduce(lambda a, b: a + b, [t[...].astype(F32) for t in terms]).astype(BF)


def pair_kernel(first, second, out):
    out[0] = first[...]
    out[1] = second[...]


def small(kernel, shape, *terms):
    return pl.pallas_call(
        kernel,
        out_shape=jax.ShapeDtypeStruct(shape, BF),
        in_specs=[pl.BlockSpec(memory_space=pltpu.VMEM)] * len(terms),
        out_specs=pl.BlockSpec(memory_space=pltpu.VMEM),
        cost_estimate=pl.CostEstimate(
            flops=len(terms) * terms[0].size,
            bytes_accessed=2 * (len(terms) + 1) * terms[0].size,
            transcendentals=0,
        ),
        compiler_params=pltpu.CompilerParams(vmem_limit_bytes=16 * MIB),
    )(*terms)


def attention_kernel(nz, far, lengths, *refs):
    pieces, (k_own, v_own, k_oth, v_oth) = refs[:nz], refs[nz : nz + 4]
    *outs, rows, ready = refs[nz + 4 :]
    device, core, chip, z = place()
    per = pieces[0].shape[1]
    requests, span = k_own.shape[0], k_own.shape[1]
    count = rows.shape[0]
    seat = count // requests
    chips, depth = ready.shape[0], ready.shape[1] - STAT
    cols = HQ * HD // chips
    heads = max(1, cols // HD)
    group = HQ // KVH
    for kz in range(nz):
        both = pieces[kz][...].astype(F32)
        for ky in range(2):
            spot = (chip ^ (2 * kz + ky)) * per
            rows[pl.ds(pl.multiple_of(spot, per), per), :] = both[ky]
    wide = group * seat
    key = lax.broadcasted_iota(jnp.int32, (span, wide), 0)
    lane = lax.broadcasted_iota(jnp.int32, (1, wide), 1) % seat
    ahead = (lane // per) * (2 * per) + core * per + lane % per - STRETCH
    first_own, first_oth = device * span, (device ^ 1) * span
    for q in range(requests):
        last = lengths[q] + ahead
        see_own, see_oth = key <= last - first_own, key <= last - first_oth
        for near_head in range(KVH // 2):
            half = z // (nz // 2) ^ far
            v = half * (KVH // 2) + near_head
            kv = pl.ds(pl.multiple_of(v * HD, HD), HD)
            asked = jnp.concatenate(
                [
                    rows[
                        q * seat : (q + 1) * seat,
                        pl.ds(pl.multiple_of((v * group + e) * HD, HD), HD),
                    ]
                    for e in range(group)
                ],
                axis=0,
            ).astype(BF)
            s_own = dot(k_own[q, :, kv], asked, NT) * (HD ** (-0.5) * LOG2E)
            s_oth = dot(k_oth[q, :, kv], asked, NT) * (HD ** (-0.5) * LOG2E)
            s_own = jnp.where(see_own, s_own, -1e30)
            s_oth = jnp.where(see_oth, s_oth, -1e30)
            top = jnp.maximum(
                jnp.max(s_own, axis=0, keepdims=True), jnp.max(s_oth, axis=0, keepdims=True)
            )
            top = jnp.maximum(top, -1e29)
            w_own = jnp.exp2(s_own - top)
            w_oth = jnp.exp2(s_oth - top)
            total = jnp.sum(w_own, axis=0, keepdims=True) + jnp.sum(w_oth, axis=0, keepdims=True)
            mixed = dot(v_own[q, :, kv].T, w_own.astype(BF), NN) + dot(
                v_oth[q, :, kv].T, w_oth.astype(BF), NN
            )
            some = total > 0.0
            safe = jnp.where(some, total, 1.0)
            mixed = (mixed * (1.0 / safe)).astype(BF)
            lse = jnp.where(some, top * (1.0 / LOG2E) + jnp.log(safe), -1e30)
            stat = with_lse(lse)
            if heads == 2 and requests == 1:
                for g in range(group // 2):
                    dest = (v * (group // 2) + g) ^ chip
                    mine = slice(2 * g * seat, 2 * (g + 1) * seat)
                    ready[dest, :depth, :] = mixed[:, mine]
                    ready[dest, depth:, :] = stat[:, mine]
            else:
                for e in range(group):
                    mine = slice(e * seat, (e + 1) * seat)
                    head = v * group + e
                    lo = (e % heads) * count + q * seat
                    for part in range(HD // depth):
                        dest = ((head * HD + part * depth) // cols) ^ chip
                        some_rows = slice(part * depth, (part + 1) * depth)
                        ready[dest, :depth, lo : lo + seat] = mixed[some_rows, mine]
                        ready[dest, depth:, lo : lo + seat] = stat[:, mine]
    order = sequence(nz)
    outs = iter(outs)
    for ky in range(2):
        taken = 0 if far else nz // 2
        for blocks in portions(nz)[:2] if far else portions(nz)[2:]:
            out = next(outs)
            for i in range(blocks):
                out[i] = ready[2 * order[taken + i] + ky]
            taken = taken + blocks


def with_lse(lse):
    parts = [x.astype(F32) for x in split3(lse)]
    return jnp.concatenate(parts + [jnp.zeros((STAT - 3, lse.shape[1]), F32)], axis=0).astype(BF)


def attention(pieces, k_own, v_own, k_oth, v_oth, lengths, chips, far):
    nz = len(pieces)
    per = pieces[0].shape[1]
    count = chips * per
    cols = HQ * HD // chips
    heads = max(1, cols // HD)
    shape = (min(cols, HD) + STAT, heads * count)
    work = 2 * k_own.size * (HQ // KVH) * 2 * count
    parts = portions(nz)[:2] if far else portions(nz)[2:]
    return pl.pallas_call(
        functools.partial(attention_kernel, nz, far),
        out_shape=[jax.ShapeDtypeStruct((blocks,) + shape, BF) for blocks in parts] * 2,
        in_specs=[pl.BlockSpec(memory_space=pltpu.SMEM)]
        + [pl.BlockSpec(memory_space=pltpu.VMEM)] * (nz + 4),
        out_specs=[pl.BlockSpec(memory_space=pltpu.VMEM)] * (2 * len(parts)),
        scratch_shapes=[
            pltpu.VMEM((count, HQ * HD), F32),
            pltpu.VMEM((chips,) + shape, BF),
        ],
        cost_estimate=pl.CostEstimate(
            flops=work, bytes_accessed=8 * k_own.size, transcendentals=work // (4 * HD)
        ),
        compiler_params=pltpu.CompilerParams(vmem_limit_bytes=24 * MIB),
        name="attention",
    )(lengths, *pieces, k_own, v_own, k_oth, v_oth)


def merged(blocks):
    depth = blocks[0].shape[0] - STAT
    lse = [jnp.sum(x[depth:].astype(F32), axis=0, keepdims=True) for x in blocks]
    best = functools.reduce(jnp.maximum, lse)
    factor = [jnp.exp(x - best) for x in lse]
    denom = functools.reduce(lambda a, b: a + b, factor)
    mixed = functools.reduce(
        lambda a, b: a + b, [x[:depth].astype(F32) * f for x, f in zip(blocks, factor)]
    )
    return mixed * (1.0 / denom), best + jnp.log(denom)


def fold_kernel(near, far, *outs):
    depth = outs[0].shape[0] - STAT
    for i, out in enumerate(outs):
        mixed, lse = merged([near[i], far[i]])
        out[:depth, :] = mixed.astype(BF)
        out[depth:, :] = with_lse(lse)


def fold(near, far):
    count = near.shape[0]
    return pl.pallas_call(
        fold_kernel,
        out_shape=[jax.ShapeDtypeStruct(near.shape[1:], BF)] * count,
        in_specs=[pl.BlockSpec(memory_space=pltpu.VMEM)] * 2,
        out_specs=[pl.BlockSpec(memory_space=pltpu.VMEM)] * count,
        cost_estimate=pl.CostEstimate(
            flops=8 * near.size, bytes_accessed=8 * near.size, transcendentals=0
        ),
        compiler_params=pltpu.CompilerParams(vmem_limit_bytes=16 * MIB),
        name="fold",
    )(near, far)


def project_kernel(nz, *refs):
    blocks, (w_own, w_oth, res_own, res_oth, home) = refs[:nz], refs[nz : nz + 5]
    outs, attn, part = refs[nz + 5 : 2 * nz + 5], refs[2 * nz + 5], refs[2 * nz + 6]
    _, core, _, z = place()
    depth = blocks[0].shape[0] - STAT
    count = part.shape[0]
    heads = blocks[0].shape[1] // count
    mixed, _ = merged([b[...] for b in blocks])
    mixed = mixed.T.astype(BF)
    if heads == 2:
        first, second = mixed[:count], mixed[count:]
        attn[...] = jnp.concatenate([first, second], axis=1)
    else:
        first, second = mixed[:, : depth // 2], mixed[:, depth // 2 :]
        attn[...] = mixed
    low = (core == 0).astype(F32)
    first, second = first.astype(F32), second.astype(F32)
    own = (first * low + second * (1.0 - low)).astype(BF)
    oth = (second * low + first * (1.0 - low)).astype(BF)
    res = jnp.concatenate([res_own[...], res_oth[...]], axis=0)
    part[:, :D] = (
        dot(home[...], res[:, :D], NN) + dot(own, w_own[...], NN) + dot(oth, w_oth[...], NN)
    )
    part[:, D:] = dot(home[...], res[:, D:], NN)
    block = outs[0].shape[0]
    for kz in range(nz):
        spot = pl.multiple_of((z ^ kz) * block, block)
        outs[kz][...] = part[pl.ds(spot, block), :].astype(BF)


def project(blocks, w_own, w_oth, res_own, res_oth, home):
    nz = len(blocks)
    count = home.shape[0]
    cols = D // (2 * nz)
    wide = res_own.shape[1]
    return pl.pallas_call(
        functools.partial(project_kernel, nz),
        out_shape=[jax.ShapeDtypeStruct((count // nz, wide), BF)] * nz
        + [jax.ShapeDtypeStruct((count, cols), BF)],
        in_specs=[pl.BlockSpec(memory_space=pltpu.VMEM)] * (nz + 5),
        out_specs=[pl.BlockSpec(memory_space=pltpu.VMEM)] * (nz + 1),
        scratch_shapes=[pltpu.VMEM((count, wide), F32)],
        cost_estimate=pl.CostEstimate(
            flops=2 * count * cols * D, bytes_accessed=4 * cols * D, transcendentals=0
        ),
        compiler_params=pltpu.CompilerParams(vmem_limit_bytes=12 * MIB),
        name="project",
    )(*blocks, w_own, w_oth, res_own, res_oth, home)


def expert_kernel(nz, width, *refs):
    mine, theirs = refs[:nz], refs[nz : 2 * nz]
    (gain, gate_up, down, turn, fill, mixed) = refs[2 * nz : 2 * nz + 6]
    *outs, stream_own, x, normed, hidden, scaled = refs[2 * nz + 6 :]
    device, core, _, z = place()
    block = mine[0].shape[0]
    half = block * nz
    cap = stream_own.shape[0]
    for kz in range(nz):
        spot = (z ^ kz) * block
        x[pl.ds(pl.multiple_of(core * half + spot, block), block), :] = mine[kz][...]
        x[pl.ds(pl.multiple_of((1 - core) * half + spot, block), block), :] = theirs[kz][...]
    stream = x[:, :D].astype(F32)
    scale = lax.rsqrt(jnp.mean(stream * stream, axis=-1, keepdims=True) + 1e-06)
    normed[...] = (stream * scale * gain[...]).astype(BF)
    extra = x[:, D:].astype(F32)
    lane = lax.broadcasted_iota(jnp.int32, extra.shape, 1)
    pick = (lane == device) | (lane == device + width)
    weight = jnp.sum(jnp.where(pick, extra, 0.0), axis=-1, keepdims=True)
    tile = 256
    for lo in range(0, EFF, tile):
        g = dot(normed[...], gate_up[0, :, lo : lo + tile], NN)
        u = dot(normed[...], gate_up[0, :, EFF + lo : EFF + lo + tile], NN)
        hidden[:, lo : lo + tile] = (g / (1.0 + jnp.exp(-g)) * u).astype(BF)
    for lo in range(0, D, tile):
        y = dot(hidden[...], down[0, :, lo : lo + tile], NN).astype(BF)
        scaled[:, lo : lo + tile] = (y.astype(F32) * weight).astype(BF)
    done = 0
    for target in outs:
        some = slice(done, done + target.shape[0])
        target[:, :D] = dot(turn[some, :], scaled[...], NN).astype(BF)
        target[:, D:] = dot(fill[some, :], mixed[...], NN).astype(BF)
        done = done + target.shape[0]
    stream_own[...] = dot(turn[(nz - 1) * cap : nz * cap, :], x[:, :D], NN).astype(BF)


def experts(mine, theirs, gain, gate_up, down, turn, fill, mixed, width, cap):
    nz = len(mine)
    block, wide = mine[0].shape
    total = 2 * nz * block
    shapes = [
        jax.ShapeDtypeStruct((blocks * cap, D + mixed.shape[1]), BF)
        for blocks in [nz] + portions(nz)
    ]
    return pl.pallas_call(
        functools.partial(expert_kernel, nz, width),
        out_shape=shapes * 2 + [jax.ShapeDtypeStruct((cap, D), BF)],
        in_specs=[pl.BlockSpec(memory_space=pltpu.VMEM)] * (2 * nz + 6),
        out_specs=[pl.BlockSpec(memory_space=pltpu.VMEM)] * (2 * len(shapes) + 1),
        scratch_shapes=[
            pltpu.VMEM((total, wide), BF),
            pltpu.VMEM((total, D), BF),
            pltpu.VMEM((total, EFF), BF),
            pltpu.VMEM((total, D), BF),
        ],
        cost_estimate=pl.CostEstimate(
            flops=6 * total * D * EFF, bytes_accessed=6 * D * EFF, transcendentals=total * EFF
        ),
        compiler_params=pltpu.CompilerParams(vmem_limit_bytes=32 * MIB),
        name="experts",
    )(*mine, *theirs, gain, gate_up, down, turn, fill, mixed)


def mix_kernel(first, keep, near, far, *outs):
    cap = outs[0].shape[0]
    for i, out in enumerate(outs):
        here = slice((first + i) * cap, (first + i + 1) * cap)
        own = keep[here, :].astype(F32) + near[here, :].astype(F32)
        other = far[i * cap : (i + 1) * cap, :].astype(F32)
        out[:, :D] = (own[:, :D] + other[:, :D]).astype(BF)
        out[:, D:] = jnp.concatenate([own[:, D:], other[:, D:]], axis=1).astype(BF)


def mix(keep, near, far, cap, first):
    count = far.shape[0] // cap
    cols = keep.shape[1] - D
    return pl.pallas_call(
        functools.partial(mix_kernel, first),
        out_shape=[jax.ShapeDtypeStruct((cap, D + 2 * cols), BF)] * count,
        in_specs=[pl.BlockSpec(memory_space=pltpu.VMEM)] * 3,
        out_specs=[pl.BlockSpec(memory_space=pltpu.VMEM)] * count,
        cost_estimate=pl.CostEstimate(
            flops=3 * far.size, bytes_accessed=8 * far.size, transcendentals=0
        ),
        compiler_params=pltpu.CompilerParams(vmem_limit_bytes=16 * MIB),
        name="mix",
    )(keep, near, far)


def finish_kernel(nz, stream, *refs):
    pieces, (attn, out) = refs[:nz], refs[nz:]
    _, _, chip, _ = place()
    cols = (pieces[0].shape[1] - D) // 2
    total = stream[...].astype(F32)
    for kz in range(nz):
        total = total + pieces[kz][:, :D].astype(F32)
    out[...] = total.astype(BF)
    if cols % 128 == 0:
        for kz in range(nz):
            for ky in range(2):
                spot = pl.multiple_of((chip ^ (2 * kz + ky)) * cols, cols)
                attn[:, pl.ds(spot, cols)] = pieces[kz][:, D + ky * cols : D + (ky + 1) * cols]
    else:
        whole = jnp.zeros(attn.shape, F32)
        lane = lax.broadcasted_iota(jnp.int32, (cols, D), 1)
        line = lax.broadcasted_iota(jnp.int32, (cols, D), 0)
        for kz in range(nz):
            for ky in range(2):
                spot = (chip ^ (2 * kz + ky)) * cols
                put = (lane == line + spot).astype(F32).astype(BF)
                part = pieces[kz][:, D + ky * cols : D + (ky + 1) * cols]
                whole = whole + dot(part, put, NN)
        attn[...] = whole.astype(BF)


def finish(stream, pieces):
    shape = jax.ShapeDtypeStruct(stream.shape, BF)
    nz = len(pieces)
    return pl.pallas_call(
        functools.partial(finish_kernel, nz),
        out_shape=[shape, shape],
        in_specs=[pl.BlockSpec(memory_space=pltpu.VMEM)] * (nz + 1),
        out_specs=[pl.BlockSpec(memory_space=pltpu.VMEM)] * 2,
        cost_estimate=pl.CostEstimate(
            flops=nz * stream.size, bytes_accessed=4 * nz * stream.size, transcendentals=0
        ),
        compiler_params=pltpu.CompilerParams(vmem_limit_bytes=16 * MIB),
        name="finish",
    )(stream, *pieces)


def body(
    queries,
    keys,
    values,
    lengths,
    owner_counts,
    row_order,
    residual,
    out_weight,
    norm_gain,
    expert_ids,
    route_weights,
    gate_up,
    expert_down,
):
    width = lax.axis_size("ctx")
    chips, nz = width // 2, width // 4
    per = queries.shape[0]
    cap = residual.shape[0]
    order = row_order.reshape(1, -1)

    def along_z(terms):
        out = [terms[0]]
        for kz in range(1, nz):
            out.append(hop(terms[kz], 4 * kz, width))
        return out

    def by_distance(blocks):
        return [blocks[sequence(nz).index(kz)] for kz in range(nz)]

    def add(*terms):
        return small(total_kernel, terms[0].shape, *terms)

    near = hop(queries, 2, width)
    k_oth = hop(keys, 1, width)
    v_oth = hop(values, 1, width)
    q_own, k_own, v_own = fetch(queries, keys, values)
    column = small(pair_kernel, (2,) + queries.shape, q_own, near)
    pieces = along_z([column] * nz)
    w_oth = hop(out_weight, 1, width)
    res_own, home, fill, turn, w_own, gain = prepare(
        owner_counts.reshape(1, -1),
        order,
        expert_ids.T,
        route_weights.T,
        residual,
        out_weight,
        norm_gain.reshape(1, -1),
        per,
        width,
    )
    res_oth = hop(res_own, 1, width)

    asked = (pieces, k_own, v_own, k_oth, v_oth, lengths, chips)
    one, two, send_one, send_two = attention(*asked, 1)
    three, send_three = attention(*asked, 0)
    count = len(portions(nz))
    fars, blocks = [], []
    for send in (send_one, send_two, send_three):
        fars.append(hop(send, 2, width))
    for i, near in enumerate((one, two, three)):
        blocks += fold(near, fars[i])
    blocks = along_z(by_distance(blocks))
    *parts, mixed = project(blocks, w_own, w_oth, res_own, res_oth, home)
    chunk = add(*along_z(parts))
    (up,) = fetch(gate_up)
    other = hop(chunk, 2, width)
    chunk = add(chunk, other)
    mine = along_z([chunk] * nz)
    theirs = [hop(x, 1, width) for x in mine]
    (down,) = fetch(expert_down)
    *halves, stream = experts(
        mine, theirs, gain, up, down, turn, fill, mixed, width, cap
    )
    keep, *keeps = halves[: count + 1]
    send, *sends = halves[count + 1 :]
    gots, fars, blocks = [], [], []
    for i in range(count):
        gots.append(hop(sends[i], 1, width))
    got = hop(send, 1, width)
    for i in range(count):
        term = add(keeps[i], gots[i])
        fars.append(hop(term, 2, width))
    for i in range(count):
        blocks += mix(keep, got, fars[i], cap, len(blocks))
    attn, layer_out = finish(stream, along_z(by_distance(blocks)))
    return (attn, layer_out)


def solution(mesh):
    placed = (
        P(("groups", "ctx"), None),
        P("groups", "ctx", None),
        P("groups", "ctx", None),
        P("groups"),
        P("groups"),
        P("groups"),
        P(("groups", "ctx"), None),
        P("ctx", None),
        P(),
        P(("groups", "ctx"), None),
        P(("groups", "ctx"), None),
        P("ctx", None, None),
        P("ctx", None, None),
    )

    return jax.shard_map(
        body,
        mesh=mesh,
        in_specs=placed,
        out_specs=(P(("groups", "ctx"), None), P(("groups", "ctx"), None)),
        check_vma=False,
    )
```

```python
import functools

import jax
import jax.numpy as jnp
from jax import lax
from jax.experimental import pallas as pl
from jax.experimental.pallas import tpu as pltpu
from jax.sharding import PartitionSpec as P


D = 2048
HQ = 16
KVH = 2
HD = 128
EFF = 768
TOPK = 8
STRETCH = 128
BF = jnp.bfloat16
F32 = jnp.float32
MIB = 1 << 20
LOG2E = 1.4426950408889634
STAT = 8


NT = (((1,), (1,)), ((), ()))
NN = (((1,), (0,)), ((), ()))


def dot(a, b, dims):
    return lax.dot_general(a, b, dims, preferred_element_type=F32)


def place():
    device = lax.axis_index("ctx")
    return device, device & 1, device >> 1, device >> 2


def hop(x, mask, width):
    return lax.ppermute(x, "ctx", [(i, i ^ mask) for i in range(width)])


def sequence(nz):
    return list(range(nz - 1, -1, -1))


def portions(nz):
    return [1, nz // 2 - 1, nz // 2]


def split3(x):
    hi = x.astype(BF)
    rest = x - hi.astype(F32)
    mid = rest.astype(BF)
    return hi, mid, (rest - mid.astype(F32)).astype(BF)


def row_ids(per, core, axis, shape):
    i = lax.broadcasted_iota(jnp.int32, shape, axis)
    return (i // per) * (2 * per) + core * per + i % per


def fetch_kernel(count, *refs):
    sems = refs[2 * count]
    copies = [
        pltpu.make_async_copy(refs[i], refs[count + i], sems.at[i]) for i in range(count)
    ]
    for copy in copies:
        copy.start()
    for copy in copies:
        copy.wait()


def in_hbm(x):
    return pltpu.with_memory_space_constraint(x, pltpu.HBM)


def fetch(*arrays):
    count = len(arrays)
    size = sum(a.size * a.dtype.itemsize for a in arrays)
    return pl.pallas_call(
        functools.partial(fetch_kernel, count),
        out_shape=[pltpu.VMEM(a.shape, a.dtype) for a in arrays],
        in_specs=[pl.BlockSpec(memory_space=pltpu.HBM)] * count,
        out_specs=[pl.BlockSpec(memory_space=pltpu.VMEM)] * count,
        scratch_shapes=[pltpu.SemaphoreType.DMA((count,))],
        cost_estimate=pl.CostEstimate(flops=0, bytes_accessed=2 * size, transcendentals=0),
        compiler_params=pltpu.CompilerParams(vmem_limit_bytes=16 * MIB),
        name="fetch",
    )(*[in_hbm(a) for a in arrays])


def prepare_kernel(per, width, *refs):
    (counts, order, ids, weights, residual, weight_in, gain_in) = refs[:7]
    (res, home, fill, turn, weight_out, gain_out) = refs[7:13]
    picks, table, own, sems = refs[13:]
    copies = [
        pltpu.make_async_copy(weight_in, weight_out, sems.at[0]),
        pltpu.make_async_copy(gain_in, gain_out, sems.at[1]),
    ]
    for copy in copies:
        copy.start()
    device, core, _, _ = place()
    cap, rows = residual.shape[0], order.shape[1]
    half = home.shape[0]
    slots = picks.shape[0]
    lane = lax.broadcasted_iota(jnp.int32, (width, width), 1)
    line = lax.broadcasted_iota(jnp.int32, (width, width), 0)
    many = counts[...].astype(F32)
    end = jnp.sum(jnp.where(lane <= line, many, 0.0), axis=1, keepdims=True)
    size = jnp.sum(jnp.where(lane == line, many, 0.0), axis=1, keepdims=True)
    p = lax.broadcasted_iota(jnp.int32, (width, rows), 1).astype(F32)
    past = (p >= end).astype(F32)
    owner = jnp.sum(past, axis=0, keepdims=True)
    start = jnp.sum(past * size, axis=0, keepdims=True)
    slot = owner * cap + p[:1] - start
    at = lax.broadcasted_iota(jnp.int32, (slots, rows), 0).astype(F32)
    picks[...] = (at == slot).astype(F32).astype(BF)
    seats = [
        (order[...] == row_ids(per, c, 0, (half, rows))).astype(F32).astype(BF)
        for c in range(2)
    ]
    mine = (order[...] == row_ids(per, core, 0, (half, rows))).astype(F32).astype(BF)
    own[...] = dot(picks[...], mine, NT).astype(BF)
    table[...] = dot(picks[...], jnp.concatenate(seats, axis=0), NT).astype(BF)
    for kc in range(2):
        for ky in range(2):
            for spot, kz in enumerate(sequence(width // 4)):
                there = device ^ (kc + 2 * ky + 4 * kz)
                there = pl.ds(pl.multiple_of(there * cap, cap), cap)
                to = (kc * 2 + ky) * (width // 4) + spot
                turn[to * cap : (to + 1) * cap, :] = table[there, :]
                fill[to * cap : (to + 1) * cap, :] = own[there, :]
    chip_picks = [
        picks[pl.ds(pl.multiple_of(o * cap, cap), cap), :] for o in (device, device ^ 1)
    ]
    home[...] = dot(mine, jnp.concatenate(chip_picks, axis=0), NT).astype(BF)
    lanes = res.shape[1] - D
    kind = lax.broadcasted_iota(jnp.int32, (lanes, cap), 0)
    norm = weights[...] / jnp.sum(weights[...], axis=0, keepdims=True)
    dense = jnp.zeros((lanes, cap), F32)
    for k in range(TOPK):
        dense = dense + jnp.where(ids[k : k + 1, :] == kind % width, norm[k : k + 1, :], 0.0)
    high = dense.astype(BF).astype(F32)
    low = jnp.where(kind < 2 * width, dense - high, 0.0)
    both = jnp.where(kind < width, high, low).astype(BF)
    i = lax.broadcasted_iota(jnp.int32, (cap, cap), 0)
    j = lax.broadcasted_iota(jnp.int32, (cap, cap), 1)
    res[:, :D] = residual[...]
    res[:, D:] = dot((i == j).astype(F32).astype(BF), both, NT).astype(BF)
    for copy in copies:
        copy.wait()


def prepare(counts, order, ids, weights, residual, out_weight, gain, per, width):
    cap, rows = residual.shape[0], order.shape[1]
    half = width // 2 * per
    lanes = -(-2 * width // 128) * 128
    slots = width * cap
    given = (counts, order, ids, weights, residual, out_weight, gain)
    return pl.pallas_call(
        functools.partial(prepare_kernel, per, width),
        out_shape=[
            jax.ShapeDtypeStruct((cap, D + lanes), BF),
            jax.ShapeDtypeStruct((half, 2 * cap), BF),
            jax.ShapeDtypeStruct((slots, half), BF),
            jax.ShapeDtypeStruct((slots, 2 * half), BF),
            pltpu.VMEM(out_weight.shape, out_weight.dtype),
            pltpu.VMEM(gain.shape, gain.dtype),
        ],
        in_specs=[pl.BlockSpec(memory_space=pltpu.VMEM)] * 5
        + [pl.BlockSpec(memory_space=pltpu.HBM)] * 2,
        out_specs=[pl.BlockSpec(memory_space=pltpu.VMEM)] * 6,
        scratch_shapes=[
            pltpu.VMEM((slots, rows), BF),
            pltpu.VMEM((slots, 2 * half), BF),
            pltpu.VMEM((slots, half), BF),
            pltpu.SemaphoreType.DMA((2,)),
        ],
        cost_estimate=pl.CostEstimate(
            flops=6 * slots * rows * half, bytes_accessed=8 * slots * half, transcendentals=0
        ),
        compiler_params=pltpu.CompilerParams(vmem_limit_bytes=12 * MIB),
        name="prepare",
    )(*[in_hbm(a) for a in given])


def total_kernel(*refs):
    terms, out = refs[:-1], refs[-1]
    out[...] = functools.reduce(lambda a, b: a + b, [t[...].astype(F32) for t in terms]).astype(BF)


def pair_kernel(first, second, out):
    out[0] = first[...]
    out[1] = second[...]


def small(kernel, shape, *terms):
    return pl.pallas_call(
        kernel,
        out_shape=jax.ShapeDtypeStruct(shape, BF),
        in_specs=[pl.BlockSpec(memory_space=pltpu.VMEM)] * len(terms),
        out_specs=pl.BlockSpec(memory_space=pltpu.VMEM),
        cost_estimate=pl.CostEstimate(
            flops=len(terms) * terms[0].size,
            bytes_accessed=2 * (len(terms) + 1) * terms[0].size,
            transcendentals=0,
        ),
        compiler_params=pltpu.CompilerParams(vmem_limit_bytes=16 * MIB),
    )(*terms)


def attention_kernel(nz, far, lengths, *refs):
    pieces, (k_own, v_own, k_oth, v_oth) = refs[:nz], refs[nz : nz + 4]
    *outs, rows, ready = refs[nz + 4 :]
    device, core, chip, z = place()
    per = pieces[0].shape[1]
    requests, span = k_own.shape[0], k_own.shape[1]
    count = rows.shape[0]
    seat = count // requests
    chips, depth = ready.shape[0], ready.shape[1] - STAT
    cols = HQ * HD // chips
    heads = max(1, cols // HD)
    group = HQ // KVH
    for kz in range(nz):
        both = pieces[kz][...].astype(F32)
        for ky in range(2):
            spot = (chip ^ (2 * kz + ky)) * per
            rows[pl.ds(pl.multiple_of(spot, per), per), :] = both[ky]
    wide = group * seat
    key = lax.broadcasted_iota(jnp.int32, (span, wide), 0)
    lane = lax.broadcasted_iota(jnp.int32, (1, wide), 1) % seat
    ahead = (lane // per) * (2 * per) + core * per + lane % per - STRETCH
    first_own, first_oth = device * span, (device ^ 1) * span
    for q in range(requests):
        last = lengths[q] + ahead
        see_own, see_oth = key <= last - first_own, key <= last - first_oth
        for near_head in range(KVH // 2):
            half = z // (nz // 2) ^ far
            v = half * (KVH // 2) + near_head
            kv = pl.ds(pl.multiple_of(v * HD, HD), HD)
            asked = jnp.concatenate(
                [
                    rows[
                        q * seat : (q + 1) * seat,
                        pl.ds(pl.multiple_of((v * group + e) * HD, HD), HD),
                    ]
                    for e in range(group)
                ],
                axis=0,
            ).astype(BF)
            s_own = dot(k_own[q, :, kv], asked, NT) * (HD ** (-0.5) * LOG2E)
            s_oth = dot(k_oth[q, :, kv], asked, NT) * (HD ** (-0.5) * LOG2E)
            s_own = jnp.where(see_own, s_own, -1e30)
            s_oth = jnp.where(see_oth, s_oth, -1e30)
            top = jnp.maximum(
                jnp.max(s_own, axis=0, keepdims=True), jnp.max(s_oth, axis=0, keepdims=True)
            )
            top = jnp.maximum(top, -1e29)
            w_own = jnp.exp2(s_own - top)
            w_oth = jnp.exp2(s_oth - top)
            total = jnp.sum(w_own, axis=0, keepdims=True) + jnp.sum(w_oth, axis=0, keepdims=True)
            mixed = dot(v_own[q, :, kv].T, w_own.astype(BF), NN) + dot(
                v_oth[q, :, kv].T, w_oth.astype(BF), NN
            )
            some = total > 0.0
            safe = jnp.where(some, total, 1.0)
            mixed = (mixed * (1.0 / safe)).astype(BF)
            lse = jnp.where(some, top * (1.0 / LOG2E) + jnp.log(safe), -1e30)
            stat = with_lse(lse)
            if heads == 2 and requests == 1:
                for g in range(group // 2):
                    dest = (v * (group // 2) + g) ^ chip
                    mine = slice(2 * g * seat, 2 * (g + 1) * seat)
                    ready[dest, :depth, :] = mixed[:, mine]
                    ready[dest, depth:, :] = stat[:, mine]
            else:
                for e in range(group):
                    mine = slice(e * seat, (e + 1) * seat)
                    head = v * group + e
                    lo = (e % heads) * count + q * seat
                    for part in range(HD // depth):
                        dest = ((head * HD + part * depth) // cols) ^ chip
                        some_rows = slice(part * depth, (part + 1) * depth)
                        ready[dest, :depth, lo : lo + seat] = mixed[some_rows, mine]
                        ready[dest, depth:, lo : lo + seat] = stat[:, mine]
    order = sequence(nz)
    outs = iter(outs)
    for ky in range(2):
        taken = 0 if far else nz // 2
        for blocks in portions(nz)[:2] if far else portions(nz)[2:]:
            out = next(outs)
            for i in range(blocks):
                out[i] = ready[2 * order[taken + i] + ky]
            taken = taken + blocks


def with_lse(lse):
    parts = [x.astype(F32) for x in split3(lse)]
    return jnp.concatenate(parts + [jnp.zeros((STAT - 3, lse.shape[1]), F32)], axis=0).astype(BF)


def attention(pieces, k_own, v_own, k_oth, v_oth, lengths, chips, far):
    nz = len(pieces)
    per = pieces[0].shape[1]
    count = chips * per
    cols = HQ * HD // chips
    heads = max(1, cols // HD)
    shape = (min(cols, HD) + STAT, heads * count)
    work = 2 * k_own.size * (HQ // KVH) * 2 * count
    parts = portions(nz)[:2] if far else portions(nz)[2:]
    return pl.pallas_call(
        functools.partial(attention_kernel, nz, far),
        out_shape=[jax.ShapeDtypeStruct((blocks,) + shape, BF) for blocks in parts] * 2,
        in_specs=[pl.BlockSpec(memory_space=pltpu.SMEM)]
        + [pl.BlockSpec(memory_space=pltpu.VMEM)] * (nz + 4),
        out_specs=[pl.BlockSpec(memory_space=pltpu.VMEM)] * (2 * len(parts)),
        scratch_shapes=[
            pltpu.VMEM((count, HQ * HD), F32),
            pltpu.VMEM((chips,) + shape, BF),
        ],
        cost_estimate=pl.CostEstimate(
            flops=work, bytes_accessed=8 * k_own.size, transcendentals=work // (4 * HD)
        ),
        compiler_params=pltpu.CompilerParams(vmem_limit_bytes=24 * MIB),
        name="attention",
    )(lengths, *pieces, k_own, v_own, k_oth, v_oth)


def merged(blocks):
    depth = blocks[0].shape[0] - STAT
    lse = [jnp.sum(x[depth:].astype(F32), axis=0, keepdims=True) for x in blocks]
    best = functools.reduce(jnp.maximum, lse)
    factor = [jnp.exp(x - best) for x in lse]
    denom = functools.reduce(lambda a, b: a + b, factor)
    mixed = functools.reduce(
        lambda a, b: a + b, [x[:depth].astype(F32) * f for x, f in zip(blocks, factor)]
    )
    return mixed * (1.0 / denom), best + jnp.log(denom)


def fold_kernel(near, far, *outs):
    depth = outs[0].shape[0] - STAT
    for i, out in enumerate(outs):
        mixed, lse = merged([near[i], far[i]])
        out[:depth, :] = mixed.astype(BF)
        out[depth:, :] = with_lse(lse)


def fold(near, far):
    count = near.shape[0]
    return pl.pallas_call(
        fold_kernel,
        out_shape=[jax.ShapeDtypeStruct(near.shape[1:], BF)] * count,
        in_specs=[pl.BlockSpec(memory_space=pltpu.VMEM)] * 2,
        out_specs=[pl.BlockSpec(memory_space=pltpu.VMEM)] * count,
        cost_estimate=pl.CostEstimate(
            flops=8 * near.size, bytes_accessed=8 * near.size, transcendentals=0
        ),
        compiler_params=pltpu.CompilerParams(vmem_limit_bytes=16 * MIB),
        name="fold",
    )(near, far)


def project_kernel(nz, *refs):
    blocks, (w_own, w_oth, res_own, res_oth, home) = refs[:nz], refs[nz : nz + 5]
    outs, attn, part = refs[nz + 5 : 2 * nz + 5], refs[2 * nz + 5], refs[2 * nz + 6]
    _, core, _, z = place()
    depth = blocks[0].shape[0] - STAT
    count = part.shape[0]
    heads = blocks[0].shape[1] // count
    mixed, _ = merged([b[...] for b in blocks])
    mixed = mixed.T.astype(BF)
    if heads == 2:
        first, second = mixed[:count], mixed[count:]
        attn[...] = jnp.concatenate([first, second], axis=1)
    else:
        first, second = mixed[:, : depth // 2], mixed[:, depth // 2 :]
        attn[...] = mixed
    low = (core == 0).astype(F32)
    first, second = first.astype(F32), second.astype(F32)
    own = (first * low + second * (1.0 - low)).astype(BF)
    oth = (second * low + first * (1.0 - low)).astype(BF)
    res = jnp.concatenate([res_own[...], res_oth[...]], axis=0)
    part[:, :D] = (
        dot(home[...], res[:, :D], NN) + dot(own, w_own[...], NN) + dot(oth, w_oth[...], NN)
    )
    part[:, D:] = dot(home[...], res[:, D:], NN)
    block = outs[0].shape[0]
    for kz in range(nz):
        spot = pl.multiple_of((z ^ kz) * block, block)
        outs[kz][...] = part[pl.ds(spot, block), :].astype(BF)


def project(blocks, w_own, w_oth, res_own, res_oth, home):
    nz = len(blocks)
    count = home.shape[0]
    cols = D // (2 * nz)
    wide = res_own.shape[1]
    return pl.pallas_call(
        functools.partial(project_kernel, nz),
        out_shape=[jax.ShapeDtypeStruct((count // nz, wide), BF)] * nz
        + [jax.ShapeDtypeStruct((count, cols), BF)],
        in_specs=[pl.BlockSpec(memory_space=pltpu.VMEM)] * (nz + 5),
        out_specs=[pl.BlockSpec(memory_space=pltpu.VMEM)] * (nz + 1),
        scratch_shapes=[pltpu.VMEM((count, wide), F32)],
        cost_estimate=pl.CostEstimate(
            flops=2 * count * cols * D, bytes_accessed=4 * cols * D, transcendentals=0
        ),
        compiler_params=pltpu.CompilerParams(vmem_limit_bytes=12 * MIB),
        name="project",
    )(*blocks, w_own, w_oth, res_own, res_oth, home)


def expert_kernel(nz, width, *refs):
    mine, theirs = refs[:nz], refs[nz : 2 * nz]
    (gain, gate_up, down, turn, fill, mixed) = refs[2 * nz : 2 * nz + 6]
    *outs, scaled, x, normed, hidden = refs[2 * nz + 6 :]
    device, core, _, z = place()
    block = mine[0].shape[0]
    half = block * nz
    cap = fill.shape[0] // width
    for kz in range(nz):
        spot = (z ^ kz) * block
        x[pl.ds(pl.multiple_of(core * half + spot, block), block), :] = mine[kz][...]
        x[pl.ds(pl.multiple_of((1 - core) * half + spot, block), block), :] = theirs[kz][...]
    stream = x[:, :D].astype(F32)
    scale = lax.rsqrt(jnp.mean(stream * stream, axis=-1, keepdims=True) + 1e-06)
    normed[...] = (stream * scale * gain[...]).astype(BF)
    extra = x[:, D:].astype(F32)
    lane = lax.broadcasted_iota(jnp.int32, extra.shape, 1)
    pick = (lane == device) | (lane == device + width)
    weight = jnp.sum(jnp.where(pick, extra, 0.0), axis=-1, keepdims=True)
    tile = 256
    for lo in range(0, EFF, tile):
        g = dot(normed[...], gate_up[0, :, lo : lo + tile], NN)
        u = dot(normed[...], gate_up[0, :, EFF + lo : EFF + lo + tile], NN)
        hidden[:, lo : lo + tile] = (g / (1.0 + jnp.exp(-g)) * u).astype(BF)
    for lo in range(0, D, tile):
        y = dot(hidden[...], down[0, :, lo : lo + tile], NN).astype(BF)
        scaled[:, lo : lo + tile] = (y.astype(F32) * weight).astype(BF)
    done = nz * cap
    for target in outs:
        some = slice(done, done + target.shape[0])
        target[:, :D] = dot(turn[some, :], scaled[...], NN).astype(BF)
        target[:, D:] = dot(fill[some, :], mixed[...], NN).astype(BF)
        done = done + target.shape[0]


def stay_kernel(scaled, x, turn, fill, mixed, keep, stream_own):
    cap = stream_own.shape[0]
    size = keep.shape[0]
    keep[:, :D] = dot(turn[:size, :], scaled[...], NN).astype(BF)
    keep[:, D:] = dot(fill[:size, :], mixed[...], NN).astype(BF)
    stream_own[...] = dot(turn[size - cap : size, :], x[:, :D], NN).astype(BF)


def stay(scaled, x, turn, fill, mixed, cap):
    size = turn.shape[0] // 4
    return pl.pallas_call(
        stay_kernel,
        out_shape=[
            jax.ShapeDtypeStruct((size, D + mixed.shape[1]), BF),
            jax.ShapeDtypeStruct((cap, D), BF),
        ],
        in_specs=[pl.BlockSpec(memory_space=pltpu.VMEM)] * 5,
        out_specs=[pl.BlockSpec(memory_space=pltpu.VMEM)] * 2,
        cost_estimate=pl.CostEstimate(
            flops=2 * size * scaled.size, bytes_accessed=6 * scaled.size, transcendentals=0
        ),
        compiler_params=pltpu.CompilerParams(vmem_limit_bytes=16 * MIB),
        name="stay",
    )(scaled, x, turn, fill, mixed)


def experts(mine, theirs, gain, gate_up, down, turn, fill, mixed, width, cap):
    nz = len(mine)
    block, wide = mine[0].shape
    total = 2 * nz * block
    shapes = [
        jax.ShapeDtypeStruct((blocks * cap, D + mixed.shape[1]), BF)
        for blocks in [nz] + portions(nz)
    ]
    return pl.pallas_call(
        functools.partial(expert_kernel, nz, width),
        out_shape=shapes[1:]
        + shapes
        + [jax.ShapeDtypeStruct((total, D), BF), jax.ShapeDtypeStruct((total, wide), BF)],
        in_specs=[pl.BlockSpec(memory_space=pltpu.VMEM)] * (2 * nz + 6),
        out_specs=[pl.BlockSpec(memory_space=pltpu.VMEM)] * (2 * len(shapes) + 1),
        scratch_shapes=[pltpu.VMEM((total, D), BF), pltpu.VMEM((total, EFF), BF)],
        cost_estimate=pl.CostEstimate(
            flops=6 * total * D * EFF, bytes_accessed=6 * D * EFF, transcendentals=total * EFF
        ),
        compiler_params=pltpu.CompilerParams(vmem_limit_bytes=32 * MIB),
        name="experts",
    )(*mine, *theirs, gain, gate_up, down, turn, fill, mixed)


def mix_kernel(first, keep, near, far, *outs):
    cap = outs[0].shape[0]
    for i, out in enumerate(outs):
        here = slice((first + i) * cap, (first + i + 1) * cap)
        own = keep[here, :].astype(F32) + near[here, :].astype(F32)
        other = far[i * cap : (i + 1) * cap, :].astype(F32)
        out[:, :D] = (own[:, :D] + other[:, :D]).astype(BF)
        out[:, D:] = jnp.concatenate([own[:, D:], other[:, D:]], axis=1).astype(BF)


def mix(keep, near, far, cap, first):
    count = far.shape[0] // cap
    cols = keep.shape[1] - D
    return pl.pallas_call(
        functools.partial(mix_kernel, first),
        out_shape=[jax.ShapeDtypeStruct((cap, D + 2 * cols), BF)] * count,
        in_specs=[pl.BlockSpec(memory_space=pltpu.VMEM)] * 3,
        out_specs=[pl.BlockSpec(memory_space=pltpu.VMEM)] * count,
        cost_estimate=pl.CostEstimate(
            flops=3 * far.size, bytes_accessed=8 * far.size, transcendentals=0
        ),
        compiler_params=pltpu.CompilerParams(vmem_limit_bytes=16 * MIB),
        name="mix",
    )(keep, near, far)


def finish_kernel(nz, stream, *refs):
    pieces, (attn, out) = refs[:nz], refs[nz:]
    _, _, chip, _ = place()
    cols = (pieces[0].shape[1] - D) // 2
    total = stream[...].astype(F32)
    for kz in range(nz):
        total = total + pieces[kz][:, :D].astype(F32)
    out[...] = total.astype(BF)
    if cols % 128 == 0:
        for kz in range(nz):
            for ky in range(2):
                spot = pl.multiple_of((chip ^ (2 * kz + ky)) * cols, cols)
                attn[:, pl.ds(spot, cols)] = pieces[kz][:, D + ky * cols : D + (ky + 1) * cols]
    else:
        whole = jnp.zeros(attn.shape, F32)
        lane = lax.broadcasted_iota(jnp.int32, (cols, D), 1)
        line = lax.broadcasted_iota(jnp.int32, (cols, D), 0)
        for kz in range(nz):
            for ky in range(2):
                spot = (chip ^ (2 * kz + ky)) * cols
                put = (lane == line + spot).astype(F32).astype(BF)
                part = pieces[kz][:, D + ky * cols : D + (ky + 1) * cols]
                whole = whole + dot(part, put, NN)
        attn[...] = whole.astype(BF)


def finish(stream, pieces):
    shape = jax.ShapeDtypeStruct(stream.shape, BF)
    nz = len(pieces)
    return pl.pallas_call(
        functools.partial(finish_kernel, nz),
        out_shape=[shape, shape],
        in_specs=[pl.BlockSpec(memory_space=pltpu.VMEM)] * (nz + 1),
        out_specs=[pl.BlockSpec(memory_space=pltpu.VMEM)] * 2,
        cost_estimate=pl.CostEstimate(
            flops=nz * stream.size, bytes_accessed=4 * nz * stream.size, transcendentals=0
        ),
        compiler_params=pltpu.CompilerParams(vmem_limit_bytes=16 * MIB),
        name="finish",
    )(stream, *pieces)


def body(
    queries,
    keys,
    values,
    lengths,
    owner_counts,
    row_order,
    residual,
    out_weight,
    norm_gain,
    expert_ids,
    route_weights,
    gate_up,
    expert_down,
):
    width = lax.axis_size("ctx")
    chips, nz = width // 2, width // 4
    per = queries.shape[0]
    cap = residual.shape[0]
    order = row_order.reshape(1, -1)

    def along_z(terms):
        out = [terms[0]]
        for kz in range(1, nz):
            out.append(hop(terms[kz], 4 * kz, width))
        return out

    def by_distance(blocks):
        return [blocks[sequence(nz).index(kz)] for kz in range(nz)]

    def add(*terms):
        return small(total_kernel, terms[0].shape, *terms)

    near = hop(queries, 2, width)
    k_oth = hop(keys, 1, width)
    v_oth = hop(values, 1, width)
    q_own, k_own, v_own = fetch(queries, keys, values)
    column = small(pair_kernel, (2,) + queries.shape, q_own, near)
    pieces = along_z([column] * nz)
    w_oth = hop(out_weight, 1, width)
    res_own, home, fill, turn, w_own, gain = prepare(
        owner_counts.reshape(1, -1),
        order,
        expert_ids.T,
        route_weights.T,
        residual,
        out_weight,
        norm_gain.reshape(1, -1),
        per,
        width,
    )
    res_oth = hop(res_own, 1, width)

    asked = (pieces, k_own, v_own, k_oth, v_oth, lengths, chips)
    one, two, send_one, send_two = attention(*asked, 1)
    three, send_three = attention(*asked, 0)
    count = len(portions(nz))
    fars, blocks = [], []
    for send in (send_one, send_two, send_three):
        fars.append(hop(send, 2, width))
    for i, near in enumerate((one, two, three)):
        blocks += fold(near, fars[i])
    blocks = along_z(by_distance(blocks))
    *parts, mixed = project(blocks, w_own, w_oth, res_own, res_oth, home)
    chunk = add(*along_z(parts))
    (up,) = fetch(gate_up)
    other = hop(chunk, 2, width)
    chunk = add(chunk, other)
    mine = along_z([chunk] * nz)
    theirs = [hop(x, 1, width) for x in mine]
    (down,) = fetch(expert_down)
    *halves, scaled, rows = experts(
        mine, theirs, gain, up, down, turn, fill, mixed, width, cap
    )
    keeps, (send, *sends) = halves[:count], halves[count:]
    keep, stream = stay(scaled, rows, turn, fill, mixed, cap)
    gots, fars, blocks = [], [], []
    for i in range(count):
        gots.append(hop(sends[i], 1, width))
    got = hop(send, 1, width)
    for i in range(count):
        term = add(keeps[i], gots[i])
        fars.append(hop(term, 2, width))
    for i in range(count):
        blocks += mix(keep, got, fars[i], cap, len(blocks))
    attn, layer_out = finish(stream, along_z(by_distance(blocks)))
    return (attn, layer_out)


def solution(mesh):
    placed = (
        P(("groups", "ctx"), None),
        P("groups", "ctx", None),
        P("groups", "ctx", None),
        P("groups"),
        P("groups"),
        P("groups"),
        P(("groups", "ctx"), None),
        P("ctx", None),
        P(),
        P(("groups", "ctx"), None),
        P(("groups", "ctx"), None),
        P("ctx", None, None),
        P("ctx", None, None),
    )

    return jax.shard_map(
        body,
        mesh=mesh,
        in_specs=placed,
        out_specs=(P(("groups", "ctx"), None), P(("groups", "ctx"), None)),
        check_vma=False,
    )
```

```python
import functools

import jax
import jax.numpy as jnp
from jax import lax
from jax.experimental import pallas as pl
from jax.experimental.pallas import tpu as pltpu
from jax.sharding import PartitionSpec as P


D = 2048
HQ = 16
KVH = 2
HD = 128
EFF = 768
TOPK = 8
STRETCH = 128
BF = jnp.bfloat16
F32 = jnp.float32
MIB = 1 << 20
LOG2E = 1.4426950408889634
STAT = 8


NT = (((1,), (1,)), ((), ()))
NN = (((1,), (0,)), ((), ()))


def dot(a, b, dims):
    return lax.dot_general(a, b, dims, preferred_element_type=F32)


def place():
    device = lax.axis_index("ctx")
    return device, device & 1, device >> 1, device >> 2


def hop(x, mask, width):
    return lax.ppermute(x, "ctx", [(i, i ^ mask) for i in range(width)])


def sequence(nz):
    return list(range(nz - 1, -1, -1))


def portions(nz):
    return [1, nz // 2 - 1, nz // 2]


def shares(nz):
    return [1, 1, nz // 2 - 1, nz // 2 - 1]


def split3(x):
    hi = x.astype(BF)
    rest = x - hi.astype(F32)
    mid = rest.astype(BF)
    return hi, mid, (rest - mid.astype(F32)).astype(BF)


def row_ids(per, core, axis, shape):
    i = lax.broadcasted_iota(jnp.int32, shape, axis)
    return (i // per) * (2 * per) + core * per + i % per


def fetch_kernel(count, *refs):
    sems = refs[2 * count]
    copies = [
        pltpu.make_async_copy(refs[i], refs[count + i], sems.at[i]) for i in range(count)
    ]
    for copy in copies:
        copy.start()
    for copy in copies:
        copy.wait()


def in_hbm(x):
    return pltpu.with_memory_space_constraint(x, pltpu.HBM)


def fetch(*arrays):
    count = len(arrays)
    size = sum(a.size * a.dtype.itemsize for a in arrays)
    return pl.pallas_call(
        functools.partial(fetch_kernel, count),
        out_shape=[pltpu.VMEM(a.shape, a.dtype) for a in arrays],
        in_specs=[pl.BlockSpec(memory_space=pltpu.HBM)] * count,
        out_specs=[pl.BlockSpec(memory_space=pltpu.VMEM)] * count,
        scratch_shapes=[pltpu.SemaphoreType.DMA((count,))],
        cost_estimate=pl.CostEstimate(flops=0, bytes_accessed=2 * size, transcendentals=0),
        compiler_params=pltpu.CompilerParams(vmem_limit_bytes=16 * MIB),
        name="fetch",
    )(*[in_hbm(a) for a in arrays])


def prepare_kernel(per, width, *refs):
    (counts, order, ids, weights, residual, weight_in, gain_in) = refs[:7]
    (res, home, fill, turn, weight_out, gain_out) = refs[7:13]
    picks, table, own, sems = refs[13:]
    copies = [
        pltpu.make_async_copy(weight_in, weight_out, sems.at[0]),
        pltpu.make_async_copy(gain_in, gain_out, sems.at[1]),
    ]
    for copy in copies:
        copy.start()
    device, core, _, _ = place()
    cap, rows = residual.shape[0], order.shape[1]
    half = home.shape[0]
    slots = picks.shape[0]
    lane = lax.broadcasted_iota(jnp.int32, (width, width), 1)
    line = lax.broadcasted_iota(jnp.int32, (width, width), 0)
    many = counts[...].astype(F32)
    end = jnp.sum(jnp.where(lane <= line, many, 0.0), axis=1, keepdims=True)
    size = jnp.sum(jnp.where(lane == line, many, 0.0), axis=1, keepdims=True)
    p = lax.broadcasted_iota(jnp.int32, (width, rows), 1).astype(F32)
    past = (p >= end).astype(F32)
    owner = jnp.sum(past, axis=0, keepdims=True)
    start = jnp.sum(past * size, axis=0, keepdims=True)
    slot = owner * cap + p[:1] - start
    at = lax.broadcasted_iota(jnp.int32, (slots, rows), 0).astype(F32)
    picks[...] = (at == slot).astype(F32).astype(BF)
    seats = [
        (order[...] == row_ids(per, c, 0, (half, rows))).astype(F32).astype(BF)
        for c in range(2)
    ]
    mine = (order[...] == row_ids(per, core, 0, (half, rows))).astype(F32).astype(BF)
    own[...] = dot(picks[...], mine, NT).astype(BF)
    table[...] = dot(picks[...], jnp.concatenate(seats, axis=0), NT).astype(BF)
    for kc in range(2):
        for ky in range(2):
            for spot, kz in enumerate(sequence(width // 4)):
                there = device ^ (kc + 2 * ky + 4 * kz)
                there = pl.ds(pl.multiple_of(there * cap, cap), cap)
                to = (kc * 2 + ky) * (width // 4) + spot
                turn[to * cap : (to + 1) * cap, :] = table[there, :]
                fill[to * cap : (to + 1) * cap, :] = own[there, :]
    chip_picks = [
        picks[pl.ds(pl.multiple_of(o * cap, cap), cap), :] for o in (device, device ^ 1)
    ]
    home[...] = dot(mine, jnp.concatenate(chip_picks, axis=0), NT).astype(BF)
    lanes = res.shape[1] - D
    kind = lax.broadcasted_iota(jnp.int32, (lanes, cap), 0)
    norm = weights[...] / jnp.sum(weights[...], axis=0, keepdims=True)
    dense = jnp.zeros((lanes, cap), F32)
    for k in range(TOPK):
        dense = dense + jnp.where(ids[k : k + 1, :] == kind % width, norm[k : k + 1, :], 0.0)
    high = dense.astype(BF).astype(F32)
    low = jnp.where(kind < 2 * width, dense - high, 0.0)
    both = jnp.where(kind < width, high, low).astype(BF)
    i = lax.broadcasted_iota(jnp.int32, (cap, cap), 0)
    j = lax.broadcasted_iota(jnp.int32, (cap, cap), 1)
    res[:, :D] = residual[...]
    res[:, D:] = dot((i == j).astype(F32).astype(BF), both, NT).astype(BF)
    for copy in copies:
        copy.wait()


def prepare(counts, order, ids, weights, residual, out_weight, gain, per, width):
    cap, rows = residual.shape[0], order.shape[1]
    half = width // 2 * per
    lanes = -(-2 * width // 128) * 128
    slots = width * cap
    given = (counts, order, ids, weights, residual, out_weight, gain)
    return pl.pallas_call(
        functools.partial(prepare_kernel, per, width),
        out_shape=[
            jax.ShapeDtypeStruct((cap, D + lanes), BF),
            jax.ShapeDtypeStruct((half, 2 * cap), BF),
            jax.ShapeDtypeStruct((slots, half), BF),
            jax.ShapeDtypeStruct((slots, 2 * half), BF),
            pltpu.VMEM(out_weight.shape, out_weight.dtype),
            pltpu.VMEM(gain.shape, gain.dtype),
        ],
        in_specs=[pl.BlockSpec(memory_space=pltpu.VMEM)] * 5
        + [pl.BlockSpec(memory_space=pltpu.HBM)] * 2,
        out_specs=[pl.BlockSpec(memory_space=pltpu.VMEM)] * 6,
        scratch_shapes=[
            pltpu.VMEM((slots, rows), BF),
            pltpu.VMEM((slots, 2 * half), BF),
            pltpu.VMEM((slots, half), BF),
            pltpu.SemaphoreType.DMA((2,)),
        ],
        cost_estimate=pl.CostEstimate(
            flops=6 * slots * rows * half, bytes_accessed=8 * slots * half, transcendentals=0
        ),
        compiler_params=pltpu.CompilerParams(vmem_limit_bytes=12 * MIB),
        name="prepare",
    )(*[in_hbm(a) for a in given])


def total_kernel(*refs):
    terms, out = refs[:-1], refs[-1]
    out[...] = functools.reduce(lambda a, b: a + b, [t[...].astype(F32) for t in terms]).astype(BF)


def pair_kernel(first, second, out):
    out[0] = first[...]
    out[1] = second[...]


def small(kernel, shape, *terms):
    return pl.pallas_call(
        kernel,
        out_shape=jax.ShapeDtypeStruct(shape, BF),
        in_specs=[pl.BlockSpec(memory_space=pltpu.VMEM)] * len(terms),
        out_specs=pl.BlockSpec(memory_space=pltpu.VMEM),
        cost_estimate=pl.CostEstimate(
            flops=len(terms) * terms[0].size,
            bytes_accessed=2 * (len(terms) + 1) * terms[0].size,
            transcendentals=0,
        ),
        compiler_params=pltpu.CompilerParams(vmem_limit_bytes=16 * MIB),
    )(*terms)


def attention_kernel(nz, far, lengths, *refs):
    pieces, (k_own, v_own, k_oth, v_oth) = refs[:nz], refs[nz : nz + 4]
    *outs, rows, ready = refs[nz + 4 :]
    device, core, chip, z = place()
    per = pieces[0].shape[1]
    requests, span = k_own.shape[0], k_own.shape[1]
    count = rows.shape[0]
    seat = count // requests
    chips, depth = ready.shape[0], ready.shape[1] - STAT
    cols = HQ * HD // chips
    heads = max(1, cols // HD)
    group = HQ // KVH
    for kz in range(nz):
        both = pieces[kz][...].astype(F32)
        for ky in range(2):
            spot = (chip ^ (2 * kz + ky)) * per
            rows[pl.ds(pl.multiple_of(spot, per), per), :] = both[ky]
    wide = group * seat
    key = lax.broadcasted_iota(jnp.int32, (span, wide), 0)
    lane = lax.broadcasted_iota(jnp.int32, (1, wide), 1) % seat
    ahead = (lane // per) * (2 * per) + core * per + lane % per - STRETCH
    first_own, first_oth = device * span, (device ^ 1) * span
    for q in range(requests):
        last = lengths[q] + ahead
        see_own, see_oth = key <= last - first_own, key <= last - first_oth
        for near_head in range(KVH // 2):
            half = z // (nz // 2) ^ far
            v = half * (KVH // 2) + near_head
            kv = pl.ds(pl.multiple_of(v * HD, HD), HD)
            asked = jnp.concatenate(
                [
                    rows[
                        q * seat : (q + 1) * seat,
                        pl.ds(pl.multiple_of((v * group + e) * HD, HD), HD),
                    ]
                    for e in range(group)
                ],
                axis=0,
            ).astype(BF)
            s_own = dot(k_own[q, :, kv], asked, NT) * (HD ** (-0.5) * LOG2E)
            s_oth = dot(k_oth[q, :, kv], asked, NT) * (HD ** (-0.5) * LOG2E)
            s_own = jnp.where(see_own, s_own, -1e30)
            s_oth = jnp.where(see_oth, s_oth, -1e30)
            top = jnp.maximum(
                jnp.max(s_own, axis=0, keepdims=True), jnp.max(s_oth, axis=0, keepdims=True)
            )
            top = jnp.maximum(top, -1e29)
            w_own = jnp.exp2(s_own - top)
            w_oth = jnp.exp2(s_oth - top)
            total = jnp.sum(w_own, axis=0, keepdims=True) + jnp.sum(w_oth, axis=0, keepdims=True)
            mixed = dot(v_own[q, :, kv].T, w_own.astype(BF), NN) + dot(
                v_oth[q, :, kv].T, w_oth.astype(BF), NN
            )
            some = total > 0.0
            safe = jnp.where(some, total, 1.0)
            mixed = (mixed * (1.0 / safe)).astype(BF)
            lse = jnp.where(some, top * (1.0 / LOG2E) + jnp.log(safe), -1e30)
            stat = with_lse(lse)
            if heads == 2 and requests == 1:
                for g in range(group // 2):
                    dest = (v * (group // 2) + g) ^ chip
                    mine = slice(2 * g * seat, 2 * (g + 1) * seat)
                    ready[dest, :depth, :] = mixed[:, mine]
                    ready[dest, depth:, :] = stat[:, mine]
            else:
                for e in range(group):
                    mine = slice(e * seat, (e + 1) * seat)
                    head = v * group + e
                    lo = (e % heads) * count + q * seat
                    for part in range(HD // depth):
                        dest = ((head * HD + part * depth) // cols) ^ chip
                        some_rows = slice(part * depth, (part + 1) * depth)
                        ready[dest, :depth, lo : lo + seat] = mixed[some_rows, mine]
                        ready[dest, depth:, lo : lo + seat] = stat[:, mine]
    order = sequence(nz)
    outs = iter(outs)
    for ky in range(2):
        taken = 0 if far else nz // 2
        for blocks in portions(nz)[:2] if far else portions(nz)[2:]:
            out = next(outs)
            for i in range(blocks):
                out[i] = ready[2 * order[taken + i] + ky]
            taken = taken + blocks


def with_lse(lse):
    parts = [x.astype(F32) for x in split3(lse)]
    return jnp.concatenate(parts + [jnp.zeros((STAT - 3, lse.shape[1]), F32)], axis=0).astype(BF)


def attention(pieces, k_own, v_own, k_oth, v_oth, lengths, chips, far):
    nz = len(pieces)
    per = pieces[0].shape[1]
    count = chips * per
    cols = HQ * HD // chips
    heads = max(1, cols // HD)
    shape = (min(cols, HD) + STAT, heads * count)
    work = 2 * k_own.size * (HQ // KVH) * 2 * count
    parts = portions(nz)[:2] if far else portions(nz)[2:]
    return pl.pallas_call(
        functools.partial(attention_kernel, nz, far),
        out_shape=[jax.ShapeDtypeStruct((blocks,) + shape, BF) for blocks in parts] * 2,
        in_specs=[pl.BlockSpec(memory_space=pltpu.SMEM)]
        + [pl.BlockSpec(memory_space=pltpu.VMEM)] * (nz + 4),
        out_specs=[pl.BlockSpec(memory_space=pltpu.VMEM)] * (2 * len(parts)),
        scratch_shapes=[
            pltpu.VMEM((count, HQ * HD), F32),
            pltpu.VMEM((chips,) + shape, BF),
        ],
        cost_estimate=pl.CostEstimate(
            flops=work, bytes_accessed=8 * k_own.size, transcendentals=work // (4 * HD)
        ),
        compiler_params=pltpu.CompilerParams(vmem_limit_bytes=24 * MIB),
        name="attention",
    )(lengths, *pieces, k_own, v_own, k_oth, v_oth)


def merged(blocks):
    depth = blocks[0].shape[0] - STAT
    lse = [jnp.sum(x[depth:].astype(F32), axis=0, keepdims=True) for x in blocks]
    best = functools.reduce(jnp.maximum, lse)
    factor = [jnp.exp(x - best) for x in lse]
    denom = functools.reduce(lambda a, b: a + b, factor)
    mixed = functools.reduce(
        lambda a, b: a + b, [x[:depth].astype(F32) * f for x, f in zip(blocks, factor)]
    )
    return mixed * (1.0 / denom), best + jnp.log(denom)


def fold_kernel(near, far, *outs):
    depth = outs[0].shape[0] - STAT
    for i, out in enumerate(outs):
        mixed, lse = merged([near[i], far[i]])
        out[:depth, :] = mixed.astype(BF)
        out[depth:, :] = with_lse(lse)


def fold(near, far):
    count = near.shape[0]
    return pl.pallas_call(
        fold_kernel,
        out_shape=[jax.ShapeDtypeStruct(near.shape[1:], BF)] * count,
        in_specs=[pl.BlockSpec(memory_space=pltpu.VMEM)] * 2,
        out_specs=[pl.BlockSpec(memory_space=pltpu.VMEM)] * count,
        cost_estimate=pl.CostEstimate(
            flops=8 * near.size, bytes_accessed=8 * near.size, transcendentals=0
        ),
        compiler_params=pltpu.CompilerParams(vmem_limit_bytes=16 * MIB),
        name="fold",
    )(near, far)


def project_kernel(nz, *refs):
    blocks, (w_own, w_oth, res_own, res_oth, home) = refs[:nz], refs[nz : nz + 5]
    outs, attn, part = refs[nz + 5 : 2 * nz + 5], refs[2 * nz + 5], refs[2 * nz + 6]
    _, core, _, z = place()
    depth = blocks[0].shape[0] - STAT
    count = part.shape[0]
    heads = blocks[0].shape[1] // count
    mixed, _ = merged([b[...] for b in blocks])
    mixed = mixed.T.astype(BF)
    if heads == 2:
        first, second = mixed[:count], mixed[count:]
        attn[...] = jnp.concatenate([first, second], axis=1)
    else:
        first, second = mixed[:, : depth // 2], mixed[:, depth // 2 :]
        attn[...] = mixed
    low = (core == 0).astype(F32)
    first, second = first.astype(F32), second.astype(F32)
    own = (first * low + second * (1.0 - low)).astype(BF)
    oth = (second * low + first * (1.0 - low)).astype(BF)
    res = jnp.concatenate([res_own[...], res_oth[...]], axis=0)
    part[:, :D] = (
        dot(home[...], res[:, :D], NN) + dot(own, w_own[...], NN) + dot(oth, w_oth[...], NN)
    )
    part[:, D:] = dot(home[...], res[:, D:], NN)
    block = outs[0].shape[0]
    for kz in range(nz):
        spot = pl.multiple_of((z ^ kz) * block, block)
        outs[kz][...] = part[pl.ds(spot, block), :].astype(BF)


def project(blocks, w_own, w_oth, res_own, res_oth, home):
    nz = len(blocks)
    count = home.shape[0]
    cols = D // (2 * nz)
    wide = res_own.shape[1]
    return pl.pallas_call(
        functools.partial(project_kernel, nz),
        out_shape=[jax.ShapeDtypeStruct((count // nz, wide), BF)] * nz
        + [jax.ShapeDtypeStruct((count, cols), BF)],
        in_specs=[pl.BlockSpec(memory_space=pltpu.VMEM)] * (nz + 5),
        out_specs=[pl.BlockSpec(memory_space=pltpu.VMEM)] * (nz + 1),
        scratch_shapes=[pltpu.VMEM((count, wide), F32)],
        cost_estimate=pl.CostEstimate(
            flops=2 * count * cols * D, bytes_accessed=4 * cols * D, transcendentals=0
        ),
        compiler_params=pltpu.CompilerParams(vmem_limit_bytes=12 * MIB),
        name="project",
    )(*blocks, w_own, w_oth, res_own, res_oth, home)


def expert_kernel(nz, width, *refs):
    mine, theirs = refs[:nz], refs[nz : 2 * nz]
    (gain, gate_up, down, turn, fill, mixed) = refs[2 * nz : 2 * nz + 6]
    *outs, scaled, x, normed, hidden = refs[2 * nz + 6 :]
    device, core, _, z = place()
    block = mine[0].shape[0]
    half = block * nz
    cap = fill.shape[0] // width
    for kz in range(nz):
        spot = (z ^ kz) * block
        x[pl.ds(pl.multiple_of(core * half + spot, block), block), :] = mine[kz][...]
        x[pl.ds(pl.multiple_of((1 - core) * half + spot, block), block), :] = theirs[kz][...]
    stream = x[:, :D].astype(F32)
    scale = lax.rsqrt(jnp.mean(stream * stream, axis=-1, keepdims=True) + 1e-06)
    normed[...] = (stream * scale * gain[...]).astype(BF)
    extra = x[:, D:].astype(F32)
    lane = lax.broadcasted_iota(jnp.int32, extra.shape, 1)
    pick = (lane == device) | (lane == device + width)
    weight = jnp.sum(jnp.where(pick, extra, 0.0), axis=-1, keepdims=True)
    tile = 256
    for lo in range(0, EFF, tile):
        g = dot(normed[...], gate_up[0, :, lo : lo + tile], NN)
        u = dot(normed[...], gate_up[0, :, EFF + lo : EFF + lo + tile], NN)
        hidden[:, lo : lo + tile] = (g / (1.0 + jnp.exp(-g)) * u).astype(BF)
    for lo in range(0, D, tile):
        y = dot(hidden[...], down[0, :, lo : lo + tile], NN).astype(BF)
        scaled[:, lo : lo + tile] = (y.astype(F32) * weight).astype(BF)
    done = nz * cap
    for target in outs:
        some = slice(done, done + target.shape[0])
        target[:, :D] = dot(turn[some, :], scaled[...], NN).astype(BF)
        target[:, D:] = dot(fill[some, :], mixed[...], NN).astype(BF)
        done = done + target.shape[0]


def stay_kernel(scaled, x, turn, fill, mixed, keep, stream_own):
    cap = stream_own.shape[0]
    size = keep.shape[0]
    keep[:, :D] = dot(turn[:size, :], scaled[...], NN).astype(BF)
    keep[:, D:] = dot(fill[:size, :], mixed[...], NN).astype(BF)
    stream_own[...] = dot(turn[size - cap : size, :], x[:, :D], NN).astype(BF)


def stay(scaled, x, turn, fill, mixed, cap):
    size = turn.shape[0] // 4
    return pl.pallas_call(
        stay_kernel,
        out_shape=[
            jax.ShapeDtypeStruct((size, D + mixed.shape[1]), BF),
            jax.ShapeDtypeStruct((cap, D), BF),
        ],
        in_specs=[pl.BlockSpec(memory_space=pltpu.VMEM)] * 5,
        out_specs=[pl.BlockSpec(memory_space=pltpu.VMEM)] * 2,
        cost_estimate=pl.CostEstimate(
            flops=2 * size * scaled.size, bytes_accessed=6 * scaled.size, transcendentals=0
        ),
        compiler_params=pltpu.CompilerParams(vmem_limit_bytes=16 * MIB),
        name="stay",
    )(scaled, x, turn, fill, mixed)


def experts(mine, theirs, gain, gate_up, down, turn, fill, mixed, width, cap):
    nz = len(mine)
    block, wide = mine[0].shape
    total = 2 * nz * block
    shapes = [
        jax.ShapeDtypeStruct((blocks * cap, D + mixed.shape[1]), BF)
        for blocks in [nz] + shares(nz)
    ]
    return pl.pallas_call(
        functools.partial(expert_kernel, nz, width),
        out_shape=shapes[1:]
        + shapes
        + [jax.ShapeDtypeStruct((total, D), BF), jax.ShapeDtypeStruct((total, wide), BF)],
        in_specs=[pl.BlockSpec(memory_space=pltpu.VMEM)] * (2 * nz + 6),
        out_specs=[pl.BlockSpec(memory_space=pltpu.VMEM)] * (2 * len(shapes) + 1),
        scratch_shapes=[pltpu.VMEM((total, D), BF), pltpu.VMEM((total, EFF), BF)],
        cost_estimate=pl.CostEstimate(
            flops=6 * total * D * EFF, bytes_accessed=6 * D * EFF, transcendentals=total * EFF
        ),
        compiler_params=pltpu.CompilerParams(vmem_limit_bytes=32 * MIB),
        name="experts",
    )(*mine, *theirs, gain, gate_up, down, turn, fill, mixed)


def mix_kernel(first, keep, near, far, *outs):
    cap = outs[0].shape[0]
    for i, out in enumerate(outs):
        here = slice((first + i) * cap, (first + i + 1) * cap)
        own = keep[here, :].astype(F32) + near[here, :].astype(F32)
        other = far[i * cap : (i + 1) * cap, :].astype(F32)
        out[:, :D] = (own[:, :D] + other[:, :D]).astype(BF)
        out[:, D:] = jnp.concatenate([own[:, D:], other[:, D:]], axis=1).astype(BF)


def mix(keep, near, far, cap, first):
    count = far.shape[0] // cap
    cols = keep.shape[1] - D
    return pl.pallas_call(
        functools.partial(mix_kernel, first),
        out_shape=[jax.ShapeDtypeStruct((cap, D + 2 * cols), BF)] * count,
        in_specs=[pl.BlockSpec(memory_space=pltpu.VMEM)] * 3,
        out_specs=[pl.BlockSpec(memory_space=pltpu.VMEM)] * count,
        cost_estimate=pl.CostEstimate(
            flops=3 * far.size, bytes_accessed=8 * far.size, transcendentals=0
        ),
        compiler_params=pltpu.CompilerParams(vmem_limit_bytes=16 * MIB),
        name="mix",
    )(keep, near, far)


def finish_kernel(nz, stream, *refs):
    pieces, (attn, out) = refs[:nz], refs[nz:]
    _, _, chip, _ = place()
    cols = (pieces[0].shape[1] - D) // 2
    total = stream[...].astype(F32)
    for kz in range(nz):
        total = total + pieces[kz][:, :D].astype(F32)
    out[...] = total.astype(BF)
    if cols % 128 == 0:
        for kz in range(nz):
            for ky in range(2):
                spot = pl.multiple_of((chip ^ (2 * kz + ky)) * cols, cols)
                attn[:, pl.ds(spot, cols)] = pieces[kz][:, D + ky * cols : D + (ky + 1) * cols]
    else:
        whole = jnp.zeros(attn.shape, F32)
        lane = lax.broadcasted_iota(jnp.int32, (cols, D), 1)
        line = lax.broadcasted_iota(jnp.int32, (cols, D), 0)
        for kz in range(nz):
            for ky in range(2):
                spot = (chip ^ (2 * kz + ky)) * cols
                put = (lane == line + spot).astype(F32).astype(BF)
                part = pieces[kz][:, D + ky * cols : D + (ky + 1) * cols]
                whole = whole + dot(part, put, NN)
        attn[...] = whole.astype(BF)


def finish(stream, pieces):
    shape = jax.ShapeDtypeStruct(stream.shape, BF)
    nz = len(pieces)
    return pl.pallas_call(
        functools.partial(finish_kernel, nz),
        out_shape=[shape, shape],
        in_specs=[pl.BlockSpec(memory_space=pltpu.VMEM)] * (nz + 1),
        out_specs=[pl.BlockSpec(memory_space=pltpu.VMEM)] * 2,
        cost_estimate=pl.CostEstimate(
            flops=nz * stream.size, bytes_accessed=4 * nz * stream.size, transcendentals=0
        ),
        compiler_params=pltpu.CompilerParams(vmem_limit_bytes=16 * MIB),
        name="finish",
    )(stream, *pieces)


def body(
    queries,
    keys,
    values,
    lengths,
    owner_counts,
    row_order,
    residual,
    out_weight,
    norm_gain,
    expert_ids,
    route_weights,
    gate_up,
    expert_down,
):
    width = lax.axis_size("ctx")
    chips, nz = width // 2, width // 4
    per = queries.shape[0]
    cap = residual.shape[0]
    order = row_order.reshape(1, -1)

    def along_z(terms):
        out = [terms[0]]
        for kz in range(1, nz):
            out.append(hop(terms[kz], 4 * kz, width))
        return out

    def by_distance(blocks):
        return [blocks[sequence(nz).index(kz)] for kz in range(nz)]

    def add(*terms):
        return small(total_kernel, terms[0].shape, *terms)

    near = hop(queries, 2, width)
    k_oth = hop(keys, 1, width)
    v_oth = hop(values, 1, width)
    q_own, k_own, v_own = fetch(queries, keys, values)
    column = small(pair_kernel, (2,) + queries.shape, q_own, near)
    pieces = along_z([column] * nz)
    w_oth = hop(out_weight, 1, width)
    res_own, home, fill, turn, w_own, gain = prepare(
        owner_counts.reshape(1, -1),
        order,
        expert_ids.T,
        route_weights.T,
        residual,
        out_weight,
        norm_gain.reshape(1, -1),
        per,
        width,
    )
    res_oth = hop(res_own, 1, width)

    asked = (pieces, k_own, v_own, k_oth, v_oth, lengths, chips)
    one, two, send_one, send_two = attention(*asked, 1)
    three, send_three = attention(*asked, 0)
    count = len(portions(nz))
    fars, blocks = [], []
    for send in (send_one, send_two, send_three):
        fars.append(hop(send, 2, width))
    for i, near in enumerate((one, two, three)):
        blocks += fold(near, fars[i])
    blocks = along_z(by_distance(blocks))
    *parts, mixed = project(blocks, w_own, w_oth, res_own, res_oth, home)
    chunk = add(*along_z(parts))
    (up,) = fetch(gate_up)
    other = hop(chunk, 2, width)
    chunk = add(chunk, other)
    mine = along_z([chunk] * nz)
    theirs = [hop(x, 1, width) for x in mine]
    (down,) = fetch(expert_down)
    *halves, scaled, rows = experts(
        mine, theirs, gain, up, down, turn, fill, mixed, width, cap
    )
    count = len(shares(nz))
    keeps, (send, *sends) = halves[:count], halves[count:]
    keep, stream = stay(scaled, rows, turn, fill, mixed, cap)
    gots, fars, blocks = [], [], []
    for i in range(count):
        gots.append(hop(sends[i], 1, width))
    got = hop(send, 1, width)
    for i in range(count):
        term = add(keeps[i], gots[i])
        fars.append(hop(term, 2, width))
    for i in range(count):
        blocks += mix(keep, got, fars[i], cap, len(blocks))
    attn, layer_out = finish(stream, along_z(by_distance(blocks)))
    return (attn, layer_out)


def solution(mesh):
    placed = (
        P(("groups", "ctx"), None),
        P("groups", "ctx", None),
        P("groups", "ctx", None),
        P("groups"),
        P("groups"),
        P("groups"),
        P(("groups", "ctx"), None),
        P("ctx", None),
        P(),
        P(("groups", "ctx"), None),
        P(("groups", "ctx"), None),
        P("ctx", None, None),
        P("ctx", None, None),
    )

    return jax.shard_map(
        body,
        mesh=mesh,
        in_specs=placed,
        out_specs=(P(("groups", "ctx"), None), P(("groups", "ctx"), None)),
        check_vma=False,
    )
```
